32 devices in a mesh: fx: 8 (over z, x), fy: 4 (over y, core).
Axes of the slice: x: 2, y: 2, z: 4, core: 2. Of those that a mesh axis runs over, the one named last changes fastest.
Arguments:
- right_side: float32 [512, 2048], P(('fx', 'fy'))
- coupling: float32 [512, 11, 4096], P(('fx', 'fy')), may hold values from -0.109375 to 0.109375
- face_columns: int32 [512, 11], P(('fx', 'fy')), may hold values from 0 to 31, as said below
- ghost_lists: int32 [128, 4], P(('fx', 'fy')), may hold values from 0 to 15, as said below
Outputs:
- solution: float32 [512, 2048], P(('fx', 'fy'))
- residual: float32 [512, 2048], P(('fx', 'fy'))
The draws below stay inside these ranges and needn't reach their ends.
Inputs may be any that keep to these rules, and one draw needn't show every extreme that they name: face_columns[f, 0] is f's own index within its block; entries 1 to 6 name other faces of the same block, all distinct and below 16; entries 7 to 10 are distinct and name received faces, 16 + d * 4 + g for the g-th face of group d of the extended list; every received slot of every block is named by some row of that block. `ghost_lists`: each row names 4 distinct faces of its block by local index.
All inputs are finite; a program needn't handle non-finite values.
Results may differ from the reference program's by a relative error of at most 0.0003.
Values sent between devices are 32-bit elements; how exact they have to be, the bound alone decides.
A program may use at most 64 MiB of HBM per device.

```python
import jax
import jax.numpy as jnp
from jax import lax

DOF = 64
NRHS = 32
BLOCKS = 11
OWNED = 7
POWERS = 3
FACE_DEV = 16
GHOST = 4
FACES = 512
N_FX = 8
N_FY = 4


def draw_right_side(key, part):
    keys = jax.random.split(key, 3)
    blocks_total = N_FX * N_FY
    block_id = (jnp.arange(FACES) // FACE_DEV).astype(jnp.float32)
    position = block_id / max(blocks_total - 1, 1) - 0.5
    base = jax.random.normal(keys[0], (FACES, DOF * NRHS), jnp.float32)
    ramp = jnp.exp(position * jnp.log(3.0))
    face_scale = jnp.exp(jax.random.uniform(keys[1], (FACES,), jnp.float32, jnp.log(0.3), jnp.log(3.0)))
    column_scale = jnp.exp(jax.random.uniform(keys[2], (NRHS,), jnp.float32, jnp.log(0.3), jnp.log(3.0)))
    column_scale = jnp.tile(column_scale, DOF)
    return base * (ramp * face_scale)[:, None] * column_scale[None, :]


def draw_face_columns(key, part):
    keys = jax.random.split(key, 3)
    blocks_total = N_FX * N_FY
    local = jnp.arange(FACES) % FACE_DEV
    row_keys = jax.random.split(keys[0], FACES)

    def owned_pick(one_key):
        return jax.random.permutation(one_key, FACE_DEV - 1)[:OWNED - 1]
    owned = jax.vmap(owned_pick)(row_keys)
    owned = owned + (owned >= local[:, None]).astype(owned.dtype)
    block_keys = jax.random.split(keys[1], blocks_total)

    def cover_pick(one_key):
        return jax.random.permutation(one_key, FACE_DEV)
    cover = jax.vmap(cover_pick)(block_keys).reshape(FACES) % (4 * GHOST)
    other_keys = jax.random.split(keys[2], FACES)

    def other_pick(one_key):
        return jax.random.permutation(one_key, 4 * GHOST - 1)[:BLOCKS - OWNED - 1]
    others = jax.vmap(other_pick)(other_keys)
    others = others + (others >= cover[:, None]).astype(others.dtype)
    received = jnp.concatenate([others, cover[:, None]], axis=1) + FACE_DEV
    return jnp.concatenate([local[:, None], owned, received], axis=1).astype(jnp.int32)


def draw_ghost_lists(key, part):
    list_keys = jax.random.split(key, 4 * N_FX * N_FY)

    def list_pick(one_key):
        return jax.random.permutation(one_key, FACE_DEV)[:GHOST]
    return jax.vmap(list_pick)(list_keys).astype(jnp.int32)


def level_of(own_key, shape, pieces, least, largest):
    def one(dim, blocks):
        draws = jax.random.uniform(jax.random.fold_in(jax.random.fold_in(own_key, 6), dim), (blocks,), jnp.float32, least / len(pieces), largest / len(pieces))
        return jnp.repeat(jnp.exp(draws), shape[dim] // blocks).reshape((-1,) + (1,) * (len(shape) - dim - 1))

    level = one(*pieces[0])
    for cut in pieces[1:]:
        level = level * one(*cut)
    return level


def centred(key, dims, deviation, limit, cuts=(), held_as=jnp.bfloat16):
    array = deviation * jax.random.normal(key, dims, jnp.float32)
    if cuts:
        array = array * level_of(key, dims, cuts, -0.22, 0.18)
    return jnp.clip(array, -limit, limit).astype(held_as)


def setup_inputs(seed: int = 0) -> dict:
    seeds = jax.random.split(jax.random.key(seed), 5)
    return {
        "right_side": draw_right_side(jax.random.fold_in(seeds[4], 71), 0),
        "coupling": centred(seeds[1], (FACES, BLOCKS, DOF * DOF), (4 * BLOCKS * DOF) ** -0.5, 0.109375, ((0, 32),), jnp.float32),
        "face_columns": draw_face_columns(jax.random.fold_in(seeds[4], 71), 0),
        "ghost_lists": draw_ghost_lists(jax.random.fold_in(seeds[4], 71), 0),
    }


def extended_grid(field, ghost_lists):
    width = field.shape[1]
    field_grid = field.reshape(N_FX, N_FY, FACE_DEV, width)
    lists = ghost_lists.reshape(N_FX, N_FY, 4, GHOST)

    def select_rows(direction):
        return jnp.take_along_axis(field_grid, lists[:, :, direction, :][..., None], axis=2)
    zero_fx = jnp.zeros((1, N_FY, GHOST, width), jnp.float32)
    zero_fy = jnp.zeros((N_FX, 1, GHOST, width), jnp.float32)
    from_lower_x = jnp.concatenate([zero_fx, select_rows(1)[:-1]], axis=0)
    from_upper_x = jnp.concatenate([select_rows(0)[1:], zero_fx], axis=0)
    from_lower_y = jnp.concatenate([zero_fy, select_rows(3)[:, :-1]], axis=1)
    from_upper_y = jnp.concatenate([select_rows(2)[:, 1:], zero_fy], axis=1)
    return jnp.concatenate([field_grid, from_lower_x, from_upper_x, from_lower_y, from_upper_y], axis=2)

def apply_coupling(field, coupling, face_columns, ghost_lists):
    extended = extended_grid(field, ghost_lists)
    column_grid = face_columns.reshape(N_FX, N_FY, FACE_DEV * BLOCKS)
    block_mats = coupling.reshape(N_FX, N_FY, FACE_DEV, BLOCKS, DOF, DOF)

    def one_row(items):
        ext_row, col_row, mat_row = items
        picked = jnp.take_along_axis(ext_row, col_row[..., None], axis=1)
        picked = picked.reshape(N_FY, FACE_DEV, BLOCKS, DOF, NRHS)
        return jnp.einsum('yfkab,yfkbr->yfar', mat_row, picked, precision=lax.Precision.HIGHEST)
    result = lax.map(one_row, (extended, column_grid, block_mats))
    return result.reshape(FACES, DOF * NRHS)

def solve_small(gram_total):
    count = NRHS
    row_ids = jnp.arange((POWERS + 1) * count)[:, None]
    col_ids = jnp.arange(POWERS * count)[None, :]
    shift_map = ((row_ids == col_ids) | (row_ids == col_ids + count)).astype(jnp.float32)
    first = (row_ids == jnp.arange(count)[None, :]).astype(jnp.float32)
    high = lax.Precision.HIGHEST
    normal_matrix = jnp.dot(shift_map.T, jnp.dot(gram_total, shift_map, precision=high), precision=high)
    right_terms = jnp.dot(shift_map.T, gram_total[:, :count], precision=high)
    factor = jnp.linalg.cholesky(normal_matrix)
    coeffs = jax.scipy.linalg.cho_solve((factor, True), right_terms)
    combo = first - jnp.dot(shift_map, coeffs, precision=high)
    return (coeffs, combo)

def reference(right_side, coupling, face_columns, ghost_lists):
    fields = [right_side]
    for power_index in range(POWERS):
        fields.append(apply_coupling(fields[-1], coupling, face_columns, ghost_lists))
    stacked = jnp.concatenate([item.reshape(FACES * DOF, NRHS) for item in fields], axis=1)
    high = lax.Precision.HIGHEST
    gram_total = jnp.dot(stacked.T.astype(jnp.float32), stacked.astype(jnp.float32), precision=high, preferred_element_type=jnp.float32)
    coeffs, combo = solve_small(gram_total)
    solution = jnp.dot(stacked[:, :POWERS * NRHS], coeffs, precision=high)
    residual = jnp.dot(stacked, combo, precision=high)
    return (solution.reshape(FACES, DOF * NRHS), residual.reshape(FACES, DOF * NRHS))
```

```python
import functools

import jax
import jax.numpy as jnp
from jax import lax
from jax.experimental import pallas as pl
from jax.experimental.pallas import tpu as pltpu
from jax.sharding import PartitionSpec as P

DOF = 64
NRHS = 32
BLOCKS = 11
OWNED = 7
POWERS = 3
LANES = 128
HALF = DOF // 2
UNROLL = 16
GROUPS = LANES // NRHS
MESH = pl.DeviceIdType.MESH
f32 = jnp.float32
bf16 = jnp.bfloat16


def split(x):
    hi = x.astype(bf16).astype(f32)
    return hi, x - hi


def lane_group(rows):
    return lax.broadcasted_iota(jnp.int32, (rows, LANES), 1) // NRHS


def pick(group, parts):
    out = parts[-1]
    for index in range(len(parts) - 2, -1, -1):
        out = jnp.where(group == index, parts[index], out)
    return out


def replicate(group, rolled, source):
    return pick(group, [rolled[(lane - source) % GROUPS] for lane in range(GROUPS)])


def rolls(x):
    return [x] + [pltpu.roll(x, step * NRHS, 1) for step in range(1, GROUPS)]


def product_tile(x, group):
    hi, lo = split(x)
    zero = jnp.zeros_like(x)
    top = pick(group, [hi, zero, lo, zero])
    bottom = pick(group, [zero, hi, zero, lo])
    return top.astype(bf16), bottom.astype(bf16)


def kernel(shape, right_hbm, coupling_ref, columns_hbm, ghost_hbm, sol_ref, res_ref,
           right_ref, columns_ref, ghost_ref, stage, spread, mats, w0, w1, w2, w3, tiles, acc, send_buf, recv_buf,
           zbuf, vbuf, gram_buf, plane_recv, line_recv, final_buf, wide,
           small_sem, load_sem, send_sem, recv_sem, ps_sem, pr_sem, ls_sem, lr_sem, as_sem, ar_sem):
    n_fx, n_fy, low, faces = shape
    plane = low * n_fy
    high = n_fx // low
    i = lax.axis_index("fx")
    j = lax.axis_index("fy")
    my_low = i % low
    my_high = i // low
    my_rank = my_low * n_fy + j
    fields = [w0, w1, w2, w3]

    def plane_target(offset):
        rank = lax.rem(my_rank + offset, plane)
        return rank, (my_high * low + rank // n_fy, rank % n_fy)

    def line_target(offset):
        place = lax.rem(my_high + offset, high)
        return (place * low + my_low, j)

    routes = [
        (1, i < n_fx - 1, (i + 1, j), i > 0),
        (0, i > 0, (i - 1, j), i < n_fx - 1),
        (3, j < n_fy - 1, (i, j + 1), j > 0),
        (2, j > 0, (i, j - 1), j < n_fy - 1),
    ]

    small = [
        pltpu.make_async_copy(right_hbm, right_ref, small_sem.at[0]),
        pltpu.make_async_copy(ghost_hbm, ghost_ref, small_sem.at[1]),
        pltpu.make_async_copy(columns_hbm, columns_ref, small_sem.at[2]),
    ]
    for load in small:
        load.start()
    loads = [pltpu.make_async_copy(coupling_ref.at[k], stage.at[k], load_sem.at[k]) for k in range(BLOCKS)]
    for load in loads:
        load.start()

    barrier = pltpu.get_barrier_semaphore()
    for _, has_target, target, _ in routes:
        @pl.when(has_target)
        def _(target=target):
            pl.semaphore_signal(barrier, inc=1, device_id=target, device_id_type=MESH)
    for offset in range(1, plane):
        pl.semaphore_signal(barrier, inc=1, device_id=plane_target(offset)[1], device_id_type=MESH)
    for offset in range(1, high):
        pl.semaphore_signal(barrier, inc=1, device_id=line_target(offset), device_id_type=MESH)

    g8 = lane_group(8)
    g64 = lane_group(DOF)
    g32 = lane_group(HALF)

    small[0].wait()
    for block in range(faces // 8):
        for tile in range(DOF // GROUPS):
            x = right_ref[8 * block:8 * block + 8, tile * LANES:(tile + 1) * LANES]
            moved = rolls(x)
            for q in range(GROUPS):
                wide[0, pl.ds(8 * block * DOF + tile * GROUPS + q, 8, stride=DOF), :] = replicate(g8, moved, q)
    for face in range(faces):
        w0[face] = wide[0, face * DOF:(face + 1) * DOF, :]

    small[1].wait()
    small[2].wait()

    def field_copies(power):
        return [
            pltpu.make_async_remote_copy(
                src_ref=send_buf.at[power, q], dst_ref=recv_buf.at[power, q],
                send_sem=send_sem.at[power, q], recv_sem=recv_sem.at[power, q],
                device_id=routes[q][2], device_id_type=MESH,
            )
            for q in range(4)
        ]

    def send_field(power):
        field = fields[power]
        copies = field_copies(power)
        for q, (row, has_target, _, _) in enumerate(routes):
            picked = [field[ghost_ref[row, g]] for g in range(GROUPS)]
            send_buf[power, q] = pick(g64, picked)
            if power == 0 and q == 0:
                count = sum(jnp.where(route[1], 1, 0) for route in routes) + (plane - 1) + (high - 1)
                pl.semaphore_wait(barrier, count)

            @pl.when(has_target)
            def _(copy=copies[q]):
                copy.start()
        return copies

    def build_own(power):
        field = fields[power]

        @pl.loop(0, faces, unroll=4)
        def _(face):
            x = field[face]
            top, bottom = product_tile(x, g64)
            tiles[face, 0:DOF] = top
            tiles[face, DOF:2 * DOF] = bottom

    def own_products():
        @pl.loop(0, faces // UNROLL)
        def _(part):
            for sub in range(UNROLL):
                face = part * UNROLL + sub
                right = jnp.concatenate([tiles[columns_ref[face, k]] for k in range(OWNED)], axis=0)
                out = jnp.dot(mats[face, :, :OWNED * LANES], right, preferred_element_type=f32)
                acc[face] = out[:HALF] + out[HALF:]

    def far_products(power):
        field = fields[power + 1]

        @pl.loop(0, faces // UNROLL)
        def _(part):
            for sub in range(UNROLL):
                face = part * UNROLL + sub
                right = jnp.concatenate(
                    [tiles[columns_ref[face, k]] for k in range(OWNED, BLOCKS)], axis=0
                )
                out = jnp.dot(mats[face, :, OWNED * LANES:], right, preferred_element_type=f32)
                total = acc[face] + (out[:HALF] + out[HALF:])
                total = total + pltpu.roll(total, LANES // 2, 1)
                turned = pltpu.roll(total, NRHS, 1)
                even = g32 % 2 == 0
                field[face, pl.ds(0, HALF, stride=2), :] = jnp.where(even, total, turned)
                field[face, pl.ds(1, HALF, stride=2), :] = jnp.where(even, turned, total)

    def receive_field(power, copies):
        for q in (2, 3, 0, 1):
            _, has_target, _, has_source = routes[q]

            @pl.when(has_source)
            def _(copy=copies[q]):
                copy.wait_recv()

            @pl.when(jnp.logical_not(has_source))
            def _(q=q):
                recv_buf[power, q] = jnp.zeros((DOF, LANES), f32)
            moved = rolls(recv_buf[power, q])
            for g in range(GROUPS):
                top, bottom = product_tile(replicate(g64, moved, g), g64)
                tiles[faces + q * GROUPS + g, 0:DOF] = top
                tiles[faces + q * GROUPS + g, DOF:2 * DOF] = bottom

            @pl.when(has_target)
            def _(copy=copies[q]):
                copy.wait_send()

    def prepare():
        for k in range(BLOCKS):
            loads[k].wait()
            for block in range(faces // 8):
                for t in range(HALF):
                    spread[k % 2, pl.ds(8 * block * HALF + t, 8, stride=HALF), :] = stage[
                        k, 8 * block:8 * block + 8, t * LANES:(t + 1) * LANES]
            for face in range(faces):
                hi, lo = split(spread[k % 2, face * HALF:(face + 1) * HALF, :])
                mats[face, 0:HALF, k * LANES:(k + 1) * LANES] = hi.astype(bf16)
                mats[face, HALF:DOF, k * LANES:(k + 1) * LANES] = lo.astype(bf16)

    for power in range(POWERS):
        copies = send_field(power)
        build_own(power)
        if power == 0:
            prepare()
        own_products()
        receive_field(power, copies)
        far_products(power)

    @pl.loop(0, faces, unroll=4)
    def _(face):
        rows = pl.ds(pl.multiple_of(face * DOF, DOF), DOF)
        a, b, c, d = [field[face] for field in fields]
        hi, lo = split(pick(g64, [a + b, b + c, c + d, a]))
        zbuf[rows, :LANES] = hi.astype(bf16)
        zbuf[rows, LANES:] = lo.astype(bf16)

    z = zbuf[...]
    both = lax.dot_general(z, z, (((0,), (0,)), ((), ())), preferred_element_type=f32)
    gram = (both[:LANES, :LANES] + both[LANES:, LANES:]) + (both[:LANES, LANES:] + both[LANES:, :LANES])
    share = LANES // plane
    for rank in range(plane):
        gram_buf[rank] = gram[rank * share:(rank + 1) * share]

    copies = []
    for offset in range(1, plane):
        rank, target = plane_target(offset)
        copy = pltpu.make_async_remote_copy(
            src_ref=gram_buf.at[rank], dst_ref=plane_recv.at[offset], send_sem=ps_sem.at[offset],
            recv_sem=pr_sem.at[offset], device_id=target, device_id_type=MESH)
        copy.start()
        copies.append(copy)

    @pl.loop(0, faces, unroll=4)
    def _(face):
        rows = pl.ds(pl.multiple_of(face * DOF, DOF), DOF)
        hi, lo = split(pick(g64, [field[face] for field in fields]))
        vbuf[rows, :LANES] = hi.astype(bf16)
        vbuf[rows, LANES:] = lo.astype(bf16)

    total = gram_buf[my_rank]
    for offset, copy in enumerate(copies, 1):
        copy.wait_recv()
        total = total + plane_recv[offset]
    line_recv[my_high] = total
    line = []
    for offset in range(1, high):
        copy = pltpu.make_async_remote_copy(
            src_ref=line_recv.at[my_high], dst_ref=line_recv.at[my_high], send_sem=ls_sem.at[offset],
            recv_sem=lr_sem.at[offset], device_id=line_target(offset), device_id_type=MESH)
        copy.start()
        line.append(copy)
    for copy in copies:
        copy.wait_send()
    for copy in line:
        copy.wait_recv()
    total = line_recv[0]
    for place in range(1, high):
        total = total + line_recv[place]
    final_buf[my_rank] = total
    gather = []
    for offset in range(1, plane):
        copy = pltpu.make_async_remote_copy(
            src_ref=final_buf.at[my_rank], dst_ref=final_buf.at[my_rank], send_sem=as_sem.at[offset],
            recv_sem=ar_sem.at[offset], device_id=plane_target(offset)[1], device_id_type=MESH)
        copy.start()
        gather.append(copy)
    for copy in line:
        copy.wait_send()
    for copy in gather:
        copy.wait_recv()

    full = jnp.concatenate([final_buf[rank] for rank in range(plane)], axis=0)
    count = POWERS * NRHS
    tiles = [full[8 * t:8 * t + 8] for t in range(count // 8)]
    sub = lax.broadcasted_iota(jnp.int32, (8, LANES), 0)

    def across(x, lane):
        return jnp.broadcast_to(x[:, lane:lane + 1], (8, LANES))

    def down(x, row):
        return jnp.broadcast_to(x[row:row + 1, :], (8, LANES))

    for home in range(len(tiles)):
        mine = tiles[home]
        cols = [across(mine, 8 * home + c) for c in range(8)]
        for step in range(8):
            inverse = 1.0 / down(cols[step], step)
            here = sub == step
            factor = cols[step]
            scaled = down(mine, step) * inverse
            mine = jnp.where(here, scaled, mine - factor * scaled)
            for c in range(step + 1, 8):
                scaled = down(cols[c], step) * inverse
                cols[c] = jnp.where(here, scaled, cols[c] - factor * scaled)
        tiles[home] = mine
        rows8 = [down(mine, c) for c in range(8)]
        order = [t % len(tiles) for t in range(home + 1, home + len(tiles))]
        for t in order:
            terms = [across(tiles[t], 8 * home + c) * rows8[c] for c in range(8)]
            while len(terms) > 1:
                terms = [terms[k] + terms[k + 1] for k in range(0, len(terms), 2)]
            tiles[t] = tiles[t] - terms[0]
    solved = jnp.concatenate(tiles, axis=0)
    coeffs = replicate(lane_group(count), rolls(solved), GROUPS - 1)
    none = jnp.zeros((NRHS, LANES), f32)
    row = lax.broadcasted_iota(jnp.int32, (LANES, LANES), 0)
    col = lax.broadcasted_iota(jnp.int32, (LANES, LANES), 1) % NRHS
    first = jnp.where(row == col, 1.0, 0.0)
    padded = jnp.concatenate([coeffs, none], axis=0)
    combo = first - (padded + jnp.concatenate([none, coeffs], axis=0))
    hi, lo = split(jnp.concatenate([padded, combo], axis=1))
    hi, lo = hi.astype(bf16), lo.astype(bf16)
    twice = jnp.concatenate([hi, hi], axis=0)

    @pl.loop(0, faces // 4, unroll=True)
    def _(quad):
        rows = pl.ds(pl.multiple_of(quad * 4 * DOF, 4 * DOF), 4 * DOF)
        left = vbuf[rows, :]
        out = jnp.dot(left, twice, preferred_element_type=f32)
        wide_part = out + jnp.dot(left[:, :LANES], lo, preferred_element_type=f32)
        wide[0, rows, :] = wide_part[:, :LANES]
        wide[1, rows, :] = wide_part[:, LANES:]
    for part, out_ref in enumerate((sol_ref, res_ref)):
        for block in range(faces // 8):
            for tile in range(DOF // GROUPS):
                parts = [
                    wide[part, pl.ds(8 * block * DOF + tile * GROUPS + q, 8, stride=DOF), :] for q in range(GROUPS)
                ]
                out_ref[8 * block:8 * block + 8, tile * LANES:(tile + 1) * LANES] = pick(g8, parts)
    for copy in gather:
        copy.wait_send()


def on_device(shape, right_side, coupling, face_columns, ghost_lists):
    n_fx, n_fy, low, faces = shape
    plane = low * n_fy
    high = n_fx // low
    share = LANES // plane
    rows = faces * DOF
    vmem = pl.BlockSpec(memory_space=pltpu.VMEM)
    hbm = pl.BlockSpec(memory_space=pltpu.HBM)
    dma = pltpu.SemaphoreType.DMA
    out = jax.ShapeDtypeStruct(right_side.shape, f32)
    return pl.pallas_call(
        functools.partial(kernel, shape),
        out_shape=(out, out),
        in_specs=[hbm] * 4,
        out_specs=(vmem, vmem),
        scratch_shapes=[
            pltpu.VMEM(right_side.shape, f32),
            pltpu.SMEM(face_columns.shape, jnp.int32),
            pltpu.SMEM(ghost_lists.shape, jnp.int32),
            pltpu.VMEM(coupling.shape, f32),
            pltpu.VMEM((2, faces * HALF, LANES), f32),
            pltpu.VMEM((faces, DOF, BLOCKS * LANES), bf16),
        ]
        + [pltpu.VMEM((faces, DOF, LANES), f32)] * (POWERS + 1)
        + [
            pltpu.VMEM((faces + 4 * GROUPS, LANES, LANES), bf16),
            pltpu.VMEM((faces, HALF, LANES), f32),
            pltpu.VMEM((POWERS, 4, DOF, LANES), f32),
            pltpu.VMEM((POWERS, 4, DOF, LANES), f32),
            pltpu.VMEM((rows, 2 * LANES), bf16),
            pltpu.VMEM((rows, 2 * LANES), bf16),
            pltpu.VMEM((plane, share, LANES), f32),
            pltpu.VMEM((plane, share, LANES), f32),
            pltpu.VMEM((high, share, LANES), f32),
            pltpu.VMEM((plane, share, LANES), f32),
            pltpu.VMEM((2, rows, LANES), f32),
            dma((3,)),
            dma((BLOCKS,)),
            dma((POWERS, 4)),
            dma((POWERS, 4)),
            dma((plane,)),
            dma((plane,)),
            dma((high,)),
            dma((high,)),
            dma((plane,)),
            dma((plane,)),
        ],
        compiler_params=pltpu.CompilerParams(
            collective_id=0, has_side_effects=True, vmem_limit_bytes=40 * 2**20
        ),
    )(*[pltpu.with_memory_space_constraint(x, pltpu.HBM) for x in (right_side, coupling, face_columns, ghost_lists)])


def solution(mesh):
    n_fx, n_fy = mesh.shape["fx"], mesh.shape["fy"]
    low = 1
    while low * low * 4 <= n_fx:
        low *= 2

    def body(right_side, coupling, face_columns, ghost_lists):
        shape = (n_fx, n_fy, low, right_side.shape[0])
        return on_device(shape, right_side, coupling.transpose(1, 0, 2), face_columns, ghost_lists)

    placed = (
        P(("fx", "fy"), None),
        P(("fx", "fy"), None, None),
        P(("fx", "fy"), None),
        P(("fx", "fy"), None),
    )
    return jax.shard_map(
        body,
        mesh=mesh,
        in_specs=placed,
        out_specs=(P(("fx", "fy"), None), P(("fx", "fy"), None)),
        check_vma=False,
    )
```

```python
import contextlib
import functools

import jax
import jax.numpy as jnp
from jax import lax
from jax.experimental import pallas as pl
from jax.experimental.pallas import tpu as pltpu
from jax.sharding import PartitionSpec as P

DOF = 64
NRHS = 32
BLOCKS = 11
OWNED = 7
POWERS = 3
LANES = 128
HALF = DOF // 2
BATCH = 3
GROUPS = LANES // NRHS
MESH = pl.DeviceIdType.MESH
f32 = jnp.float32
bf16 = jnp.bfloat16


def split(x):
    hi = x.astype(bf16).astype(f32)
    return hi, x - hi


def lane_group(rows):
    return lax.broadcasted_iota(jnp.int32, (rows, LANES), 1) // NRHS


def pick(group, parts):
    out = parts[-1]
    for index in range(len(parts) - 2, -1, -1):
        out = jnp.where(group == index, parts[index], out)
    return out


def replicate(group, rolled, source):
    return pick(group, [rolled[(lane - source) % GROUPS] for lane in range(GROUPS)])


def rolls(x):
    return [x] + [pltpu.roll(x, step * NRHS, 1) for step in range(1, GROUPS)]


def product_tile(x, group):
    hi, lo = split(x)
    zero = jnp.zeros_like(x)
    top = pick(group, [hi, zero, lo, zero])
    bottom = pick(group, [zero, hi, zero, lo])
    return top.astype(bf16), bottom.astype(bf16)


def scope(name):
    return contextlib.nullcontext()


def eliminate(tiles, inverse):
    tiles = list(tiles)
    sub = lax.broadcasted_iota(jnp.int32, (8, LANES), 0)
    lanes = lax.broadcasted_iota(jnp.int32, (8, LANES), 1)

    def across(x, lane):
        return jnp.broadcast_to(x[:, lane:lane + 1], (8, LANES))

    def down(x, row):
        return jnp.broadcast_to(x[row:row + 1, :], (8, LANES))

    for home in range(len(tiles)):
        mine = tiles[home]
        cols = [across(mine, 8 * home + c) for c in range(8)]
        for step in range(8):
            pivot = 1.0 / down(cols[step], step)
            here = sub == step
            factor = cols[step]
            if inverse:
                mine = jnp.where(lanes == 8 * home + step, jnp.where(here, 1.0, 0.0), mine)
            scaled = down(mine, step) * pivot
            mine = jnp.where(here, scaled, mine - factor * scaled)
            for c in range(step + 1, 8):
                scaled = down(cols[c], step) * pivot
                cols[c] = jnp.where(here, scaled, cols[c] - factor * scaled)
        tiles[home] = mine
        rows8 = [down(mine, c) for c in range(8)]
        for t in [t % len(tiles) for t in range(home + 1, home + len(tiles))]:
            terms = [across(tiles[t], 8 * home + c) * rows8[c] for c in range(8)]
            while len(terms) > 1:
                terms = [terms[k] + terms[k + 1] for k in range(0, len(terms), 2)]
            base = jnp.where(lanes // 8 == home, 0.0, tiles[t]) if inverse else tiles[t]
            tiles[t] = base - terms[0]
    return jnp.concatenate(tiles, axis=0)


def high_dot(left, right, dims):
    return lax.dot_general(left, right, (dims, ((), ())), precision=lax.Precision.HIGHEST, preferred_element_type=f32)


def kernel(shape, right_hbm, coupling_hbm, columns_hbm, ghost_hbm, sol_ref, res_ref,
           right_ref, columns_ref, ghost_ref,
           stage, spread, mats, w0, w1, w2, w3, tiles, acc, send_buf, recv_buf,
           zbuf, newest, vbuf, early_buf, early_plane, early_line, early_all,
           late_buf, late_plane, late_line, late_all, wide,
           small_sem, load_sem, send_sem, recv_sem, gram_sem):
    n_fx, n_fy, low, faces = shape
    plane = low * n_fy
    high = n_fx // low
    i = lax.axis_index("fx")
    j = lax.axis_index("fy")
    my_low = i % low
    my_high = i // low
    my_rank = my_low * n_fy + j
    fields = [w0, w1, w2, w3]

    def plane_target(offset):
        rank = lax.rem(my_rank + offset, plane)
        return rank, (my_high * low + rank // n_fy, rank % n_fy)

    def line_target(offset):
        place = lax.rem(my_high + offset, high)
        return (place * low + my_low, j)

    routes = [
        (1, i < n_fx - 1, (i + 1, j), i > 0),
        (0, i > 0, (i - 1, j), i < n_fx - 1),
        (3, j < n_fy - 1, (i, j + 1), j > 0),
        (2, j > 0, (i, j - 1), j < n_fy - 1),
    ]

    small = [
        pltpu.make_async_copy(src, dst, small_sem.at[place])
        for place, (src, dst) in enumerate([
            (right_hbm, right_ref), (ghost_hbm, ghost_ref), (columns_hbm, columns_ref),
        ])
    ]
    for load in small:
        load.start()
    batches = [(k, min(k + BATCH, BLOCKS)) for k in range(0, BLOCKS, BATCH)]
    loads = [
        pltpu.make_async_copy(coupling_hbm.at[first:last], stage.at[first:last], load_sem.at[place])
        for place, (first, last) in enumerate(batches)
    ]
    for load in loads:
        load.start()

    barrier = pltpu.get_barrier_semaphore()
    for _, has_target, target, _ in routes:
        @pl.when(has_target)
        def _(target=target):
            pl.semaphore_signal(barrier, inc=1, device_id=target, device_id_type=MESH)
    for offset in range(1, plane):
        pl.semaphore_signal(barrier, inc=1, device_id=plane_target(offset)[1], device_id_type=MESH)
    for offset in range(1, high):
        pl.semaphore_signal(barrier, inc=1, device_id=line_target(offset), device_id_type=MESH)

    g8 = lane_group(8)
    g64 = lane_group(DOF)
    g32 = lane_group(HALF)

    with scope("relay"):
        small[0].wait()
        for block in range(faces // 8):
            for tile in range(DOF // GROUPS):
                x = right_ref[8 * block:8 * block + 8, tile * LANES:(tile + 1) * LANES]
                moved = rolls(x)
                for q in range(GROUPS):
                    wide[pl.ds(8 * block * DOF + tile * GROUPS + q, 8, stride=DOF), :] = replicate(g8, moved, q)
        for face in range(faces):
            w0[face] = wide[face * DOF:(face + 1) * DOF, :]
        small[1].wait()

    def field_copies(power):
        return [
            pltpu.make_async_remote_copy(
                src_ref=send_buf.at[power, q], dst_ref=recv_buf.at[power, q],
                send_sem=send_sem.at[q], recv_sem=recv_sem.at[power % 2, q],
                device_id=routes[q][2], device_id_type=MESH,
            )
            for q in range(4)
        ]

    def send_field(power):
        field = fields[power]
        copies = field_copies(power)
        for q, (row, _, _, _) in enumerate(routes):
            picked = [field[ghost_ref[row, g]] for g in range(GROUPS)]
            send_buf[power, q] = pick(g64, picked)
        if power == 0:
            count = sum(jnp.where(route[1], 1, 0) for route in routes) + (plane - 1) + (high - 1)
            pl.semaphore_wait(barrier, count)
        far_down = my_low == 0
        starts = [
            (1, jnp.logical_and(routes[1][1], far_down)),
            (0, routes[0][1]),
            (1, jnp.logical_and(routes[1][1], jnp.logical_not(far_down))),
            (2, routes[2][1]),
            (3, routes[3][1]),
        ]
        for q, needed in starts:
            @pl.when(needed)
            def _(copy=copies[q]):
                copy.start()
        return copies

    def build_own(power):
        field = fields[power]

        @pl.loop(0, faces, unroll=4)
        def _(face):
            x = field[face]
            top, bottom = product_tile(x, g64)
            tiles[face, 0:DOF] = top
            tiles[face, DOF:2 * DOF] = bottom

    def own_products():
        for face in range(faces):
            left = jnp.concatenate([mats[face * BLOCKS + k] for k in range(OWNED)], axis=1)
            right = jnp.concatenate([tiles[columns_ref[face, k]] for k in range(OWNED)], axis=0)
            out = jnp.dot(left, right, preferred_element_type=f32)
            acc[face] = out[:HALF] + out[HALF:]

    def far_products(power):
        field = fields[power + 1]
        for face in range(faces):
            left = jnp.concatenate([mats[face * BLOCKS + k] for k in range(OWNED, BLOCKS)], axis=1)
            right = jnp.concatenate([tiles[columns_ref[face, k]] for k in range(OWNED, BLOCKS)], axis=0)
            out = jnp.dot(left, right, preferred_element_type=f32)
            total = acc[face] + (out[:HALF] + out[HALF:])
            total = total + pltpu.roll(total, LANES // 2, 1)
            turned = pltpu.roll(total, NRHS, 1)
            even = g32 % 2 == 0
            field[face, pl.ds(0, HALF, stride=2), :] = jnp.where(even, total, turned)
            field[face, pl.ds(1, HALF, stride=2), :] = jnp.where(even, turned, total)

    def receive_field(power, copies):
        for q in (2, 3, 0, 1):
            _, has_target, _, has_source = routes[q]

            with scope("recv%d_%d" % (power, q)):
                @pl.when(has_source)
                def _(copy=copies[q]):
                    copy.wait_recv()

                @pl.when(jnp.logical_not(has_source))
                def _(q=q):
                    recv_buf[power, q] = jnp.zeros((DOF, LANES), f32)
            with scope("conv%d_%d" % (power, q)):
                moved = rolls(recv_buf[power, q])
                for g in range(GROUPS):
                    top, bottom = product_tile(replicate(g64, moved, g), g64)
                    tiles[faces + q * GROUPS + g, 0:DOF] = top
                    tiles[faces + q * GROUPS + g, DOF:2 * DOF] = bottom

            @pl.when(has_target)
            def _(copy=copies[q]):
                copy.wait_send()

    def prepare():
        for k in range(BLOCKS):
            for place, (first, _) in enumerate(batches):
                if first == k:
                    loads[place].wait()
            for block in range(faces // 8):
                for t in range(HALF):
                    spread[k % 2, pl.ds(8 * block * HALF + t, 8, stride=HALF), :] = stage[
                        k, 8 * block:8 * block + 8, t * LANES:(t + 1) * LANES]
            for face in range(faces):
                hi, lo = split(spread[k % 2, face * HALF:(face + 1) * HALF, :])
                mats[face * BLOCKS + k, 0:HALF] = hi.astype(bf16)
                mats[face * BLOCKS + k, HALF:DOF] = lo.astype(bf16)

    def wait_for(buf, count, sem):
        whole = buf.at[0:count]
        pltpu.make_async_copy(whole, whole, sem).wait()

    def scatter(which, buf, landed):
        for offset in range(1, plane):
            rank, target = plane_target(offset)
            pltpu.make_async_remote_copy(
                src_ref=buf.at[rank], dst_ref=landed.at[offset - 1], send_sem=gram_sem.at[which, 0],
                recv_sem=gram_sem.at[which, 1], device_id=target, device_id_type=MESH).start()

    def scatter_sum(which, buf, landed):
        total = buf[my_rank]
        wait_for(landed, plane - 1, gram_sem.at[which, 1])
        for offset in range(1, plane):
            total = total + landed[offset - 1]
        return total

    def exchange(which, line, total):
        line[my_high] = total
        for offset in range(1, high):
            pltpu.make_async_remote_copy(
                src_ref=line.at[my_high], dst_ref=line.at[my_high], send_sem=gram_sem.at[which, 2],
                recv_sem=gram_sem.at[which, 3], device_id=line_target(offset), device_id_type=MESH).start()

    def exchange_sum(which, line):
        wait_for(line, high - 1, gram_sem.at[which, 3])
        total = line[0]
        for place in range(1, high):
            total = total + line[place]
        return total

    def gather(which, final, total):
        final[my_rank] = total
        for offset in range(1, plane):
            pltpu.make_async_remote_copy(
                src_ref=final.at[my_rank], dst_ref=final.at[my_rank], send_sem=gram_sem.at[which, 4],
                recv_sem=gram_sem.at[which, 5], device_id=plane_target(offset)[1], device_id_type=MESH).start()

    def gathered(which, final):
        wait_for(final, plane - 1, gram_sem.at[which, 5])
        return jnp.concatenate([final[rank] for rank in range(plane)], axis=0)

    def early_gram():
        @pl.loop(0, faces, unroll=4)
        def _(face):
            rows = pl.ds(pl.multiple_of(face * DOF, DOF), DOF)
            a, b, c = w0[face], w1[face], w2[face]
            hi, lo = split(pick(g64, [a + b, b + c, jnp.zeros_like(a), a]))
            zbuf[rows, :LANES] = hi.astype(bf16)
            zbuf[rows, LANES:] = lo.astype(bf16)

        z = zbuf[...]
        both = lax.dot_general(z, z, (((0,), (0,)), ((), ())), preferred_element_type=f32)
        gram = (both[:LANES, :LANES] + both[LANES:, LANES:]) + (both[:LANES, LANES:] + both[LANES:, :LANES])
        share = early_buf.shape[1]
        for rank in range(plane):
            early_buf[rank] = gram[rank * share:(rank + 1) * share]

    def late_gram():
        @pl.loop(0, faces, unroll=4)
        def _(face):
            rows = pl.ds(pl.multiple_of(face * DOF, DOF), DOF)
            hi, lo = split(w2[face] + w3[face])
            zero = jnp.zeros_like(hi)
            zbuf[rows, :LANES] = zbuf[rows, :LANES] + pick(g64, [zero, zero, hi, zero]).astype(bf16)
            zbuf[rows, LANES:] = zbuf[rows, LANES:] + pick(g64, [zero, zero, lo, zero]).astype(bf16)
            newest[rows, :] = pick(g64, [hi, lo, zero, zero]).astype(bf16)

        both = lax.dot_general(newest[...], zbuf[...], (((0,), (0,)), ((), ())), preferred_element_type=f32)
        gram = (both[:NRHS, :LANES] + both[NRHS:2 * NRHS, LANES:]) + (both[:NRHS, LANES:] + both[NRHS:2 * NRHS, :LANES])
        share = late_buf.shape[1]
        for rank in range(plane):
            late_buf[rank] = gram[rank * share:(rank + 1) * share]

    flat = [field.reshape(faces * DOF, LANES) for field in fields]

    def order_rows():
        for block in range(faces // 8):
            for pair in range(DOF // GROUPS // 2):
                for q in range(GROUPS):
                    halves = []
                    for tile in (2 * pair, 2 * pair + 1):
                        at = pl.ds(8 * block * DOF + tile * GROUPS + q, 8, stride=DOF)
                        halves.append(pick(g8, [view[at, :] for view in flat]))
                    hi, lo = split(jnp.concatenate(halves, axis=0))
                    row = 8 * (block * (DOF // GROUPS) + 2 * pair)
                    vbuf[q, row:row + 16, :LANES] = hi.astype(bf16)
                    vbuf[q, row:row + 16, LANES:] = lo.astype(bf16)

    for power in range(POWERS):
        with scope("send%d" % power):
            copies = send_field(power)
        with scope("build%d" % power):
            build_own(power)
        if power == 0:
            with scope("prepare"):
                prepare()
                small[2].wait()
        if power == POWERS - 1:
            with scope("egram"):
                early_gram()
                scatter(0, early_buf, early_plane)
        with scope("own%d" % power):
            own_products()
        receive_field(power, copies)
        with scope("far%d" % power):
            far_products(power)

    with scope("lgram"):
        late_gram()
        scatter(1, late_buf, late_plane)
    with scope("eplane"):
        exchange(0, early_line, scatter_sum(0, early_buf, early_plane))
    with scope("order"):
        order_rows()
    with scope("lplane"):
        exchange(1, late_line, scatter_sum(1, late_buf, late_plane))
    with scope("eline"):
        gather(0, early_all, exchange_sum(0, early_line))
    with scope("lline"):
        gather(1, late_all, exchange_sum(1, late_line))
    with scope("eall"):
        system = gathered(0, early_all)
    with scope("esolve"):
        count = 2 * NRHS
        solved = eliminate([system[t:t + 8] for t in range(0, count, 8)], True)
        spread_early = replicate(lane_group(count), rolls(solved), GROUPS - 1)
    with scope("lall"):
        last = gathered(1, late_all)
    with scope("lsolve"):
        left_half = lax.broadcasted_iota(jnp.int32, (NRHS, LANES), 1) < count
        cross = jnp.where(left_half, last, 0.0)
        pad = jnp.zeros((LANES - count, LANES), f32)
        done = high_dot(cross, jnp.concatenate([solved, pad], axis=0), ((1,), (0,)))
        inner = jnp.where(left_half, done, 0.0)
        schur = high_dot(inner, jnp.concatenate([cross, jnp.zeros((LANES - NRHS, LANES), f32)], axis=0), ((1,), (1,)))
        small_system = pltpu.roll(jnp.where(left_half, 0.0, last - done), LANES // 2, 1) - schur
        newest_part = eliminate([small_system[t:t + 8] for t in range(0, NRHS, 8)], False)
        newest_part = replicate(g32, rolls(newest_part), 1)
        older = spread_early - high_dot(inner, newest_part, ((0,), (0,)))[:count]
        coeffs = jnp.concatenate([older, newest_part], axis=0)
    with scope("coeffs"):
        none = jnp.zeros((NRHS, LANES), f32)
        row = lax.broadcasted_iota(jnp.int32, (LANES, LANES), 0)
        col = lax.broadcasted_iota(jnp.int32, (LANES, LANES), 1) % NRHS
        first = jnp.where(row == col, 1.0, 0.0)
        padded = jnp.concatenate([coeffs, none], axis=0)
        combo = first - (padded + jnp.concatenate([none, coeffs], axis=0))
        hi, lo = split(jnp.concatenate([padded, combo], axis=1))
        group = lax.broadcasted_iota(jnp.int32, (LANES, 2 * LANES), 1) % LANES // NRHS
        his = [jnp.where(group == q, hi, 0.0).astype(bf16) for q in range(GROUPS)]
        los = [jnp.where(group == q, lo, 0.0).astype(bf16) for q in range(GROUPS)]
        right = jnp.concatenate(his + his + los, axis=0)
    with scope("outdot"):
        vhi = [vbuf[q, :, :LANES] for q in range(GROUPS)]
        vlo = [vbuf[q, :, LANES:] for q in range(GROUPS)]
        out = jnp.dot(jnp.concatenate(vhi + vlo + vhi, axis=1), right, preferred_element_type=f32)
        for part, out_ref in enumerate((sol_ref, res_ref)):
            for block in range(faces // 8):
                for tile in range(DOF // GROUPS):
                    row = 8 * (block * (DOF // GROUPS) + tile)
                    out_ref[8 * block:8 * block + 8, tile * LANES:(tile + 1) * LANES] = out[
                        row:row + 8, part * LANES:(part + 1) * LANES]
    with scope("drain"):
        for which, bufs in enumerate([(early_plane, early_line, early_all), (late_plane, late_line, late_all)]):
            for phase, (buf, amount) in enumerate(zip(bufs, (plane - 1, high - 1, plane - 1))):
                wait_for(buf, amount, gram_sem.at[which, 2 * phase])


def on_device(shape, right_side, coupling, face_columns, ghost_lists):
    n_fx, n_fy, low, faces = shape
    plane = low * n_fy
    high = n_fx // low
    rows = faces * DOF
    early = 2 * NRHS // plane
    late = NRHS // plane
    vmem = pl.BlockSpec(memory_space=pltpu.VMEM)
    hbm = pl.BlockSpec(memory_space=pltpu.HBM)
    dma = pltpu.SemaphoreType.DMA
    i32 = jnp.int32
    out = jax.ShapeDtypeStruct(right_side.shape, f32)
    gram = []
    for share in (early, late):
        gram += [
            pltpu.VMEM((plane, share, LANES), f32),
            pltpu.VMEM((plane - 1, share, LANES), f32),
            pltpu.VMEM((high, share, LANES), f32),
            pltpu.VMEM((plane, share, LANES), f32),
        ]
    return pl.pallas_call(
        functools.partial(kernel, shape),
        out_shape=(out, out),
        in_specs=[hbm] * 4,
        out_specs=(vmem, vmem),
        scratch_shapes=[
            pltpu.VMEM(right_side.shape, f32),
            pltpu.SMEM(face_columns.shape, i32),
            pltpu.SMEM(ghost_lists.shape, i32),
            pltpu.VMEM(coupling.shape, f32),
            pltpu.VMEM((2, faces * HALF, LANES), f32),
            pltpu.VMEM((faces * BLOCKS, DOF, LANES), bf16),
        ]
        + [pltpu.VMEM((faces, DOF, LANES), f32)] * (POWERS + 1)
        + [
            pltpu.VMEM((faces + 4 * GROUPS, LANES, LANES), bf16),
            pltpu.VMEM((faces, HALF, LANES), f32),
            pltpu.VMEM((POWERS, 4, DOF, LANES), f32),
            pltpu.VMEM((POWERS, 4, DOF, LANES), f32),
            pltpu.VMEM((rows, 2 * LANES), bf16),
            pltpu.VMEM((rows, LANES), bf16),
            pltpu.VMEM((GROUPS, rows // GROUPS, 2 * LANES), bf16),
        ]
        + gram
        + [
            pltpu.VMEM((rows, LANES), f32),
            dma((3,)),
            dma((-(-BLOCKS // BATCH),)),
            dma((4,)),
            dma((2, 4)),
            dma((2, 6)),
        ],
        compiler_params=pltpu.CompilerParams(
            collective_id=0, has_side_effects=True, vmem_limit_bytes=40 * 2**20
        ),
    )(*[pltpu.with_memory_space_constraint(x, pltpu.HBM) for x in (right_side, coupling, face_columns, ghost_lists)])


def solution(mesh):
    n_fx, n_fy = mesh.shape["fx"], mesh.shape["fy"]
    low = 1
    while low * low * 4 <= n_fx:
        low *= 2

    def body(right_side, coupling, face_columns, ghost_lists):
        shape = (n_fx, n_fy, low, right_side.shape[0])
        return on_device(shape, right_side, coupling.transpose(1, 0, 2), face_columns, ghost_lists)

    placed = (
        P(("fx", "fy"), None),
        P(("fx", "fy"), None, None),
        P(("fx", "fy"), None),
        P(("fx", "fy"), None),
    )
    return jax.shard_map(
        body,
        mesh=mesh,
        in_specs=placed,
        out_specs=(P(("fx", "fy"), None), P(("fx", "fy"), None)),
        check_vma=False,
    )
```

```python
import contextlib
import functools

import jax
import jax.numpy as jnp
from jax import lax
from jax.experimental import pallas as pl
from jax.experimental.pallas import tpu as pltpu
from jax.sharding import PartitionSpec as P

DOF = 64
NRHS = 32
BLOCKS = 11
OWNED = 7
POWERS = 3
LANES = 128
HALF = DOF // 2
BATCH = 3
TOKENS = 2 * (POWERS - 1)
GROUPS = LANES // NRHS
MESH = pl.DeviceIdType.MESH
f32 = jnp.float32
bf16 = jnp.bfloat16


def split(x):
    hi = x.astype(bf16).astype(f32)
    return hi, x - hi


def lane_group(rows):
    return lax.broadcasted_iota(jnp.int32, (rows, LANES), 1) // NRHS


def pick(group, parts):
    out = parts[-1]
    for index in range(len(parts) - 2, -1, -1):
        out = jnp.where(group == index, parts[index], out)
    return out


def replicate(group, rolled, source):
    return pick(group, [rolled[(lane - source) % GROUPS] for lane in range(GROUPS)])


def rolls(x):
    return [x] + [pltpu.roll(x, step * NRHS, 1) for step in range(1, GROUPS)]


def product_tile(x, group):
    hi, lo = split(x)
    zero = jnp.zeros_like(x)
    top = pick(group, [hi, zero, lo, zero])
    bottom = pick(group, [zero, hi, zero, lo])
    return top.astype(bf16), bottom.astype(bf16)


def scope(name):
    return contextlib.nullcontext()


def eliminate(tiles, inverse):
    sub = lax.broadcasted_iota(jnp.int32, (8, LANES), 0)
    lanes = lax.broadcasted_iota(jnp.int32, (8, LANES), 1)

    def across(x, lane):
        return jnp.broadcast_to(x[:, lane:lane + 1], (8, LANES))

    def down(x, row):
        return jnp.broadcast_to(x[row:row + 1, :], (8, LANES))

    scales = []
    for home, tile in enumerate(tiles):
        diagonal = jnp.sum(jnp.where(lanes == 8 * home + sub, tile, 0.0), axis=1, keepdims=True)
        scales.append(1.0 / jnp.broadcast_to(diagonal, (8, LANES)))
    tiles = [tile * scale for tile, scale in zip(tiles, scales)]

    for home in range(len(tiles)):
        mine = tiles[home]
        cols = [across(mine, 8 * home + c) for c in range(8)]
        for p in range(0, 8, 2):
            q = p + 1
            left, right = cols[p], cols[q]
            a, b, c, d = down(left, p), down(right, p), down(left, q), down(right, q)
            pivot = 1.0 / (a * d - b * c)

            def update(x):
                top, bottom = down(x, p), down(x, q)
                top, bottom = d * top - b * bottom, a * bottom - c * top
                rest = x - pivot * (left * top + right * bottom)
                return jnp.where(sub == p, pivot * top, jnp.where(sub == q, pivot * bottom, rest))

            if inverse:
                own = jnp.where(lanes == 8 * home + sub, scales[home], 0.0)
                mine = jnp.where((lanes == 8 * home + p) | (lanes == 8 * home + q), jnp.where((sub == p) | (sub == q), own, 0.0), mine)
            mine = update(mine)
            cols = [update(x) if place > q else x for place, x in enumerate(cols)]
        tiles[home] = mine
        rows8 = [down(mine, c) for c in range(8)]
        for t in [t % len(tiles) for t in range(home + 1, home + len(tiles))]:
            terms = [across(tiles[t], 8 * home + c) * rows8[c] for c in range(8)]
            while len(terms) > 1:
                terms = [terms[k] + terms[k + 1] for k in range(0, len(terms), 2)]
            base = jnp.where(lanes // 8 == home, 0.0, tiles[t]) if inverse else tiles[t]
            tiles[t] = base - terms[0]
    return jnp.concatenate(tiles, axis=0)


def high_dot(left, right, dims):
    return lax.dot_general(left, right, (dims, ((), ())), precision=lax.Precision.HIGHEST, preferred_element_type=f32)


def kernel(shape, right_hbm, coupling_hbm, columns_hbm, ghost_hbm, sol_ref, res_ref,
           right_ref, columns_ref, ghost_ref,
           stage, mats, w0, w1, w2, w3, tiles, acc, send_buf, recv_buf,
           zbuf, newest, vbuf, early_buf, early_plane, early_line, early_all,
           late_plane, late_line,
           small_sem, load_sem, send_sem, recv_sem, gram_sem, token_sem):
    n_fx, n_fy, low, faces = shape
    plane = low * n_fy
    high = n_fx // low
    i = lax.axis_index("fx")
    j = lax.axis_index("fy")
    my_low = i % low
    my_high = i // low
    my_rank = my_low * n_fy + j
    fields = [w0, w1, w2, w3]

    def plane_target(offset):
        rank = lax.rem(my_rank + offset, plane)
        return rank, (my_high * low + rank // n_fy, rank % n_fy)

    def line_target(offset):
        place = lax.rem(my_high + offset, high)
        return (place * low + my_low, j)

    routes = [
        (1, i < n_fx - 1, (i + 1, j), i > 0),
        (0, i > 0, (i - 1, j), i < n_fx - 1),
        (3, j < n_fy - 1, (i, j + 1), j > 0),
        (2, j > 0, (i, j - 1), j < n_fy - 1),
    ]

    small = [
        pltpu.make_async_copy(src, dst, small_sem.at[place])
        for place, (src, dst) in enumerate([
            (ghost_hbm, ghost_ref), (columns_hbm, columns_ref),
        ])
    ]
    rights = [
        pltpu.make_async_copy(right_hbm.at[:, :, s], right_ref.at[:, s], small_sem.at[2]) for s in range(8)
    ]
    for load in rights + small:
        load.start()
    batches = [(k, min(k + BATCH, BLOCKS)) for k in range(0, BLOCKS, BATCH)]
    loads = [
        [
            pltpu.make_async_copy(coupling_hbm.at[k, :, :, s], stage.at[k, :, s], load_sem.at[place])
            for k in range(first, last) for s in range(8)
        ]
        for place, (first, last) in enumerate(batches)
    ]
    barrier = pltpu.get_barrier_semaphore()
    for _, has_target, target, _ in routes:
        @pl.when(has_target)
        def _(target=target):
            pl.semaphore_signal(barrier, inc=1, device_id=target, device_id_type=MESH)
    reach = TOKENS + 1
    neighbours = sum(jnp.where(route[1], 1, 0) for route in routes)
    strangers = []
    if low + n_fy - 2 > reach:
        for offset in range(1, plane):
            target = plane_target(offset)[1]
            strangers.append((jnp.abs(target[0] - i) + jnp.abs(target[1] - j) > reach, target))
    if (high - 1) * low > reach + 1:
        for offset in range(1, high):
            target = line_target(offset)
            strangers.append((jnp.abs(target[0] - i) > reach + 1, target))
    for strange, target in strangers:
        @pl.when(strange)
        def _(target=target):
            pl.semaphore_signal(barrier, inc=1, device_id=target, device_id_type=MESH)

    def pass_token(place):
        for _, has_target, target, _ in routes:
            @pl.when(has_target)
            def _(target=target):
                pl.semaphore_signal(token_sem.at[place], inc=1, device_id=target, device_id_type=MESH)

    def take_token(place):
        pl.semaphore_wait(token_sem.at[place], neighbours)

    for batch in loads:
        for load in batch:
            load.start()

    g8 = lane_group(8)
    g64 = lane_group(DOF)
    g32 = lane_group(HALF)

    with scope("relay"):
        pltpu.make_async_copy(right_ref, right_ref, small_sem.at[2]).wait()
        sub = lax.broadcasted_iota(jnp.int32, (8, LANES), 0)
        turn = (g8 - sub) % GROUPS
        for face in range(faces):
            for tile in range(0, DOF // GROUPS, 2):
                x = right_ref[face // 8, face % 8, tile:tile + 2, :]
                x = jnp.where(sub < GROUPS, jnp.broadcast_to(x[0:1], (8, LANES)), jnp.broadcast_to(x[1:2], (8, LANES)))
                w0[face, tile * GROUPS:tile * GROUPS + 8, :] = pick(turn, rolls(x))
        small[0].wait()

    def field_copies(power):
        return [
            pltpu.make_async_remote_copy(
                src_ref=send_buf.at[power, q], dst_ref=recv_buf.at[power, q],
                send_sem=send_sem.at[q], recv_sem=recv_sem.at[power % 2, q],
                device_id=routes[q][2], device_id_type=MESH,
            )
            for q in range(4)
        ]

    def send_field(power):
        field = fields[power]
        copies = field_copies(power)
        for q, (row, _, _, _) in enumerate(routes):
            picked = [field[ghost_ref[row, g]] for g in range(GROUPS)]
            send_buf[power, q] = pick(g64, picked)
        if power == 0:
            pl.semaphore_wait(barrier, neighbours + sum(jnp.where(strange, 1, 0) for strange, _ in strangers))
            pass_token(0)
        for copy, route in zip(copies, routes):
            @pl.when(route[1])
            def _(copy=copy):
                copy.start()
        return copies

    def build_own(power):
        field = fields[power]

        @pl.loop(0, faces, unroll=4)
        def _(face):
            x = field[face]
            top, bottom = product_tile(x, g64)
            tiles[face, 0:DOF] = top
            tiles[face, DOF:2 * DOF] = bottom

    def own_products():
        for face in range(faces):
            left = mats[face, :, :OWNED * LANES]
            right = jnp.concatenate([tiles[columns_ref[face, k]] for k in range(OWNED)], axis=0)
            out = jnp.dot(left, right, preferred_element_type=f32)
            acc[face] = out[:HALF] + out[HALF:]

    def far_products(power):
        field = fields[power + 1]
        for face in range(faces):
            left = mats[face, :, OWNED * LANES:]
            right = jnp.concatenate([tiles[columns_ref[face, k]] for k in range(OWNED, BLOCKS)], axis=0)
            out = jnp.dot(left, right, preferred_element_type=f32)
            total = acc[face] + (out[:HALF] + out[HALF:])
            total = total + pltpu.roll(total, LANES // 2, 1)
            turned = pltpu.roll(total, NRHS, 1)
            even = g32 % 2 == 0
            field[face, pl.ds(0, HALF, stride=2), :] = jnp.where(even, total, turned)
            field[face, pl.ds(1, HALF, stride=2), :] = jnp.where(even, turned, total)

    def receive_field(power, copies):
        for q in (2, 3, 0, 1):
            _, has_target, _, has_source = routes[q]

            with scope("recv%d_%d" % (power, q)):
                @pl.when(has_source)
                def _(copy=copies[q]):
                    copy.wait_recv()

                @pl.when(jnp.logical_not(has_source))
                def _(q=q):
                    recv_buf[power, q] = jnp.zeros((DOF, LANES), f32)
            with scope("conv%d_%d" % (power, q)):
                moved = rolls(recv_buf[power, q])
                for g in range(GROUPS):
                    top, bottom = product_tile(replicate(g64, moved, g), g64)
                    tiles[faces + q * GROUPS + g, 0:DOF] = top
                    tiles[faces + q * GROUPS + g, DOF:2 * DOF] = bottom

            @pl.when(has_target)
            def _(copy=copies[q]):
                copy.wait_send()

    def prepare():
        for place, (first, last) in enumerate(batches):
            whole = stage.at[first:last]
            pltpu.make_async_copy(whole, whole, load_sem.at[place]).wait()
            for k in range(first, last):
                for face in range(faces):
                    hi, lo = split(stage[k, face // 8, face % 8])
                    mats[face, 0:HALF, k * LANES:(k + 1) * LANES] = hi.astype(bf16)
                    mats[face, HALF:DOF, k * LANES:(k + 1) * LANES] = lo.astype(bf16)

    def wait_for(buf, count, sem):
        whole = buf.at[0:count]
        pltpu.make_async_copy(whole, whole, sem).wait()

    def scatter(which, buf, landed):
        for offset in range(1, plane):
            rank, target = plane_target(offset)
            pltpu.make_async_remote_copy(
                src_ref=buf.at[rank], dst_ref=landed.at[offset - 1], send_sem=gram_sem.at[which, 0],
                recv_sem=gram_sem.at[which, 1], device_id=target, device_id_type=MESH).start()

    def scatter_sum(which, buf, landed):
        total = buf[my_rank]
        wait_for(landed, plane - 1, gram_sem.at[which, 1])
        for offset in range(1, plane):
            total = total + landed[offset - 1]
        return total

    def exchange(which, line, total):
        line[my_high] = total
        for offset in range(1, high):
            pltpu.make_async_remote_copy(
                src_ref=line.at[my_high], dst_ref=line.at[my_high], send_sem=gram_sem.at[which, 2],
                recv_sem=gram_sem.at[which, 3], device_id=line_target(offset), device_id_type=MESH).start()

    def add_all(buf, count):
        terms = [buf[place] for place in range(count)]
        while len(terms) > 1:
            terms = [sum(terms[k:k + 2][1:], terms[k]) for k in range(0, len(terms), 2)]
        return terms[0]

    def exchange_sum(which, line):
        wait_for(line, high - 1, gram_sem.at[which, 3])
        return add_all(line, high)

    def gather(which, final, first):
        for offset in range(1, plane):
            pltpu.make_async_remote_copy(
                src_ref=final.at[my_rank], dst_ref=final.at[my_rank], send_sem=gram_sem.at[which, first],
                recv_sem=gram_sem.at[which, first + 1], device_id=plane_target(offset)[1], device_id_type=MESH).start()

    def gathered(which, final):
        wait_for(final, plane - 1, gram_sem.at[which, 5])
        return jnp.concatenate([final[rank] for rank in range(plane)], axis=0)

    def early_gram():
        @pl.loop(0, faces, unroll=4)
        def _(face):
            rows = pl.ds(pl.multiple_of(face * DOF, DOF), DOF)
            a, b, c = w0[face], w1[face], w2[face]
            hi, lo = split(pick(g64, [a + b, b + c, jnp.zeros_like(a), a]))
            zbuf[rows, :LANES] = hi.astype(bf16)
            zbuf[rows, LANES:] = lo.astype(bf16)

        z = zbuf[...]
        both = lax.dot_general(z, z, (((0,), (0,)), ((), ())), preferred_element_type=f32)
        gram = (both[:LANES, :LANES] + both[LANES:, LANES:]) + (both[:LANES, LANES:] + both[LANES:, :LANES])
        share = early_buf.shape[1]
        for rank in range(plane):
            early_buf[rank] = gram[rank * share:(rank + 1) * share]

    def late_gram():
        @pl.loop(0, faces, unroll=4)
        def _(face):
            rows = pl.ds(pl.multiple_of(face * DOF, DOF), DOF)
            hi, lo = split(w2[face] + w3[face])
            zero = jnp.zeros_like(hi)
            zbuf[rows, :LANES] = zbuf[rows, :LANES] + pick(g64, [zero, zero, hi, zero]).astype(bf16)
            zbuf[rows, LANES:] = zbuf[rows, LANES:] + pick(g64, [zero, zero, lo, zero]).astype(bf16)
            newest[rows, :] = pick(g64, [hi, lo, zero, zero]).astype(bf16)

        both = lax.dot_general(newest[...], zbuf[...], (((0,), (0,)), ((), ())), preferred_element_type=f32)
        gram = (both[:NRHS, :LANES] + both[NRHS:2 * NRHS, LANES:]) + (both[:NRHS, LANES:] + both[NRHS:2 * NRHS, :LANES])
        late_plane[my_rank] = gram

    flat = [field.reshape(faces * DOF, LANES) for field in fields]

    def order_rows():
        for block in range(faces // 8):
            for pair in range(DOF // GROUPS // 2):
                for q in range(GROUPS):
                    halves = []
                    for tile in (2 * pair, 2 * pair + 1):
                        at = pl.ds(8 * block * DOF + tile * GROUPS + q, 8, stride=DOF)
                        halves.append(pick(g8, [view[at, :] for view in flat]))
                    hi, lo = split(jnp.concatenate(halves, axis=0))
                    row = 8 * (block * (DOF // GROUPS) + 2 * pair)
                    vbuf[q, row:row + 16, :LANES] = hi.astype(bf16)
                    vbuf[q, row:row + 16, LANES:] = lo.astype(bf16)

    for power in range(POWERS):
        with scope("send%d" % power):
            copies = send_field(power)
        if power == POWERS - 1:
            with scope("egram"):
                early_gram()
                scatter(0, early_buf, early_plane)
        with scope("build%d" % power):
            build_own(power)
        if power == 0:
            with scope("prepare"):
                prepare()
                small[1].wait()
        with scope("own%d" % power):
            own_products()
        if power < TOKENS // 2:
            take_token(2 * power)
            pass_token(2 * power + 1)
        receive_field(power, copies)
        with scope("far%d" % power):
            far_products(power)
        if power < TOKENS // 2:
            take_token(2 * power + 1)
            if 2 * power + 2 < TOKENS:
                pass_token(2 * power + 2)

    with scope("eplane"):
        exchange(0, early_line, scatter_sum(0, early_buf, early_plane))
    with scope("lgram"):
        late_gram()
        gather(1, late_plane, 0)
    with scope("order"):
        order_rows()
    with scope("lplane"):
        wait_for(late_plane, plane - 1, gram_sem.at[1, 1])
        exchange(1, late_line, add_all(late_plane, plane))
    with scope("eline"):
        early_all[my_rank] = exchange_sum(0, early_line)
        gather(0, early_all, 4)
    with scope("eall"):
        system = gathered(0, early_all)
    with scope("esolve"):
        count = 2 * NRHS
        solved = eliminate([system[t:t + 8] for t in range(0, count, 8)], True)
        spread_early = replicate(lane_group(count), rolls(solved), GROUPS - 1)
    with scope("lall"):
        last = exchange_sum(1, late_line)
    with scope("lsolve"):
        left_half = lax.broadcasted_iota(jnp.int32, (NRHS, LANES), 1) < count
        cross = jnp.where(left_half, last, 0.0)
        pad = jnp.zeros((LANES - count, LANES), f32)
        done = high_dot(cross, jnp.concatenate([solved, pad], axis=0), ((1,), (0,)))
        inner = jnp.where(left_half, done, 0.0)
        outer = high_dot(jnp.where(lax.broadcasted_iota(jnp.int32, (count, LANES), 1) < count, solved, 0.0), jnp.concatenate([cross, jnp.zeros((LANES - NRHS, LANES), f32)], axis=0), ((1,), (1,)))
        schur = high_dot(inner, jnp.concatenate([cross, jnp.zeros((LANES - NRHS, LANES), f32)], axis=0), ((1,), (1,)))
        small_system = pltpu.roll(jnp.where(left_half, 0.0, last - done), LANES // 2, 1) - schur
        newest_part = eliminate([small_system[t:t + 8] for t in range(0, NRHS, 8)], False)
        newest_part = replicate(g32, rolls(newest_part), 1)
        older = spread_early - high_dot(outer[:, :NRHS], newest_part, ((1,), (0,)))
        coeffs = jnp.concatenate([older, newest_part], axis=0)
    with scope("coeffs"):
        none = jnp.zeros((NRHS, LANES), f32)
        row = lax.broadcasted_iota(jnp.int32, (LANES, LANES), 0)
        col = lax.broadcasted_iota(jnp.int32, (LANES, LANES), 1) % NRHS
        first = jnp.where(row == col, 1.0, 0.0)
        padded = jnp.concatenate([coeffs, none], axis=0)
        combo = first - (padded + jnp.concatenate([none, coeffs], axis=0))
        hi, lo = split(jnp.concatenate([padded, combo], axis=1))
        group = lax.broadcasted_iota(jnp.int32, (LANES, 2 * LANES), 1) % LANES // NRHS
        his = [jnp.where(group == q, hi, 0.0).astype(bf16) for q in range(GROUPS)]
        los = [jnp.where(group == q, lo, 0.0).astype(bf16) for q in range(GROUPS)]
        right = jnp.concatenate(his + his + los, axis=0)
    with scope("outdot"):
        vhi = [vbuf[q, :, :LANES] for q in range(GROUPS)]
        vlo = [vbuf[q, :, LANES:] for q in range(GROUPS)]
        out = jnp.dot(jnp.concatenate(vhi + vlo + vhi, axis=1), right, preferred_element_type=f32)
        for part, out_ref in enumerate((sol_ref, res_ref)):
            for block in range(faces // 8):
                for tile in range(DOF // GROUPS):
                    row = 8 * (block * (DOF // GROUPS) + tile)
                    out_ref[8 * block:8 * block + 8, tile * LANES:(tile + 1) * LANES] = out[
                        row:row + 8, part * LANES:(part + 1) * LANES]
    with scope("drain"):
        for which, bufs in enumerate([(early_plane, early_line, early_all), (late_plane, late_line)]):
            for phase, (buf, amount) in enumerate(zip(bufs, (plane - 1, high - 1, plane - 1))):
                wait_for(buf, amount, gram_sem.at[which, 2 * phase])


def put_out(sol_ref, res_ref, sol_out, res_out, sem):
    copies = [
        pltpu.make_async_copy(sol_ref, sol_out, sem.at[0]),
        pltpu.make_async_copy(res_ref, res_out, sem.at[1]),
    ]
    for copy in copies:
        copy.start()
    for copy in copies:
        copy.wait()


def on_device(shape, right_side, coupling, face_columns, ghost_lists):
    n_fx, n_fy, low, faces = shape
    plane = low * n_fy
    high = n_fx // low
    right_rows = right_side.reshape(faces // 8, 8, DOF // GROUPS, LANES).transpose(0, 2, 1, 3)
    coupling = coupling.reshape(faces // 8, 8, BLOCKS, HALF, LANES).transpose(2, 0, 3, 1, 4)
    rows = faces * DOF
    early = 2 * NRHS // plane
    vmem = pl.BlockSpec(memory_space=pltpu.VMEM)
    hbm = pl.BlockSpec(memory_space=pltpu.HBM)
    dma = pltpu.SemaphoreType.DMA
    i32 = jnp.int32
    out = jax.ShapeDtypeStruct(right_side.shape, f32)
    gram = [
        pltpu.VMEM((plane, early, LANES), f32),
        pltpu.VMEM((plane - 1, early, LANES), f32),
        pltpu.VMEM((high, early, LANES), f32),
        pltpu.VMEM((plane, early, LANES), f32),
        pltpu.VMEM((plane, NRHS, LANES), f32),
        pltpu.VMEM((high, NRHS, LANES), f32),
    ]
    results = pl.pallas_call(
        functools.partial(kernel, shape),
        out_shape=(out, out),
        in_specs=[hbm] * 4,
        out_specs=(vmem, vmem),
        scratch_shapes=[
            pltpu.VMEM((faces // 8, 8, DOF // GROUPS, LANES), f32),
            pltpu.SMEM(face_columns.shape, i32),
            pltpu.SMEM(ghost_lists.shape, i32),
            pltpu.VMEM((BLOCKS, faces // 8, 8, HALF, LANES), f32),
            pltpu.VMEM((faces, DOF, BLOCKS * LANES), bf16),
        ]
        + [pltpu.VMEM((faces, DOF, LANES), f32)] * (POWERS + 1)
        + [
            pltpu.VMEM((faces + 4 * GROUPS, LANES, LANES), bf16),
            pltpu.VMEM((faces, HALF, LANES), f32),
            pltpu.VMEM((POWERS, 4, DOF, LANES), f32),
            pltpu.VMEM((POWERS, 4, DOF, LANES), f32),
            pltpu.VMEM((rows, 2 * LANES), bf16),
            pltpu.VMEM((rows, LANES), bf16),
            pltpu.VMEM((GROUPS, rows // GROUPS, 2 * LANES), bf16),
        ]
        + gram
        + [
            dma((3,)),
            dma((-(-BLOCKS // BATCH),)),
            dma((4,)),
            dma((2, 4)),
            dma((2, 6)),
            pltpu.SemaphoreType.REGULAR((TOKENS,)),
        ],
        compiler_params=pltpu.CompilerParams(
            collective_id=0, has_side_effects=True, vmem_limit_bytes=40 * 2**20
        ),
    )(*[pltpu.with_memory_space_constraint(x, pltpu.HBM) for x in (right_rows, coupling, face_columns, ghost_lists)])
    return pl.pallas_call(
        put_out,
        out_shape=(out, out),
        in_specs=[vmem, vmem],
        out_specs=(hbm, hbm),
        scratch_shapes=[dma((2,))],
        compiler_params=pltpu.CompilerParams(vmem_limit_bytes=2**20),
    )(*results)


def solution(mesh):
    n_fx, n_fy = mesh.shape["fx"], mesh.shape["fy"]
    low = 1
    while low * low * 4 <= n_fx:
        low *= 2

    def body(right_side, coupling, face_columns, ghost_lists):
        shape = (n_fx, n_fy, low, right_side.shape[0])
        return on_device(shape, right_side, coupling, face_columns, ghost_lists)

    placed = (
        P(("fx", "fy"), None),
        P(("fx", "fy"), None, None),
        P(("fx", "fy"), None),
        P(("fx", "fy"), None),
    )
    return jax.shard_map(
        body,
        mesh=mesh,
        in_specs=placed,
        out_specs=(P(("fx", "fy"), None), P(("fx", "fy"), None)),
        check_vma=False,
    )
```

```python
import contextlib
import functools

import jax
import jax.numpy as jnp
from jax import lax
from jax.experimental import pallas as pl
from jax.experimental.pallas import tpu as pltpu
from jax.sharding import PartitionSpec as P

DOF = 64
NRHS = 32
BLOCKS = 11
OWNED = 7
POWERS = 3
LANES = 128
HALF = DOF // 2
BATCH = 11
PIECES = 1
TOKENS = 2 * (POWERS - 1)
GROUPS = LANES // NRHS
MESH = pl.DeviceIdType.MESH
f32 = jnp.float32
bf16 = jnp.bfloat16


def split(x):
    hi = x.astype(bf16).astype(f32)
    return hi, x - hi


def lane_group(rows):
    return lax.broadcasted_iota(jnp.int32, (rows, LANES), 1) // NRHS


def pick(group, parts):
    out = parts[-1]
    for index in range(len(parts) - 2, -1, -1):
        out = jnp.where(group == index, parts[index], out)
    return out


def replicate(group, rolled, source):
    return pick(group, [rolled[(lane - source) % GROUPS] for lane in range(GROUPS)])


def rolls(x):
    return [x] + [pltpu.roll(x, step * NRHS, 1) for step in range(1, GROUPS)]


def product_tile(x, group):
    hi, lo = split(x)
    return halves(jnp.where(group < GROUPS // 2, hi, lo), group)


def halves(x, group):
    zero = jnp.zeros_like(x)
    even = group % 2 == 0
    return jnp.where(even, x, zero).astype(bf16), jnp.where(even, zero, x).astype(bf16)


def scope(name):
    return contextlib.nullcontext()


def across_gather(x, lane):
    return jnp.take_along_axis(x, jnp.full((8, LANES), lane, jnp.int32), axis=1)


def across_sum(x, lane):
    lanes = lax.broadcasted_iota(jnp.int32, (8, LANES), 1)
    return jnp.broadcast_to(jnp.sum(jnp.where(lanes == lane, x, 0.0), axis=1, keepdims=True), (8, LANES))


def eliminate(tiles, inverse, across):
    tiles = list(tiles)
    sub = lax.broadcasted_iota(jnp.int32, (8, LANES), 0)
    lanes = lax.broadcasted_iota(jnp.int32, (8, LANES), 1)

    def down(x, row):
        return jnp.broadcast_to(x[row:row + 1, :], (8, LANES))

    for home in range(len(tiles)):
        mine = tiles[home]
        cols = [across(mine, 8 * home + c) for c in range(8)]
        for step in range(8):
            pivot = 1.0 / down(cols[step], step)
            here = sub == step
            factor = cols[step]
            if inverse:
                mine = jnp.where(lanes == 8 * home + step, jnp.where(here, 1.0, 0.0), mine)
            scaled = down(mine, step) * pivot
            mine = jnp.where(here, scaled, mine - factor * scaled)
            for c in range(step + 1, 8):
                scaled = down(cols[c], step) * pivot
                cols[c] = jnp.where(here, scaled, cols[c] - factor * scaled)
        tiles[home] = mine
        rows8 = [down(mine, c) for c in range(8)]
        for t in [t % len(tiles) for t in range(home + 1, home + len(tiles))]:
            terms = [across(tiles[t], 8 * home + c) * rows8[c] for c in range(8)]
            while len(terms) > 1:
                terms = [terms[k] + terms[k + 1] for k in range(0, len(terms), 2)]
            base = jnp.where(lanes // 8 == home, 0.0, tiles[t]) if inverse else tiles[t]
            tiles[t] = base - terms[0]
    return jnp.concatenate(tiles, axis=0)


def split3(x):
    hi, rest = split(x)
    mid, low = split(rest)
    return [part.astype(bf16) for part in (hi, mid, low)]


def high_dot(left, right, dims):
    rows = left.shape[0]
    along = 1 - dims[1][0]
    left = jnp.concatenate(split3(left), axis=0)
    right = jnp.concatenate(split3(right), axis=along)
    out = lax.dot_general(left, right, (dims, ((), ())), preferred_element_type=f32)
    width = out.shape[1] // 3

    def block(i, j):
        return out[i * rows:(i + 1) * rows, j * width:(j + 1) * width]

    small = (block(1, 1) + block(0, 2)) + block(2, 0)
    return block(0, 0) + ((block(0, 1) + block(1, 0)) + small)


def kernel(shape, right_hbm, coupling_hbm, columns_hbm, ghost_hbm, sol_ref, res_ref,
           right_ref, columns_ref, ghost_ref,
           stage, mats, w0, w1, w2, w3, ordered, tiles, acc, send_buf, recv_buf,
           zbuf, newest, vbuf, early_buf, early_plane, early_line, early_all,
           late_plane, late_line,
           small_sem, load_sem, send_sem, recv_sem, gram_sem, token_sem):
    n_fx, n_fy, low, faces = shape
    plane = low * n_fy
    high = n_fx // low
    i = lax.axis_index("fx")
    j = lax.axis_index("fy")
    my_low = i % low
    my_high = i // low
    my_rank = my_low * n_fy + j
    fields = [w0, w1, w2, w3]

    def plane_target(offset):
        rank = lax.rem(my_rank + offset, plane)
        return rank, (my_high * low + rank // n_fy, rank % n_fy)

    def line_target(offset):
        place = lax.rem(my_high + offset, high)
        return (place * low + my_low, j)

    routes = [
        (1, i < n_fx - 1, (i + 1, j), i > 0),
        (0, i > 0, (i - 1, j), i < n_fx - 1),
        (3, j < n_fy - 1, (i, j + 1), j > 0),
        (2, j > 0, (i, j - 1), j < n_fy - 1),
    ]

    small = [
        pltpu.make_async_copy(src, dst, small_sem.at[place])
        for place, (src, dst) in enumerate([
            (ghost_hbm, ghost_ref), (columns_hbm, columns_ref),
        ])
    ]
    rights = [
        pltpu.make_async_copy(right_hbm.at[:, :, s], right_ref.at[:, s], small_sem.at[2]) for s in range(8)
    ]
    for load in rights + small:
        load.start()
    batches = [(k, min(k + BATCH, BLOCKS)) for k in range(0, BLOCKS, BATCH)]
    loads = [
        [
            pltpu.make_async_copy(coupling_hbm.at[k, :, :, s], stage.at[k, :, s], load_sem.at[place])
            for k in range(first, last) for s in range(8)
        ]
        for place, (first, last) in enumerate(batches)
    ]
    barrier = pltpu.get_barrier_semaphore()
    for _, has_target, target, _ in routes:
        @pl.when(has_target)
        def _(target=target):
            pl.semaphore_signal(barrier, inc=1, device_id=target, device_id_type=MESH)
    reach = TOKENS + 1
    neighbours = sum(jnp.where(route[1], 1, 0) for route in routes)
    strangers = []
    if low + n_fy - 2 > reach:
        for offset in range(1, plane):
            target = plane_target(offset)[1]
            strangers.append((jnp.abs(target[0] - i) + jnp.abs(target[1] - j) > reach, target))
    if (high - 1) * low > reach + 1:
        for offset in range(1, high):
            target = line_target(offset)
            strangers.append((jnp.abs(target[0] - i) > reach + 1, target))
    for strange, target in strangers:
        @pl.when(strange)
        def _(target=target):
            pl.semaphore_signal(barrier, inc=1, device_id=target, device_id_type=MESH)

    def pass_token(place):
        for _, has_target, target, _ in routes:
            @pl.when(has_target)
            def _(target=target):
                pl.semaphore_signal(token_sem.at[place % 2], inc=1, device_id=target, device_id_type=MESH)

    def take_token(place):
        pl.semaphore_wait(token_sem.at[place % 2], neighbours)

    for batch in loads:
        for load in batch:
            load.start()

    g8 = lane_group(8)
    g64 = lane_group(DOF)
    g32 = lane_group(HALF)

    with scope("relay"):
        pltpu.make_async_copy(right_ref, right_ref, small_sem.at[2]).wait()
        sub = lax.broadcasted_iota(jnp.int32, (8, LANES), 0)
        turn = (g8 - sub) % GROUPS
        for face in range(faces):
            for tile in range(0, DOF // GROUPS, 2):
                x = right_ref[face // 8, face % 8, tile:tile + 2, :]
                x = jnp.where(sub < GROUPS, jnp.broadcast_to(x[0:1], (8, LANES)), jnp.broadcast_to(x[1:2], (8, LANES)))
                w0[face, tile * GROUPS:tile * GROUPS + 8, :] = pick(turn, rolls(x))
        small[0].wait()

    def field_copies(power):
        return [
            pltpu.make_async_remote_copy(
                src_ref=send_buf.at[power, q], dst_ref=recv_buf.at[power, q],
                send_sem=send_sem.at[q], recv_sem=recv_sem.at[power % 2, q],
                device_id=routes[q][2], device_id_type=MESH,
            )
            for q in range(4)
        ]

    def send_field(power):
        field = fields[power]
        copies = field_copies(power)
        for q, (row, _, _, _) in enumerate(routes):
            picked = [field[ghost_ref[row, g]] for g in range(GROUPS)]
            send_buf[power, q] = pick(g64, picked)
        if power == 0:
            pl.semaphore_wait(barrier, neighbours + sum(jnp.where(strange, 1, 0) for strange, _ in strangers))
            pass_token(0)
        for copy, route in zip(copies, routes):
            @pl.when(route[1])
            def _(copy=copy):
                copy.start()
        return copies

    def build_own(power):
        field = fields[power]

        @pl.loop(0, faces, unroll=4)
        def _(face):
            x = field[face]
            top, bottom = product_tile(x, g64)
            tiles[face, 0:DOF] = top
            tiles[face, DOF:2 * DOF] = bottom

    def own_products():
        for face in range(faces):
            left = mats[face, :, :OWNED * LANES]
            right = jnp.concatenate([tiles[columns_ref[face, k]] for k in range(OWNED)], axis=0)
            out = jnp.dot(left, right, preferred_element_type=f32)
            acc[face] = out[:HALF] + out[HALF:]

    def far_products(power, part):
        field = fields[power + 1]
        for face in part:
            left = mats[face, :, OWNED * LANES:]
            right = jnp.concatenate([tiles[columns_ref[face, k]] for k in range(OWNED, BLOCKS)], axis=0)
            out = jnp.dot(left, right, preferred_element_type=f32)
            total = acc[face] + (out[:HALF] + out[HALF:])
            total = total + pltpu.roll(total, LANES // 2, 1)
            turned = pltpu.roll(total, NRHS, 1)
            even = g32 % 2 == 0
            first, second = jnp.where(even, total, turned), jnp.where(even, turned, total)
            field[face, pl.ds(0, HALF, stride=2), :] = first
            field[face, pl.ds(1, HALF, stride=2), :] = second
            both = jnp.concatenate([first, second], axis=0)
            if power < POWERS - 1:
                ordered[power + 1, face] = both
            else:
                late_rows(face, both)

    def first_rows():
        for face in range(faces):
            rows = slice(face * DOF, (face + 1) * DOF)
            a = jnp.concatenate([w0[face, pl.ds(parity, HALF, stride=2), :] for parity in range(2)], axis=0)
            hi, lo = split(pick(g64, [a + ordered[1, face], jnp.zeros_like(a), jnp.zeros_like(a), a]))
            zbuf[rows, :LANES] = hi.astype(bf16)
            zbuf[rows, LANES:] = lo.astype(bf16)
            newest[rows, :] = jnp.where(g64 < 2, hi, pltpu.roll(lo, LANES // 2, 1)).astype(bf16)

    def late_rows(face, newer):
        rows = slice(face * DOF, (face + 1) * DOF)
        hi, lo = split(ordered[POWERS - 1, face] + newer)
        zero = jnp.zeros_like(hi)
        third = g64 == POWERS - 1
        zbuf[rows, :LANES] = zbuf[rows, :LANES] + jnp.where(third, hi, zero).astype(bf16)
        zbuf[rows, LANES:] = zbuf[rows, LANES:] + jnp.where(third, lo, zero).astype(bf16)
        newest[rows, :] = jnp.where(g64 == 0, hi, lo).astype(bf16)

    def receive_field(power, copies):
        for q in (2, 3, 0, 1):
            _, has_target, _, has_source = routes[q]

            with scope("recv%d_%d" % (power, q)):
                @pl.when(has_source)
                def _(copy=copies[q]):
                    copy.wait_recv()

                @pl.when(jnp.logical_not(has_source))
                def _(q=q):
                    recv_buf[power, q] = jnp.zeros((DOF, LANES), f32)
            with scope("conv%d_%d" % (power, q)):
                hi, lo = split(recv_buf[power, q])
                hi, lo = rolls(hi), rolls(lo)
                for g in range(GROUPS):
                    top, bottom = halves(pick(g64, [
                        (hi if lane < GROUPS // 2 else lo)[(lane - g) % GROUPS] for lane in range(GROUPS)
                    ]), g64)
                    tiles[faces + q * GROUPS + g, 0:DOF] = top
                    tiles[faces + q * GROUPS + g, DOF:2 * DOF] = bottom

            @pl.when(has_target)
            def _(copy=copies[q]):
                copy.wait_send()

    def prepare():
        for place, (first, last) in enumerate(batches):
            whole = stage.at[first:last]
            pltpu.make_async_copy(whole, whole, load_sem.at[place]).wait()
            for k in range(first, last):
                for face in range(faces):
                    hi, lo = split(stage[k, face // 8, face % 8])
                    mats[face, 0:HALF, k * LANES:(k + 1) * LANES] = hi.astype(bf16)
                    mats[face, HALF:DOF, k * LANES:(k + 1) * LANES] = lo.astype(bf16)

    def wait_for(buf, count, sem):
        whole = buf.at[0:count]
        pltpu.make_async_copy(whole, whole, sem).wait()

    def scatter(which, buf, landed):
        for offset in range(1, plane):
            rank, target = plane_target(offset)
            pltpu.make_async_remote_copy(
                src_ref=buf.at[rank], dst_ref=landed.at[offset - 1], send_sem=gram_sem.at[which, 0],
                recv_sem=gram_sem.at[which, 1], device_id=target, device_id_type=MESH).start()

    def scatter_sum(which, buf, landed):
        total = buf[my_rank]
        wait_for(landed, plane - 1, gram_sem.at[which, 1])
        for offset in range(1, plane):
            total = total + landed[offset - 1]
        return total

    def exchange(which, line, total):
        line[my_high] = total
        for offset in range(1, high):
            pltpu.make_async_remote_copy(
                src_ref=line.at[my_high], dst_ref=line.at[my_high], send_sem=gram_sem.at[which, 2],
                recv_sem=gram_sem.at[which, 3], device_id=line_target(offset), device_id_type=MESH).start()

    def add_all(buf, count):
        terms = [buf[place] for place in range(count)]
        while len(terms) > 1:
            terms = [sum(terms[k:k + 2][1:], terms[k]) for k in range(0, len(terms), 2)]
        return terms[0]

    def exchange_sum(which, line):
        wait_for(line, high - 1, gram_sem.at[which, 3])
        return add_all(line, high)

    def gather(which, final, first):
        for offset in range(1, plane):
            pltpu.make_async_remote_copy(
                src_ref=final.at[my_rank], dst_ref=final.at[my_rank], send_sem=gram_sem.at[which, first],
                recv_sem=gram_sem.at[which, first + 1], device_id=plane_target(offset)[1], device_id_type=MESH).start()

    def gathered(which, final):
        wait_for(final, plane - 1, gram_sem.at[which, 5])
        return jnp.concatenate([final[rank] for rank in range(plane)], axis=0)

    def early_gram():
        @pl.loop(0, faces, unroll=4)
        def _(face):
            rows = pl.ds(pl.multiple_of(face * DOF, DOF), DOF)
            hi, lo = split(ordered[1, face] + ordered[2, face])
            hi, lo = hi.astype(bf16), lo.astype(bf16)
            second = g64 == 1
            zbuf[rows, :LANES] = jnp.where(second, hi, zbuf[rows, :LANES])
            zbuf[rows, LANES:] = jnp.where(second, lo, zbuf[rows, LANES:])
            newest[rows, :] = jnp.where(second, hi, jnp.where(g64 == 3, lo, newest[rows, :]))

        both = lax.dot_general(newest[...], zbuf[...], (((0,), (0,)), ((), ())), preferred_element_type=f32)
        half = 2 * NRHS
        gram = (both[:half, :LANES] + both[half:, LANES:]) + (both[:half, LANES:] + both[half:, :LANES])
        share = early_buf.shape[1]
        for rank in range(plane):
            early_buf[rank] = gram[rank * share:(rank + 1) * share]

    def late_gram():
        both = lax.dot_general(newest[:, :2 * NRHS], zbuf[...], (((0,), (0,)), ((), ())), preferred_element_type=f32)
        gram = (both[:NRHS, :LANES] + both[NRHS:2 * NRHS, LANES:]) + (both[:NRHS, LANES:] + both[NRHS:2 * NRHS, :LANES])
        late_plane[my_rank] = gram

    flat = [field.reshape(faces * DOF, LANES) for field in fields]

    def order_rows():
        for block in range(faces // 8):
            for pair in range(DOF // GROUPS // 2):
                for q in range(GROUPS):
                    halves = []
                    for tile in (2 * pair, 2 * pair + 1):
                        at = pl.ds(8 * block * DOF + tile * GROUPS + q, 8, stride=DOF)
                        halves.append(pick(g8, [view[at, :] for view in flat]))
                    hi, lo = split(jnp.concatenate(halves, axis=0))
                    row = 8 * (block * (DOF // GROUPS) + 2 * pair)
                    vbuf[q, row:row + 16, :LANES] = hi.astype(bf16)
                    vbuf[q, row:row + 16, LANES:] = lo.astype(bf16)

    for power in range(POWERS):
        with scope("send%d" % power):
            copies = send_field(power)
        if power == POWERS - 1:
            with scope("egram"):
                early_gram()
                scatter(0, early_buf, early_plane)
        with scope("build%d" % power):
            build_own(power)
        if power == 0:
            with scope("prepare"):
                prepare()
                small[1].wait()
        with scope("own%d" % power):
            own_products()
        if power == 1:
            first_rows()
        if power < TOKENS // 2:
            take_token(2 * power)
            pass_token(2 * power + 1)
        receive_field(power, copies)
        with scope("far%d" % power):
            far_products(power, range(faces // 2))
            if power == POWERS - 1:
                with scope("eplane"):
                    exchange(0, early_line, scatter_sum(0, early_buf, early_plane))
            far_products(power, range(faces // 2, faces))
        if power < TOKENS // 2:
            take_token(2 * power + 1)
            if 2 * power + 2 < TOKENS:
                pass_token(2 * power + 2)

    with scope("lgram"):
        late_gram()
        gather(1, late_plane, 0)
    with scope("order"):
        order_rows()
    with scope("eline"):
        early_all[my_rank] = exchange_sum(0, early_line)
        gather(0, early_all, 4)
    with scope("lplane"):
        wait_for(late_plane, plane - 1, gram_sem.at[1, 1])
        exchange(1, late_line, add_all(late_plane, plane))
    with scope("eall"):
        system = gathered(0, early_all)
    with scope("esolve"):
        count = 2 * NRHS
        solved = eliminate([system[t:t + 8] for t in range(0, count, 8)], True, across_gather)
        spread_early = replicate(lane_group(count), rolls(solved), GROUPS - 1)
    with scope("lall"):
        last = exchange_sum(1, late_line)
    with scope("lsolve"):
        left_half = lax.broadcasted_iota(jnp.int32, (NRHS, LANES), 1) < count
        cross = jnp.where(left_half, last, 0.0)
        pad = jnp.zeros((LANES - count, LANES), f32)
        done = high_dot(cross, jnp.concatenate([solved, pad], axis=0), ((1,), (0,)))
        inner = jnp.where(left_half, done, 0.0)
        outer = high_dot(jnp.where(lax.broadcasted_iota(jnp.int32, (count, LANES), 1) < count, solved, 0.0), jnp.concatenate([cross, jnp.zeros((LANES - NRHS, LANES), f32)], axis=0), ((1,), (1,)))
        schur = high_dot(inner, jnp.concatenate([cross, jnp.zeros((LANES - NRHS, LANES), f32)], axis=0), ((1,), (1,)))
        small_system = pltpu.roll(jnp.where(left_half, 0.0, last - done), LANES // 2, 1) - schur
        newest_part = eliminate([small_system[t:t + 8] for t in range(0, NRHS, 8)], False, across_sum)
        newest_part = replicate(g32, rolls(newest_part), 1)
        older = spread_early - high_dot(outer[:, :NRHS], newest_part, ((1,), (0,)))
        coeffs = jnp.concatenate([older, newest_part], axis=0)
    with scope("coeffs"):
        none = jnp.zeros((NRHS, LANES), f32)
        row = lax.broadcasted_iota(jnp.int32, (LANES, LANES), 0)
        col = lax.broadcasted_iota(jnp.int32, (LANES, LANES), 1) % NRHS
        first = jnp.where(row == col, 1.0, 0.0)
        padded = jnp.concatenate([coeffs, none], axis=0)
        combo = first - (padded + jnp.concatenate([none, coeffs], axis=0))
        hi, lo = split(jnp.concatenate([padded, combo], axis=1))
        group = lax.broadcasted_iota(jnp.int32, (LANES, 2 * LANES), 1) % LANES // NRHS
        his = [jnp.where(group == q, hi, 0.0).astype(bf16) for q in range(GROUPS)]
        los = [jnp.where(group == q, lo, 0.0).astype(bf16) for q in range(GROUPS)]
        right = jnp.concatenate(his + his + los, axis=0)
    with scope("outdot"):
        vhi = [vbuf[q, :, :LANES] for q in range(GROUPS)]
        vlo = [vbuf[q, :, LANES:] for q in range(GROUPS)]
        out = jnp.dot(jnp.concatenate(vhi + vlo + vhi, axis=1), right, preferred_element_type=f32)
        for part, out_ref in enumerate((sol_ref, res_ref)):
            for block in range(faces // 8):
                for tile in range(DOF // GROUPS):
                    row = 8 * (block * (DOF // GROUPS) + tile)
                    out_ref[8 * block:8 * block + 8, tile * LANES:(tile + 1) * LANES] = out[
                        row:row + 8, part * LANES:(part + 1) * LANES]
    with scope("drain"):
        for which, bufs in enumerate([(early_plane, early_line, early_all), (late_plane, late_line)]):
            for phase, (buf, amount) in enumerate(zip(bufs, (plane - 1, high - 1, plane - 1))):
                wait_for(buf, amount, gram_sem.at[which, 2 * phase])


def put_out(sol_ref, res_ref, sol_out, res_out, sem):
    width = sol_ref.shape[1] // PIECES
    copies = [
        pltpu.make_async_copy(src.at[:, pl.ds(piece * width, width)], dst.at[:, pl.ds(piece * width, width)], sem.at[part, piece])
        for part, (src, dst) in enumerate([(sol_ref, sol_out), (res_ref, res_out)]) for piece in range(PIECES)
    ]
    for copy in copies:
        copy.start()
    for copy in copies:
        copy.wait()


def on_device(shape, right_side, coupling, face_columns, ghost_lists):
    n_fx, n_fy, low, faces = shape
    plane = low * n_fy
    high = n_fx // low
    right_rows = right_side.reshape(faces // 8, 8, DOF // GROUPS, LANES).transpose(0, 2, 1, 3)
    coupling = coupling.reshape(faces // 8, 8, BLOCKS, HALF, LANES).transpose(2, 0, 3, 1, 4)
    rows = faces * DOF
    early = 2 * NRHS // plane
    vmem = pl.BlockSpec(memory_space=pltpu.VMEM)
    hbm = pl.BlockSpec(memory_space=pltpu.HBM)
    dma = pltpu.SemaphoreType.DMA
    i32 = jnp.int32
    out = jax.ShapeDtypeStruct(right_side.shape, f32)
    gram = [
        pltpu.VMEM((plane, early, LANES), f32),
        pltpu.VMEM((plane - 1, early, LANES), f32),
        pltpu.VMEM((high, early, LANES), f32),
        pltpu.VMEM((plane, early, LANES), f32),
        pltpu.VMEM((plane, NRHS, LANES), f32),
        pltpu.VMEM((high, NRHS, LANES), f32),
    ]
    results = pl.pallas_call(
        functools.partial(kernel, shape),
        out_shape=(out, out),
        in_specs=[hbm] * 4,
        out_specs=(vmem, vmem),
        scratch_shapes=[
            pltpu.VMEM((faces // 8, 8, DOF // GROUPS, LANES), f32),
            pltpu.SMEM(face_columns.shape, i32),
            pltpu.SMEM(ghost_lists.shape, i32),
            pltpu.VMEM((BLOCKS, faces // 8, 8, HALF, LANES), f32),
            pltpu.VMEM((faces, DOF, BLOCKS * LANES), bf16),
        ]
        + [pltpu.VMEM((faces, DOF, LANES), f32)] * (POWERS + 1)
        + [
            pltpu.VMEM((POWERS, faces, DOF, LANES), f32),
            pltpu.VMEM((faces + 4 * GROUPS, LANES, LANES), bf16),
            pltpu.VMEM((faces, HALF, LANES), f32),
            pltpu.VMEM((POWERS, 4, DOF, LANES), f32),
            pltpu.VMEM((POWERS, 4, DOF, LANES), f32),
            pltpu.VMEM((rows, 2 * LANES), bf16),
            pltpu.VMEM((rows, LANES), bf16),
            pltpu.VMEM((GROUPS, rows // GROUPS, 2 * LANES), bf16),
        ]
        + gram
        + [
            dma((3,)),
            dma((-(-BLOCKS // BATCH),)),
            dma((4,)),
            dma((2, 4)),
            dma((2, 6)),
            pltpu.SemaphoreType.REGULAR((2,)),
        ],
        compiler_params=pltpu.CompilerParams(
            collective_id=0, has_side_effects=True, vmem_limit_bytes=40 * 2**20
        ),
    )(*[pltpu.with_memory_space_constraint(x, pltpu.HBM) for x in (right_rows, coupling, face_columns, ghost_lists)])
    return pl.pallas_call(
        put_out,
        out_shape=(out, out),
        in_specs=[vmem, vmem],
        out_specs=(hbm, hbm),
        scratch_shapes=[dma((2, PIECES))],
        compiler_params=pltpu.CompilerParams(vmem_limit_bytes=2**20),
    )(*results)


def solution(mesh):
    n_fx, n_fy = mesh.shape["fx"], mesh.shape["fy"]
    low = 1
    while low * low * 4 <= n_fx:
        low *= 2

    def body(right_side, coupling, face_columns, ghost_lists):
        shape = (n_fx, n_fy, low, right_side.shape[0])
        return on_device(shape, right_side, coupling, face_columns, ghost_lists)

    placed = (
        P(("fx", "fy"), None),
        P(("fx", "fy"), None, None),
        P(("fx", "fy"), None),
        P(("fx", "fy"), None),
    )
    return jax.shard_map(
        body,
        mesh=mesh,
        in_specs=placed,
        out_specs=(P(("fx", "fy"), None), P(("fx", "fy"), None)),
        check_vma=False,
    )
```

```python
import contextlib
import functools

import jax
import jax.numpy as jnp
from jax import lax
from jax.experimental import pallas as pl
from jax.experimental.pallas import tpu as pltpu
from jax.sharding import PartitionSpec as P

DOF = 64
NRHS = 32
BLOCKS = 11
OWNED = 7
POWERS = 3
LANES = 128
HALF = DOF // 2
BATCH = 11
PIECES = 1
TOKENS = 2 * (POWERS - 1)
GROUPS = LANES // NRHS
MESH = pl.DeviceIdType.MESH
f32 = jnp.float32
bf16 = jnp.bfloat16


def split(x):
    hi = x.astype(bf16).astype(f32)
    return hi, x - hi


def lane_group(rows):
    return lax.broadcasted_iota(jnp.int32, (rows, LANES), 1) // NRHS


def pick(group, parts):
    out = parts[-1]
    for index in range(len(parts) - 2, -1, -1):
        out = jnp.where(group == index, parts[index], out)
    return out


def replicate(group, rolled, source):
    return pick(group, [rolled[(lane - source) % GROUPS] for lane in range(GROUPS)])


def rolls(x):
    return [x] + [pltpu.roll(x, step * NRHS, 1) for step in range(1, GROUPS)]


def product_tile(x, group):
    hi, lo = split(x)
    return halves(jnp.where(group < GROUPS // 2, hi, lo), group)


def halves(x, group):
    zero = jnp.zeros_like(x)
    even = group % 2 == 0
    return jnp.where(even, x, zero).astype(bf16), jnp.where(even, zero, x).astype(bf16)


def scope(name):
    return contextlib.nullcontext()


def across_gather(x, lane):
    return jnp.take_along_axis(x, jnp.full((8, LANES), lane, jnp.int32), axis=1)


def across_sum(x, lane):
    lanes = lax.broadcasted_iota(jnp.int32, (8, LANES), 1)
    return jnp.broadcast_to(jnp.sum(jnp.where(lanes == lane, x, 0.0), axis=1, keepdims=True), (8, LANES))


def eliminate(tiles, inverse, across):
    tiles = list(tiles)
    sub = lax.broadcasted_iota(jnp.int32, (8, LANES), 0)
    lanes = lax.broadcasted_iota(jnp.int32, (8, LANES), 1)

    def down(x, row):
        return jnp.broadcast_to(x[row:row + 1, :], (8, LANES))

    for home in range(len(tiles)):
        mine = tiles[home]
        cols = [across(mine, 8 * home + c) for c in range(8)]
        for step in range(8):
            pivot = 1.0 / down(cols[step], step)
            here = sub == step
            factor = cols[step]
            if inverse:
                mine = jnp.where(lanes == 8 * home + step, jnp.where(here, 1.0, 0.0), mine)
            scaled = down(mine, step) * pivot
            mine = jnp.where(here, scaled, mine - factor * scaled)
            for c in range(step + 1, 8):
                scaled = down(cols[c], step) * pivot
                cols[c] = jnp.where(here, scaled, cols[c] - factor * scaled)
        tiles[home] = mine
        rows8 = [down(mine, c) for c in range(8)]
        for t in [t % len(tiles) for t in range(home + 1, home + len(tiles))]:
            terms = [across(tiles[t], 8 * home + c) * rows8[c] for c in range(8)]
            while len(terms) > 1:
                terms = [terms[k] + terms[k + 1] for k in range(0, len(terms), 2)]
            base = jnp.where(lanes // 8 == home, 0.0, tiles[t]) if inverse else tiles[t]
            tiles[t] = base - terms[0]
    return jnp.concatenate(tiles, axis=0)


def split3(x):
    hi, rest = split(x)
    mid, low = split(rest)
    return [part.astype(bf16) for part in (hi, mid, low)]


def high_dot(left, right, dims):
    rows = left.shape[0]
    along = 1 - dims[1][0]
    left = jnp.concatenate(split3(left), axis=0)
    right = jnp.concatenate(split3(right), axis=along)
    out = lax.dot_general(left, right, (dims, ((), ())), preferred_element_type=f32)
    width = out.shape[1] // 3

    def block(i, j):
        return out[i * rows:(i + 1) * rows, j * width:(j + 1) * width]

    small = (block(1, 1) + block(0, 2)) + block(2, 0)
    return block(0, 0) + ((block(0, 1) + block(1, 0)) + small)


def kernel(shape, right_hbm, coupling_hbm, columns_hbm, ghost_hbm, sol_ref, res_ref,
           right_ref, columns_ref, ghost_ref,
           stage, mats, w0, w1, w2, w3, ordered, tiles, acc, send_buf, recv_buf,
           zbuf, newest, vbuf, early_buf, early_plane, early_line, early_all,
           late_plane, late_line,
           small_sem, load_sem, send_sem, recv_sem, gram_sem, token_sem):
    n_fx, n_fy, low, faces = shape
    plane = low * n_fy
    high = n_fx // low
    i = lax.axis_index("fx")
    j = lax.axis_index("fy")
    my_low = i % low
    my_high = i // low
    my_rank = my_low * n_fy + j
    fields = [w0, w1, w2, w3]

    def plane_target(offset):
        rank = lax.rem(my_rank + offset, plane)
        return rank, (my_high * low + rank // n_fy, rank % n_fy)

    def line_target(offset):
        place = lax.rem(my_high + offset, high)
        return (place * low + my_low, j)

    routes = [
        (1, i < n_fx - 1, (i + 1, j), i > 0),
        (0, i > 0, (i - 1, j), i < n_fx - 1),
        (3, j < n_fy - 1, (i, j + 1), j > 0),
        (2, j > 0, (i, j - 1), j < n_fy - 1),
    ]

    small = [
        pltpu.make_async_copy(src, dst, small_sem.at[place])
        for place, (src, dst) in enumerate([
            (ghost_hbm, ghost_ref), (columns_hbm, columns_ref),
        ])
    ]
    rights = [
        pltpu.make_async_copy(right_hbm.at[:, :, s], right_ref.at[:, s], small_sem.at[2]) for s in range(8)
    ]
    for load in rights + small:
        load.start()
    batches = [(k, min(k + BATCH, BLOCKS)) for k in range(0, BLOCKS, BATCH)]
    loads = [
        [
            pltpu.make_async_copy(coupling_hbm.at[k, :, :, s], stage.at[k, :, s], load_sem.at[place])
            for k in range(first, last) for s in range(8)
        ]
        for place, (first, last) in enumerate(batches)
    ]
    barrier = pltpu.get_barrier_semaphore()
    for _, has_target, target, _ in routes:
        @pl.when(has_target)
        def _(target=target):
            pl.semaphore_signal(barrier, inc=1, device_id=target, device_id_type=MESH)
    reach = TOKENS + 1
    neighbours = sum(jnp.where(route[1], 1, 0) for route in routes)
    strangers = []
    if low + n_fy - 2 > reach:
        for offset in range(1, plane):
            target = plane_target(offset)[1]
            strangers.append((jnp.abs(target[0] - i) + jnp.abs(target[1] - j) > reach, target))
    if (high - 1) * low > reach + 1:
        for offset in range(1, high):
            target = line_target(offset)
            strangers.append((jnp.abs(target[0] - i) > reach + 1, target))
    for strange, target in strangers:
        @pl.when(strange)
        def _(target=target):
            pl.semaphore_signal(barrier, inc=1, device_id=target, device_id_type=MESH)

    def pass_token(place):
        for _, has_target, target, _ in routes:
            @pl.when(has_target)
            def _(target=target):
                pl.semaphore_signal(token_sem.at[place % 2], inc=1, device_id=target, device_id_type=MESH)

    def take_token(place):
        pl.semaphore_wait(token_sem.at[place % 2], neighbours)

    for batch in loads:
        for load in batch:
            load.start()

    g8 = lane_group(8)
    g64 = lane_group(DOF)
    g32 = lane_group(HALF)

    with scope("relay"):
        pltpu.make_async_copy(right_ref, right_ref, small_sem.at[2]).wait()
        sub = lax.broadcasted_iota(jnp.int32, (8, LANES), 0)
        turn = (g8 - sub) % GROUPS
        for face in range(faces):
            for tile in range(0, DOF // GROUPS, 2):
                x = right_ref[face // 8, face % 8, tile:tile + 2, :]
                x = jnp.where(sub < GROUPS, jnp.broadcast_to(x[0:1], (8, LANES)), jnp.broadcast_to(x[1:2], (8, LANES)))
                w0[face, tile * GROUPS:tile * GROUPS + 8, :] = pick(turn, rolls(x))
        small[0].wait()

    def field_copies(power):
        return [
            pltpu.make_async_remote_copy(
                src_ref=send_buf.at[power, q], dst_ref=recv_buf.at[power, q],
                send_sem=send_sem.at[q], recv_sem=recv_sem.at[power % 2, q],
                device_id=routes[q][2], device_id_type=MESH,
            )
            for q in range(4)
        ]

    def start_copies(copies, directions):
        for q in directions:
            @pl.when(routes[q][1])
            def _(copy=copies[q]):
                copy.start()

    def send_field(power, copies, directions):
        field = fields[power]
        for q in directions:
            picked = [field[ghost_ref[routes[q][0], g]] for g in range(GROUPS)]
            send_buf[power, q] = pick(g64, picked)
        if power == 0:
            pl.semaphore_wait(barrier, neighbours + sum(jnp.where(strange, 1, 0) for strange, _ in strangers))
            pass_token(0)
        start_copies(copies, directions)

    def send_products(power, copies, directions):
        listed = {q: [ghost_ref[routes[q][0], g] for g in range(GROUPS)] for q in directions}
        for q in directions:
            pairs = [far_rows(face) for face in listed[q]]
            for parity in range(2):
                send_buf[power, q, pl.ds(parity, HALF, stride=2), :] = pick(g32, [pair[parity] for pair in pairs])
        start_copies(copies, directions)

    def build_own(power):
        field = fields[power]

        @pl.loop(0, faces, unroll=4)
        def _(face):
            x = field[face]
            top, bottom = product_tile(x, g64)
            tiles[face, 0:DOF] = top
            tiles[face, DOF:2 * DOF] = bottom

    def own_products():
        for face in range(faces):
            left = mats[face, :, :OWNED * LANES]
            right = jnp.concatenate([tiles[columns_ref[face, k]] for k in range(OWNED)], axis=0)
            out = jnp.dot(left, right, preferred_element_type=f32)
            acc[face] = out[:HALF] + out[HALF:]

    def far_rows(face):
        left = mats[face, :, OWNED * LANES:]
        right = jnp.concatenate([tiles[columns_ref[face, k]] for k in range(OWNED, BLOCKS)], axis=0)
        out = jnp.dot(left, right, preferred_element_type=f32)
        total = acc[face] + (out[:HALF] + out[HALF:])
        total = total + pltpu.roll(total, LANES // 2, 1)
        turned = pltpu.roll(total, NRHS, 1)
        even = g32 % 2 == 0
        return jnp.where(even, total, turned), jnp.where(even, turned, total)

    def far_products(power, part):
        field = fields[power + 1]
        for face in part:
            first, second = far_rows(face)
            field[face, pl.ds(0, HALF, stride=2), :] = first
            field[face, pl.ds(1, HALF, stride=2), :] = second
            both = jnp.concatenate([first, second], axis=0)
            if power < POWERS - 1:
                ordered[power + 1, face] = both
            else:
                late_rows(face, both)

    def first_rows():
        for face in range(faces):
            rows = slice(face * DOF, (face + 1) * DOF)
            a = jnp.concatenate([w0[face, pl.ds(parity, HALF, stride=2), :] for parity in range(2)], axis=0)
            hi, lo = split(pick(g64, [a + ordered[1, face], jnp.zeros_like(a), jnp.zeros_like(a), a]))
            zbuf[rows, :LANES] = hi.astype(bf16)
            zbuf[rows, LANES:] = lo.astype(bf16)
            newest[rows, :] = jnp.where(g64 < 2, hi, pltpu.roll(lo, LANES // 2, 1)).astype(bf16)

    def late_rows(face, newer):
        rows = slice(face * DOF, (face + 1) * DOF)
        hi, lo = split(ordered[POWERS - 1, face] + newer)
        zero = jnp.zeros_like(hi)
        third = g64 == POWERS - 1
        zbuf[rows, :LANES] = zbuf[rows, :LANES] + jnp.where(third, hi, zero).astype(bf16)
        zbuf[rows, LANES:] = zbuf[rows, LANES:] + jnp.where(third, lo, zero).astype(bf16)
        newest[rows, :] = jnp.where(g64 == 0, hi, lo).astype(bf16)

    def receive_field(power, copies):
        for q in (2, 3, 0, 1):
            _, has_target, _, has_source = routes[q]

            with scope("recv%d_%d" % (power, q)):
                @pl.when(has_source)
                def _(copy=copies[q]):
                    copy.wait_recv()

                @pl.when(jnp.logical_not(has_source))
                def _(q=q):
                    recv_buf[power, q] = jnp.zeros((DOF, LANES), f32)
            with scope("conv%d_%d" % (power, q)):
                hi, lo = split(recv_buf[power, q])
                hi, lo = rolls(hi), rolls(lo)
                for g in range(GROUPS):
                    top, bottom = halves(pick(g64, [
                        (hi if lane < GROUPS // 2 else lo)[(lane - g) % GROUPS] for lane in range(GROUPS)
                    ]), g64)
                    tiles[faces + q * GROUPS + g, 0:DOF] = top
                    tiles[faces + q * GROUPS + g, DOF:2 * DOF] = bottom

            @pl.when(has_target)
            def _(copy=copies[q]):
                copy.wait_send()

    def prepare():
        for place, (first, last) in enumerate(batches):
            whole = stage.at[first:last]
            pltpu.make_async_copy(whole, whole, load_sem.at[place]).wait()
            for k in range(first, last):
                for face in range(faces):
                    hi, lo = split(stage[k, face // 8, face % 8])
                    mats[face, 0:HALF, k * LANES:(k + 1) * LANES] = hi.astype(bf16)
                    mats[face, HALF:DOF, k * LANES:(k + 1) * LANES] = lo.astype(bf16)

    def wait_for(buf, count, sem):
        whole = buf.at[0:count]
        pltpu.make_async_copy(whole, whole, sem).wait()

    def scatter(which, buf, landed):
        for offset in range(1, plane):
            rank, target = plane_target(offset)
            pltpu.make_async_remote_copy(
                src_ref=buf.at[rank], dst_ref=landed.at[offset - 1], send_sem=gram_sem.at[which, 0],
                recv_sem=gram_sem.at[which, 1], device_id=target, device_id_type=MESH).start()

    def scatter_sum(which, buf, landed):
        total = buf[my_rank]
        wait_for(landed, plane - 1, gram_sem.at[which, 1])
        for offset in range(1, plane):
            total = total + landed[offset - 1]
        return total

    def exchange(which, line, total):
        line[my_high] = total
        for offset in range(1, high):
            pltpu.make_async_remote_copy(
                src_ref=line.at[my_high], dst_ref=line.at[my_high], send_sem=gram_sem.at[which, 2],
                recv_sem=gram_sem.at[which, 3], device_id=line_target(offset), device_id_type=MESH).start()

    def add_all(buf, count):
        terms = [buf[place] for place in range(count)]
        while len(terms) > 1:
            terms = [sum(terms[k:k + 2][1:], terms[k]) for k in range(0, len(terms), 2)]
        return terms[0]

    def exchange_sum(which, line):
        wait_for(line, high - 1, gram_sem.at[which, 3])
        return add_all(line, high)

    def gather(which, final, first):
        for offset in range(1, plane):
            pltpu.make_async_remote_copy(
                src_ref=final.at[my_rank], dst_ref=final.at[my_rank], send_sem=gram_sem.at[which, first],
                recv_sem=gram_sem.at[which, first + 1], device_id=plane_target(offset)[1], device_id_type=MESH).start()

    def gathered(which, final):
        wait_for(final, plane - 1, gram_sem.at[which, 5])
        return jnp.concatenate([final[rank] for rank in range(plane)], axis=0)

    def early_gram():
        @pl.loop(0, faces, unroll=4)
        def _(face):
            rows = pl.ds(pl.multiple_of(face * DOF, DOF), DOF)
            hi, lo = split(ordered[1, face] + ordered[2, face])
            hi, lo = hi.astype(bf16), lo.astype(bf16)
            second = g64 == 1
            zbuf[rows, :LANES] = jnp.where(second, hi, zbuf[rows, :LANES])
            zbuf[rows, LANES:] = jnp.where(second, lo, zbuf[rows, LANES:])
            newest[rows, :] = jnp.where(second, hi, jnp.where(g64 == 3, lo, newest[rows, :]))

        both = lax.dot_general(newest[...], zbuf[...], (((0,), (0,)), ((), ())), preferred_element_type=f32)
        half = 2 * NRHS
        gram = (both[:half, :LANES] + both[half:, LANES:]) + (both[:half, LANES:] + both[half:, :LANES])
        share = early_buf.shape[1]
        for rank in range(plane):
            early_buf[rank] = gram[rank * share:(rank + 1) * share]

    def late_gram():
        both = lax.dot_general(newest[:, :2 * NRHS], zbuf[...], (((0,), (0,)), ((), ())), preferred_element_type=f32)
        gram = (both[:NRHS, :LANES] + both[NRHS:2 * NRHS, LANES:]) + (both[:NRHS, LANES:] + both[NRHS:2 * NRHS, :LANES])
        late_plane[my_rank] = gram

    flat = [field.reshape(faces * DOF, LANES) for field in fields]

    def order_rows():
        for block in range(faces // 8):
            for pair in range(DOF // GROUPS // 2):
                for q in range(GROUPS):
                    halves = []
                    for tile in (2 * pair, 2 * pair + 1):
                        at = pl.ds(8 * block * DOF + tile * GROUPS + q, 8, stride=DOF)
                        halves.append(pick(g8, [view[at, :] for view in flat]))
                    hi, lo = split(jnp.concatenate(halves, axis=0))
                    row = 8 * (block * (DOF // GROUPS) + 2 * pair)
                    vbuf[q, row:row + 16, :LANES] = hi.astype(bf16)
                    vbuf[q, row:row + 16, LANES:] = lo.astype(bf16)

    copies = field_copies(0)
    with scope("send0"):
        send_field(0, copies, range(4))
    for power in range(POWERS):
        if power == POWERS - 1:
            with scope("egram"):
                early_gram()
                scatter(0, early_buf, early_plane)
        with scope("build%d" % power):
            build_own(power)
        if power == 0:
            with scope("prepare"):
                prepare()
                small[1].wait()
        with scope("own%d" % power):
            own_products()
        if power == 1:
            first_rows()
        if power < TOKENS // 2:
            take_token(2 * power)
            pass_token(2 * power + 1)
        receive_field(power, copies)
        if power < TOKENS // 2:
            take_token(2 * power + 1)
            if 2 * power + 2 < TOKENS:
                pass_token(2 * power + 2)
        if power < POWERS - 1:
            copies = field_copies(power + 1)
            with scope("send%d" % (power + 1)):
                send_products(power + 1, copies, (0, 1))
            with scope("far%d" % power):
                far_products(power, range(faces))
            with scope("sendy%d" % (power + 1)):
                send_field(power + 1, copies, (2, 3))
        else:
            with scope("far%d" % power):
                far_products(power, range(faces // 2))
                with scope("eplane"):
                    exchange(0, early_line, scatter_sum(0, early_buf, early_plane))
                far_products(power, range(faces // 2, faces))

    with scope("lgram"):
        late_gram()
        gather(1, late_plane, 0)
    with scope("order"):
        order_rows()
    with scope("eline"):
        early_all[my_rank] = exchange_sum(0, early_line)
        gather(0, early_all, 4)
    with scope("lplane"):
        wait_for(late_plane, plane - 1, gram_sem.at[1, 1])
        exchange(1, late_line, add_all(late_plane, plane))
    with scope("eall"):
        system = gathered(0, early_all)
    with scope("esolve"):
        count = 2 * NRHS
        solved = eliminate([system[t:t + 8] for t in range(0, count, 8)], True, across_gather)
        spread_early = replicate(lane_group(count), rolls(solved), GROUPS - 1)
    with scope("lall"):
        last = exchange_sum(1, late_line)
    with scope("lsolve"):
        left_half = lax.broadcasted_iota(jnp.int32, (NRHS, LANES), 1) < count
        cross = jnp.where(left_half, last, 0.0)
        pad = jnp.zeros((LANES - count, LANES), f32)
        done = high_dot(cross, jnp.concatenate([solved, pad], axis=0), ((1,), (0,)))
        inner = jnp.where(left_half, done, 0.0)
        outer = high_dot(jnp.where(lax.broadcasted_iota(jnp.int32, (count, LANES), 1) < count, solved, 0.0), jnp.concatenate([cross, jnp.zeros((LANES - NRHS, LANES), f32)], axis=0), ((1,), (1,)))
        schur = high_dot(inner, jnp.concatenate([cross, jnp.zeros((LANES - NRHS, LANES), f32)], axis=0), ((1,), (1,)))
        small_system = pltpu.roll(jnp.where(left_half, 0.0, last - done), LANES // 2, 1) - schur
        newest_part = eliminate([small_system[t:t + 8] for t in range(0, NRHS, 8)], False, across_sum)
        newest_part = replicate(g32, rolls(newest_part), 1)
        older = spread_early - high_dot(outer[:, :NRHS], newest_part, ((1,), (0,)))
        coeffs = jnp.concatenate([older, newest_part], axis=0)
    with scope("coeffs"):
        none = jnp.zeros((NRHS, LANES), f32)
        row = lax.broadcasted_iota(jnp.int32, (LANES, LANES), 0)
        col = lax.broadcasted_iota(jnp.int32, (LANES, LANES), 1) % NRHS
        first = jnp.where(row == col, 1.0, 0.0)
        padded = jnp.concatenate([coeffs, none], axis=0)
        combo = first - (padded + jnp.concatenate([none, coeffs], axis=0))
        hi, lo = split(jnp.concatenate([padded, combo], axis=1))
        group = lax.broadcasted_iota(jnp.int32, (LANES, 2 * LANES), 1) % LANES // NRHS
        his = [jnp.where(group == q, hi, 0.0).astype(bf16) for q in range(GROUPS)]
        los = [jnp.where(group == q, lo, 0.0).astype(bf16) for q in range(GROUPS)]
        right = jnp.concatenate(his + his + los, axis=0)
    with scope("outdot"):
        vhi = [vbuf[q, :, :LANES] for q in range(GROUPS)]
        vlo = [vbuf[q, :, LANES:] for q in range(GROUPS)]
        out = jnp.dot(jnp.concatenate(vhi + vlo + vhi, axis=1), right, preferred_element_type=f32)
        for part, out_ref in enumerate((sol_ref, res_ref)):
            for block in range(faces // 8):
                for tile in range(DOF // GROUPS):
                    row = 8 * (block * (DOF // GROUPS) + tile)
                    out_ref[8 * block:8 * block + 8, tile * LANES:(tile + 1) * LANES] = out[
                        row:row + 8, part * LANES:(part + 1) * LANES]
    with scope("drain"):
        for which, bufs in enumerate([(early_plane, early_line, early_all), (late_plane, late_line)]):
            for phase, (buf, amount) in enumerate(zip(bufs, (plane - 1, high - 1, plane - 1))):
                wait_for(buf, amount, gram_sem.at[which, 2 * phase])


def put_out(sol_ref, res_ref, sol_out, res_out, sem):
    width = sol_ref.shape[1] // PIECES
    copies = [
        pltpu.make_async_copy(src.at[:, pl.ds(piece * width, width)], dst.at[:, pl.ds(piece * width, width)], sem.at[part, piece])
        for part, (src, dst) in enumerate([(sol_ref, sol_out), (res_ref, res_out)]) for piece in range(PIECES)
    ]
    for copy in copies:
        copy.start()
    for copy in copies:
        copy.wait()


def on_device(shape, right_side, coupling, face_columns, ghost_lists):
    n_fx, n_fy, low, faces = shape
    plane = low * n_fy
    high = n_fx // low
    right_rows = right_side.reshape(faces // 8, 8, DOF // GROUPS, LANES).transpose(0, 2, 1, 3)
    coupling = coupling.reshape(faces // 8, 8, BLOCKS, HALF, LANES).transpose(2, 0, 3, 1, 4)
    rows = faces * DOF
    early = 2 * NRHS // plane
    vmem = pl.BlockSpec(memory_space=pltpu.VMEM)
    hbm = pl.BlockSpec(memory_space=pltpu.HBM)
    dma = pltpu.SemaphoreType.DMA
    i32 = jnp.int32
    out = jax.ShapeDtypeStruct(right_side.shape, f32)
    gram = [
        pltpu.VMEM((plane, early, LANES), f32),
        pltpu.VMEM((plane - 1, early, LANES), f32),
        pltpu.VMEM((high, early, LANES), f32),
        pltpu.VMEM((plane, early, LANES), f32),
        pltpu.VMEM((plane, NRHS, LANES), f32),
        pltpu.VMEM((high, NRHS, LANES), f32),
    ]
    results = pl.pallas_call(
        functools.partial(kernel, shape),
        out_shape=(out, out),
        in_specs=[hbm] * 4,
        out_specs=(vmem, vmem),
        scratch_shapes=[
            pltpu.VMEM((faces // 8, 8, DOF // GROUPS, LANES), f32),
            pltpu.SMEM(face_columns.shape, i32),
            pltpu.SMEM(ghost_lists.shape, i32),
            pltpu.VMEM((BLOCKS, faces // 8, 8, HALF, LANES), f32),
            pltpu.VMEM((faces, DOF, BLOCKS * LANES), bf16),
        ]
        + [pltpu.VMEM((faces, DOF, LANES), f32)] * (POWERS + 1)
        + [
            pltpu.VMEM((POWERS, faces, DOF, LANES), f32),
            pltpu.VMEM((faces + 4 * GROUPS, LANES, LANES), bf16),
            pltpu.VMEM((faces, HALF, LANES), f32),
            pltpu.VMEM((POWERS, 4, DOF, LANES), f32),
            pltpu.VMEM((POWERS, 4, DOF, LANES), f32),
            pltpu.VMEM((rows, 2 * LANES), bf16),
            pltpu.VMEM((rows, LANES), bf16),
            pltpu.VMEM((GROUPS, rows // GROUPS, 2 * LANES), bf16),
        ]
        + gram
        + [
            dma((3,)),
            dma((-(-BLOCKS // BATCH),)),
            dma((4,)),
            dma((2, 4)),
            dma((2, 6)),
            pltpu.SemaphoreType.REGULAR((2,)),
        ],
        compiler_params=pltpu.CompilerParams(
            collective_id=0, has_side_effects=True, vmem_limit_bytes=40 * 2**20
        ),
    )(*[pltpu.with_memory_space_constraint(x, pltpu.HBM) for x in (right_rows, coupling, face_columns, ghost_lists)])
    return pl.pallas_call(
        put_out,
        out_shape=(out, out),
        in_specs=[vmem, vmem],
        out_specs=(hbm, hbm),
        scratch_shapes=[dma((2, PIECES))],
        compiler_params=pltpu.CompilerParams(vmem_limit_bytes=2**20),
    )(*results)


def solution(mesh):
    n_fx, n_fy = mesh.shape["fx"], mesh.shape["fy"]
    low = 1
    while low * low * 4 <= n_fx:
        low *= 2

    def body(right_side, coupling, face_columns, ghost_lists):
        shape = (n_fx, n_fy, low, right_side.shape[0])
        return on_device(shape, right_side, coupling, face_columns, ghost_lists)

    placed = (
        P(("fx", "fy"), None),
        P(("fx", "fy"), None, None),
        P(("fx", "fy"), None),
        P(("fx", "fy"), None),
    )
    return jax.shard_map(
        body,
        mesh=mesh,
        in_specs=placed,
        out_specs=(P(("fx", "fy"), None), P(("fx", "fy"), None)),
        check_vma=False,
    )
```

```python
import contextlib
import functools

import jax
import jax.numpy as jnp
from jax import lax
from jax.experimental import pallas as pl
from jax.experimental.pallas import tpu as pltpu
from jax.sharding import PartitionSpec as P

DOF = 64
NRHS = 32
BLOCKS = 11
OWNED = 7
POWERS = 3
LANES = 128
HALF = DOF // 2
BATCH = 11
PIECES = 1
TOKENS = 2 * (POWERS - 1)
GROUPS = LANES // NRHS
MESH = pl.DeviceIdType.MESH
f32 = jnp.float32
bf16 = jnp.bfloat16


def split(x):
    hi = x.astype(bf16).astype(f32)
    return hi, x - hi


def lane_group(rows):
    return lax.broadcasted_iota(jnp.int32, (rows, LANES), 1) // NRHS


def pick(group, parts):
    out = parts[-1]
    for index in range(len(parts) - 2, -1, -1):
        out = jnp.where(group == index, parts[index], out)
    return out


def replicate(group, rolled, source):
    return pick(group, [rolled[(lane - source) % GROUPS] for lane in range(GROUPS)])


def rolls(x):
    return [x] + [pltpu.roll(x, step * NRHS, 1) for step in range(1, GROUPS)]


def product_tile(x, group):
    hi, lo = split(x)
    return halves(jnp.where(group < GROUPS // 2, hi, lo), group)


def halves(x, group):
    zero = jnp.zeros_like(x)
    even = group % 2 == 0
    return jnp.where(even, x, zero).astype(bf16), jnp.where(even, zero, x).astype(bf16)


def scope(name):
    return contextlib.nullcontext()


def across_gather(x, lane):
    return jnp.take_along_axis(x, jnp.full((8, LANES), lane, jnp.int32), axis=1)


def across_sum(x, lane):
    lanes = lax.broadcasted_iota(jnp.int32, (8, LANES), 1)
    return jnp.broadcast_to(jnp.sum(jnp.where(lanes == lane, x, 0.0), axis=1, keepdims=True), (8, LANES))


def eliminate(tiles, inverse, across, rights=()):
    tiles, rights = list(tiles), list(rights)
    sub = lax.broadcasted_iota(jnp.int32, (8, LANES), 0)
    lanes = lax.broadcasted_iota(jnp.int32, (8, LANES), 1)

    def down(x, row):
        return jnp.broadcast_to(x[row:row + 1, :], (8, LANES))

    for home in range(len(tiles)):
        mine = tiles[home]
        cols = [across(mine, 8 * home + c) for c in range(8)]
        for step in range(8):
            pivot = 1.0 / down(cols[step], step)
            here = sub == step
            factor = cols[step]
            if inverse:
                mine = jnp.where(lanes == 8 * home + step, jnp.where(here, 1.0, 0.0), mine)
            scaled = down(mine, step) * pivot
            mine = jnp.where(here, scaled, mine - factor * scaled)
            if rights:
                scaled = down(rights[home], step) * pivot
                rights[home] = jnp.where(here, scaled, rights[home] - factor * scaled)
            for c in range(step + 1, 8):
                scaled = down(cols[c], step) * pivot
                cols[c] = jnp.where(here, scaled, cols[c] - factor * scaled)
        tiles[home] = mine
        rows8 = [down(mine, c) for c in range(8)]
        for t in [t % len(tiles) for t in range(home + 1, home + len(tiles))]:
            factors = [across(tiles[t], 8 * home + c) for c in range(8)]
            base = jnp.where(lanes // 8 == home, 0.0, tiles[t]) if inverse else tiles[t]
            tiles[t] = base - tree([factor * row for factor, row in zip(factors, rows8)])
            if rights:
                rights[t] = rights[t] - tree([factor * down(rights[home], c) for c, factor in enumerate(factors)])
    return jnp.concatenate(rights or tiles, axis=0)


def tree(terms):
    while len(terms) > 1:
        terms = [terms[k] + terms[k + 1] for k in range(0, len(terms), 2)]
    return terms[0]


def split3(x):
    hi, rest = split(x)
    mid, low = split(rest)
    return [part.astype(bf16) for part in (hi, mid, low)]


def high_dot(left, right, dims):
    rows = left.shape[0]
    along = 1 - dims[1][0]
    left = jnp.concatenate(split3(left), axis=0)
    right = jnp.concatenate(split3(right), axis=along)
    out = lax.dot_general(left, right, (dims, ((), ())), preferred_element_type=f32)
    width = out.shape[1] // 3

    def block(i, j):
        return out[i * rows:(i + 1) * rows, j * width:(j + 1) * width]

    small = (block(1, 1) + block(0, 2)) + block(2, 0)
    return block(0, 0) + ((block(0, 1) + block(1, 0)) + small)


def kernel(shape, right_hbm, coupling_hbm, columns_hbm, ghost_hbm, sol_ref, res_ref,
           right_ref, columns_ref, ghost_ref,
           stage, mats, w0, w1, w2, w3, ordered, tiles, acc, send_buf, recv_buf,
           zbuf, newest, vbuf, early_buf, early_plane, early_line, early_all,
           late_plane, late_line,
           small_sem, load_sem, send_sem, recv_sem, gram_sem, token_sem):
    n_fx, n_fy, low, faces = shape
    plane = low * n_fy
    high = n_fx // low
    i = lax.axis_index("fx")
    j = lax.axis_index("fy")
    my_low = i % low
    my_high = i // low
    my_rank = my_low * n_fy + j
    fields = [w0, w1, w2, w3]

    def plane_target(offset):
        rank = lax.rem(my_rank + offset, plane)
        return rank, (my_high * low + rank // n_fy, rank % n_fy)

    def line_target(offset):
        place = lax.rem(my_high + offset, high)
        return (place * low + my_low, j)

    routes = [
        (1, i < n_fx - 1, (i + 1, j), i > 0),
        (0, i > 0, (i - 1, j), i < n_fx - 1),
        (3, j < n_fy - 1, (i, j + 1), j > 0),
        (2, j > 0, (i, j - 1), j < n_fy - 1),
    ]

    barrier = pltpu.get_barrier_semaphore()
    for _, has_target, target, _ in routes:
        @pl.when(has_target)
        def _(target=target):
            pl.semaphore_signal(barrier, inc=1, device_id=target, device_id_type=MESH)

    small = [
        pltpu.make_async_copy(src, dst, small_sem.at[place])
        for place, (src, dst) in enumerate([
            (ghost_hbm, ghost_ref), (columns_hbm, columns_ref),
        ])
    ]
    rights = [
        pltpu.make_async_copy(right_hbm.at[:, :, s], right_ref.at[:, s], small_sem.at[2]) for s in range(8)
    ]
    for load in rights + small:
        load.start()
    batches = [(k, min(k + BATCH, BLOCKS)) for k in range(0, BLOCKS, BATCH)]
    loads = [
        [
            pltpu.make_async_copy(coupling_hbm.at[k, :, :, s], stage.at[k, :, s], load_sem.at[place])
            for k in range(first, last) for s in range(8)
        ]
        for place, (first, last) in enumerate(batches)
    ]
    reach = TOKENS + 1
    neighbours = sum(jnp.where(route[1], 1, 0) for route in routes)
    strangers = []
    if low + n_fy - 2 > reach:
        for offset in range(1, plane):
            target = plane_target(offset)[1]
            strangers.append((jnp.abs(target[0] - i) + jnp.abs(target[1] - j) > reach, target))
    if (high - 1) * low > reach + 1:
        for offset in range(1, high):
            target = line_target(offset)
            strangers.append((jnp.abs(target[0] - i) > reach + 1, target))
    for strange, target in strangers:
        @pl.when(strange)
        def _(target=target):
            pl.semaphore_signal(barrier, inc=1, device_id=target, device_id_type=MESH)

    def pass_token(place):
        for _, has_target, target, _ in routes:
            @pl.when(has_target)
            def _(target=target):
                pl.semaphore_signal(token_sem.at[place % 2], inc=1, device_id=target, device_id_type=MESH)

    def take_token(place):
        pl.semaphore_wait(token_sem.at[place % 2], neighbours)

    for batch in loads:
        for load in batch:
            load.start()

    g8 = lane_group(8)
    g64 = lane_group(DOF)
    g32 = lane_group(HALF)

    with scope("relay"):
        pltpu.make_async_copy(right_ref, right_ref, small_sem.at[2]).wait()
        sub = lax.broadcasted_iota(jnp.int32, (8, LANES), 0)
        turn = (g8 - sub) % GROUPS
        for face in range(faces):
            for tile in range(0, DOF // GROUPS, 2):
                x = right_ref[face // 8, face % 8, tile:tile + 2, :]
                x = jnp.where(sub < GROUPS, jnp.broadcast_to(x[0:1], (8, LANES)), jnp.broadcast_to(x[1:2], (8, LANES)))
                w0[face, tile * GROUPS:tile * GROUPS + 8, :] = pick(turn, rolls(x))
        small[0].wait()

    def field_copies(power):
        return [
            pltpu.make_async_remote_copy(
                src_ref=send_buf.at[power, q], dst_ref=recv_buf.at[power, q],
                send_sem=send_sem.at[q], recv_sem=recv_sem.at[power % 2, q],
                device_id=routes[q][2], device_id_type=MESH,
            )
            for q in range(4)
        ]

    def start_copies(copies, directions):
        for q in directions:
            @pl.when(routes[q][1])
            def _(copy=copies[q]):
                copy.start()

    def send_field(power, copies, directions):
        field = fields[power]
        for q in directions:
            picked = [field[ghost_ref[routes[q][0], g]] for g in range(GROUPS)]
            send_buf[power, q] = pick(g64, picked)
        if power == 0:
            pl.semaphore_wait(barrier, neighbours + sum(jnp.where(strange, 1, 0) for strange, _ in strangers))
        start_copies(copies, directions)
        if power == 0:
            pass_token(0)

    def send_products(power, copies, directions):
        listed = {q: [ghost_ref[routes[q][0], g] for g in range(GROUPS)] for q in directions}
        for q in directions:
            pairs = [far_rows(face) for face in listed[q]]
            for parity in range(2):
                send_buf[power, q, pl.ds(parity, HALF, stride=2), :] = pick(g32, [pair[parity] for pair in pairs])
        start_copies(copies, directions)

    def build_own(power):
        field = fields[power]

        @pl.loop(0, faces, unroll=4)
        def _(face):
            x = field[face]
            top, bottom = product_tile(x, g64)
            tiles[face, 0:DOF] = top
            tiles[face, DOF:2 * DOF] = bottom

    def own_products():
        for face in range(faces):
            left = mats[face, :, :OWNED * LANES]
            right = jnp.concatenate([tiles[columns_ref[face, k]] for k in range(OWNED)], axis=0)
            out = jnp.dot(left, right, preferred_element_type=f32)
            acc[face] = out[:HALF] + out[HALF:]

    def far_rows(face):
        left = mats[face, :, OWNED * LANES:]
        right = jnp.concatenate([tiles[columns_ref[face, k]] for k in range(OWNED, BLOCKS)], axis=0)
        out = jnp.dot(left, right, preferred_element_type=f32)
        total = acc[face] + (out[:HALF] + out[HALF:])
        total = total + pltpu.roll(total, LANES // 2, 1)
        turned = pltpu.roll(total, NRHS, 1)
        even = g32 % 2 == 0
        return jnp.where(even, total, turned), jnp.where(even, turned, total)

    def far_products(power, part):
        field = fields[power + 1]
        for face in part:
            first, second = far_rows(face)
            field[face, pl.ds(0, HALF, stride=2), :] = first
            field[face, pl.ds(1, HALF, stride=2), :] = second
            both = jnp.concatenate([first, second], axis=0)
            if power < POWERS - 1:
                ordered[power + 1, face] = both
            else:
                late_rows(face, both)

    def first_rows():
        for face in range(faces):
            rows = slice(face * DOF, (face + 1) * DOF)
            a = jnp.concatenate([w0[face, pl.ds(parity, HALF, stride=2), :] for parity in range(2)], axis=0)
            hi, lo = split(pick(g64, [a + ordered[1, face], jnp.zeros_like(a), jnp.zeros_like(a), a]))
            zbuf[rows, :LANES] = hi.astype(bf16)
            zbuf[rows, LANES:] = lo.astype(bf16)
            newest[rows, :] = jnp.where(g64 < 2, hi, pltpu.roll(lo, LANES // 2, 1)).astype(bf16)

    def late_rows(face, newer):
        rows = slice(face * DOF, (face + 1) * DOF)
        hi, lo = split(ordered[POWERS - 1, face] + newer)
        zero = jnp.zeros_like(hi)
        third = g64 == POWERS - 1
        zbuf[rows, :LANES] = zbuf[rows, :LANES] + jnp.where(third, hi, zero).astype(bf16)
        zbuf[rows, LANES:] = zbuf[rows, LANES:] + jnp.where(third, lo, zero).astype(bf16)
        newest[rows, :] = jnp.where(g64 == 0, hi, lo).astype(bf16)

    def receive_field(power, copies, directions):
        for q in directions:
            has_source = routes[q][3]

            @pl.when(has_source)
            def _(copy=copies[q]):
                copy.wait_recv()

            @pl.when(jnp.logical_not(has_source))
            def _(q=q):
                recv_buf[power, q] = jnp.zeros((DOF, LANES), f32)
        for q in directions:
            hi, lo = split(recv_buf[power, q])
            hi, lo = rolls(hi), rolls(lo)
            for g in range(GROUPS):
                top, bottom = halves(pick(g64, [
                    (hi if lane < GROUPS // 2 else lo)[(lane - g) % GROUPS] for lane in range(GROUPS)
                ]), g64)
                tiles[faces + q * GROUPS + g, 0:DOF] = top
                tiles[faces + q * GROUPS + g, DOF:2 * DOF] = bottom

    def finish_sends(copies):
        for q in range(4):
            @pl.when(routes[q][1])
            def _(copy=copies[q]):
                copy.wait_send()

    def prepare():
        for place, (first, last) in enumerate(batches):
            whole = stage.at[first:last]
            pltpu.make_async_copy(whole, whole, load_sem.at[place]).wait()
            for k in range(first, last):
                for face in range(faces):
                    hi, lo = split(stage[k, face // 8, face % 8])
                    mats[face, 0:HALF, k * LANES:(k + 1) * LANES] = hi.astype(bf16)
                    mats[face, HALF:DOF, k * LANES:(k + 1) * LANES] = lo.astype(bf16)

    def wait_for(buf, count, sem):
        whole = buf.at[0:count]
        pltpu.make_async_copy(whole, whole, sem).wait()

    def scatter(which, buf, landed):
        for offset in range(1, plane):
            rank, target = plane_target(offset)
            pltpu.make_async_remote_copy(
                src_ref=buf.at[rank], dst_ref=landed.at[offset - 1], send_sem=gram_sem.at[which, 0],
                recv_sem=gram_sem.at[which, 1], device_id=target, device_id_type=MESH).start()

    def scatter_sum(which, buf, landed):
        total = buf[my_rank]
        wait_for(landed, plane - 1, gram_sem.at[which, 1])
        for offset in range(1, plane):
            total = total + landed[offset - 1]
        return total

    def exchange(which, line, total):
        line[my_high] = total
        for offset in range(1, high):
            pltpu.make_async_remote_copy(
                src_ref=line.at[my_high], dst_ref=line.at[my_high], send_sem=gram_sem.at[which, 2],
                recv_sem=gram_sem.at[which, 3], device_id=line_target(offset), device_id_type=MESH).start()

    def add_all(buf, count):
        terms = [buf[place] for place in range(count)]
        while len(terms) > 1:
            terms = [sum(terms[k:k + 2][1:], terms[k]) for k in range(0, len(terms), 2)]
        return terms[0]

    def exchange_sum(which, line):
        wait_for(line, high - 1, gram_sem.at[which, 3])
        return add_all(line, high)

    def gather(which, final, first):
        for offset in range(1, plane):
            pltpu.make_async_remote_copy(
                src_ref=final.at[my_rank], dst_ref=final.at[my_rank], send_sem=gram_sem.at[which, first],
                recv_sem=gram_sem.at[which, first + 1], device_id=plane_target(offset)[1], device_id_type=MESH).start()

    def gathered(which, final):
        wait_for(final, plane - 1, gram_sem.at[which, 5])
        return jnp.concatenate([final[rank] for rank in range(plane)], axis=0)

    def early_gram():
        @pl.loop(0, faces, unroll=4)
        def _(face):
            rows = pl.ds(pl.multiple_of(face * DOF, DOF), DOF)
            hi, lo = split(ordered[1, face] + ordered[2, face])
            hi, lo = hi.astype(bf16), lo.astype(bf16)
            second = g64 == 1
            zbuf[rows, :LANES] = jnp.where(second, hi, zbuf[rows, :LANES])
            zbuf[rows, LANES:] = jnp.where(second, lo, zbuf[rows, LANES:])
            newest[rows, :] = jnp.where(second, hi, jnp.where(g64 == 3, lo, newest[rows, :]))

        both = lax.dot_general(newest[...], zbuf[...], (((0,), (0,)), ((), ())), preferred_element_type=f32)
        half = 2 * NRHS
        gram = (both[:half, :LANES] + both[half:, LANES:]) + (both[:half, LANES:] + both[half:, :LANES])
        share = early_buf.shape[1]
        for rank in range(plane):
            early_buf[rank] = gram[rank * share:(rank + 1) * share]

    def late_gram():
        both = lax.dot_general(newest[:, :2 * NRHS], zbuf[...], (((0,), (0,)), ((), ())), preferred_element_type=f32)
        gram = (both[:NRHS, :LANES] + both[NRHS:2 * NRHS, LANES:]) + (both[:NRHS, LANES:] + both[NRHS:2 * NRHS, :LANES])
        late_plane[my_rank] = gram

    flat = [field.reshape(faces * DOF, LANES) for field in fields]

    def order_rows():
        for block in range(faces // 8):
            for pair in range(DOF // GROUPS // 2):
                for q in range(GROUPS):
                    halves = []
                    for tile in (2 * pair, 2 * pair + 1):
                        at = pl.ds(8 * block * DOF + tile * GROUPS + q, 8, stride=DOF)
                        halves.append(pick(g8, [view[at, :] for view in flat]))
                    hi, lo = split(jnp.concatenate(halves, axis=0))
                    row = 8 * (block * (DOF // GROUPS) + 2 * pair)
                    vbuf[q, row:row + 16, :LANES] = hi.astype(bf16)
                    vbuf[q, row:row + 16, LANES:] = lo.astype(bf16)

    copies = field_copies(0)
    with scope("send0"):
        send_field(0, copies, range(4))
    for power in range(POWERS):
        if power == POWERS - 1:
            with scope("egram"):
                early_gram()
                scatter(0, early_buf, early_plane)
        with scope("build%d" % power):
            build_own(power)
        if power == 0:
            with scope("prepare"):
                prepare()
                small[1].wait()
        with scope("own%d" % power):
            own_products()
        if power == 1:
            first_rows()
        if power < TOKENS // 2:
            take_token(2 * power)
            pass_token(2 * power + 1)
        with scope("recvy%d" % power):
            receive_field(power, copies, (2, 3))
            finish_sends(copies)
            if power < TOKENS // 2:
                take_token(2 * power + 1)
        with scope("recvx%d" % power):
            receive_field(power, copies, (0, 1))
        if power < POWERS - 1:
            copies = field_copies(power + 1)
            with scope("send%d" % (power + 1)):
                send_products(power + 1, copies, (0, 1))
            if power < TOKENS // 2 and 2 * power + 2 < TOKENS:
                pass_token(2 * power + 2)
            with scope("far%d" % power):
                far_products(power, range(faces))
            with scope("sendy%d" % (power + 1)):
                send_field(power + 1, copies, (2, 3))
        else:
            with scope("far%d" % power):
                far_products(power, range(faces // 2))
                with scope("eplane"):
                    exchange(0, early_line, scatter_sum(0, early_buf, early_plane))
                far_products(power, range(faces // 2, faces))

    with scope("lgram"):
        late_gram()
        gather(1, late_plane, 0)
    with scope("order"):
        order_rows()
    with scope("eline"):
        early_all[my_rank] = exchange_sum(0, early_line)
        gather(0, early_all, 4)
    with scope("lplane"):
        wait_for(late_plane, plane - 1, gram_sem.at[1, 1])
        exchange(1, late_line, add_all(late_plane, plane))
    with scope("eall"):
        system = gathered(0, early_all)
    with scope("esolve"):
        count = 2 * NRHS
        solved = eliminate([system[t:t + 8] for t in range(0, count, 8)], True, across_gather)
        spread_early = replicate(lane_group(count), rolls(solved), GROUPS - 1)
    with scope("lall"):
        last = exchange_sum(1, late_line)
    with scope("lsolve"):
        left_half = lax.broadcasted_iota(jnp.int32, (NRHS, LANES), 1) < count
        cross = jnp.where(left_half, last, 0.0)
        pad = jnp.zeros((LANES - count, LANES), f32)
        done = high_dot(cross, jnp.concatenate([solved, pad], axis=0), ((1,), (0,)))
        inner = jnp.where(left_half, done, 0.0)
        outer = high_dot(jnp.where(lax.broadcasted_iota(jnp.int32, (count, LANES), 1) < count, solved, 0.0), jnp.concatenate([cross, jnp.zeros((LANES - NRHS, LANES), f32)], axis=0), ((1,), (1,)))
        schur = high_dot(inner, jnp.concatenate([cross, jnp.zeros((LANES - NRHS, LANES), f32)], axis=0), ((1,), (1,)))
        turned = rolls(last - done)
        small_system = turned[GROUPS // 2] - schur
        rights = replicate(g32, turned, GROUPS - 1)
        cuts = range(0, NRHS, 8)
        newest_part = eliminate(
            [small_system[t:t + 8] for t in cuts], False, across_sum, [rights[t:t + 8] for t in cuts])
        older = spread_early - high_dot(outer[:, :NRHS], newest_part, ((1,), (0,)))
        coeffs = jnp.concatenate([older, newest_part], axis=0)
    with scope("coeffs"):
        none = jnp.zeros((NRHS, LANES), f32)
        row = lax.broadcasted_iota(jnp.int32, (LANES, LANES), 0)
        col = lax.broadcasted_iota(jnp.int32, (LANES, LANES), 1) % NRHS
        first = jnp.where(row == col, 1.0, 0.0)
        padded = jnp.concatenate([coeffs, none], axis=0)
        combo = first - (padded + jnp.concatenate([none, coeffs], axis=0))
        hi, lo = split(jnp.concatenate([padded, combo], axis=1))
        group = lax.broadcasted_iota(jnp.int32, (LANES, 2 * LANES), 1) % LANES // NRHS
        his = [jnp.where(group == q, hi, 0.0).astype(bf16) for q in range(GROUPS)]
        los = [jnp.where(group == q, lo, 0.0).astype(bf16) for q in range(GROUPS)]
        right = jnp.concatenate(his + his + los, axis=0)
    with scope("outdot"):
        vhi = [vbuf[q, :, :LANES] for q in range(GROUPS)]
        vlo = [vbuf[q, :, LANES:] for q in range(GROUPS)]
        out = jnp.dot(jnp.concatenate(vhi + vlo + vhi, axis=1), right, preferred_element_type=f32)
        for part, out_ref in enumerate((sol_ref, res_ref)):
            for block in range(faces // 8):
                for tile in range(DOF // GROUPS):
                    row = 8 * (block * (DOF // GROUPS) + tile)
                    out_ref[8 * block:8 * block + 8, tile * LANES:(tile + 1) * LANES] = out[
                        row:row + 8, part * LANES:(part + 1) * LANES]
    with scope("drain"):
        for which, bufs in enumerate([(early_plane, early_line, early_all), (late_plane, late_line)]):
            for phase, (buf, amount) in enumerate(zip(bufs, (plane - 1, high - 1, plane - 1))):
                wait_for(buf, amount, gram_sem.at[which, 2 * phase])


def put_out(sol_ref, res_ref, sol_out, res_out, sem):
    width = sol_ref.shape[1] // PIECES
    copies = [
        pltpu.make_async_copy(src.at[:, pl.ds(piece * width, width)], dst.at[:, pl.ds(piece * width, width)], sem.at[part, piece])
        for part, (src, dst) in enumerate([(sol_ref, sol_out), (res_ref, res_out)]) for piece in range(PIECES)
    ]
    for copy in copies:
        copy.start()
    for copy in copies:
        copy.wait()


def on_device(shape, right_side, coupling, face_columns, ghost_lists):
    n_fx, n_fy, low, faces = shape
    plane = low * n_fy
    high = n_fx // low
    right_rows = right_side.reshape(faces // 8, 8, DOF // GROUPS, LANES).transpose(0, 2, 1, 3)
    coupling = coupling.reshape(faces // 8, 8, BLOCKS, HALF, LANES).transpose(2, 0, 3, 1, 4)
    rows = faces * DOF
    early = 2 * NRHS // plane
    vmem = pl.BlockSpec(memory_space=pltpu.VMEM)
    hbm = pl.BlockSpec(memory_space=pltpu.HBM)
    dma = pltpu.SemaphoreType.DMA
    i32 = jnp.int32
    out = jax.ShapeDtypeStruct(right_side.shape, f32)
    gram = [
        pltpu.VMEM((plane, early, LANES), f32),
        pltpu.VMEM((plane - 1, early, LANES), f32),
        pltpu.VMEM((high, early, LANES), f32),
        pltpu.VMEM((plane, early, LANES), f32),
        pltpu.VMEM((plane, NRHS, LANES), f32),
        pltpu.VMEM((high, NRHS, LANES), f32),
    ]
    results = pl.pallas_call(
        functools.partial(kernel, shape),
        out_shape=(out, out),
        in_specs=[hbm] * 4,
        out_specs=(vmem, vmem),
        scratch_shapes=[
            pltpu.VMEM((faces // 8, 8, DOF // GROUPS, LANES), f32),
            pltpu.SMEM(face_columns.shape, i32),
            pltpu.SMEM(ghost_lists.shape, i32),
            pltpu.VMEM((BLOCKS, faces // 8, 8, HALF, LANES), f32),
            pltpu.VMEM((faces, DOF, BLOCKS * LANES), bf16),
        ]
        + [pltpu.VMEM((faces, DOF, LANES), f32)] * (POWERS + 1)
        + [
            pltpu.VMEM((POWERS, faces, DOF, LANES), f32),
            pltpu.VMEM((faces + 4 * GROUPS, LANES, LANES), bf16),
            pltpu.VMEM((faces, HALF, LANES), f32),
            pltpu.VMEM((POWERS, 4, DOF, LANES), f32),
            pltpu.VMEM((POWERS, 4, DOF, LANES), f32),
            pltpu.VMEM((rows, 2 * LANES), bf16),
            pltpu.VMEM((rows, LANES), bf16),
            pltpu.VMEM((GROUPS, rows // GROUPS, 2 * LANES), bf16),
        ]
        + gram
        + [
            dma((3,)),
            dma((-(-BLOCKS // BATCH),)),
            dma((4,)),
            dma((2, 4)),
            dma((2, 6)),
            pltpu.SemaphoreType.REGULAR((2,)),
        ],
        compiler_params=pltpu.CompilerParams(
            collective_id=0, has_side_effects=True, vmem_limit_bytes=40 * 2**20
        ),
    )(*[pltpu.with_memory_space_constraint(x, pltpu.HBM) for x in (right_rows, coupling, face_columns, ghost_lists)])
    return pl.pallas_call(
        put_out,
        out_shape=(out, out),
        in_specs=[vmem, vmem],
        out_specs=(hbm, hbm),
        scratch_shapes=[dma((2, PIECES))],
        compiler_params=pltpu.CompilerParams(vmem_limit_bytes=2**20),
    )(*results)


def solution(mesh):
    n_fx, n_fy = mesh.shape["fx"], mesh.shape["fy"]
    low = 1
    while low * low * 4 <= n_fx:
        low *= 2

    def body(right_side, coupling, face_columns, ghost_lists):
        shape = (n_fx, n_fy, low, right_side.shape[0])
        return on_device(shape, right_side, coupling, face_columns, ghost_lists)

    placed = (
        P(("fx", "fy"), None),
        P(("fx", "fy"), None, None),
        P(("fx", "fy"), None),
        P(("fx", "fy"), None),
    )
    return jax.shard_map(
        body,
        mesh=mesh,
        in_specs=placed,
        out_specs=(P(("fx", "fy"), None), P(("fx", "fy"), None)),
        check_vma=False,
    )
```

```python
import contextlib
import functools

import jax
import jax.numpy as jnp
from jax import lax
from jax.experimental import pallas as pl
from jax.experimental.pallas import tpu as pltpu
from jax.sharding import PartitionSpec as P

DOF = 64
NRHS = 32
BLOCKS = 11
OWNED = 7
POWERS = 3
LANES = 128
HALF = DOF // 2
BATCH = 11
PIECES = 1
TOKENS = 2 * (POWERS - 1)
GROUPS = LANES // NRHS
MESH = pl.DeviceIdType.MESH
f32 = jnp.float32
bf16 = jnp.bfloat16


def split(x):
    hi = x.astype(bf16).astype(f32)
    return hi, x - hi


def lane_group(rows):
    return lax.broadcasted_iota(jnp.int32, (rows, LANES), 1) // NRHS


def pick(group, parts):
    out = parts[-1]
    for index in range(len(parts) - 2, -1, -1):
        out = jnp.where(group == index, parts[index], out)
    return out


def replicate(group, rolled, source):
    return pick(group, [rolled[(lane - source) % GROUPS] for lane in range(GROUPS)])


def rolls(x):
    return [x] + [pltpu.roll(x, step * NRHS, 1) for step in range(1, GROUPS)]


def product_tile(x, group):
    hi, lo = split(x)
    return halves(jnp.where(group < GROUPS // 2, hi, lo), group)


def halves(x, group):
    zero = jnp.zeros_like(x)
    even = group % 2 == 0
    return jnp.where(even, x, zero).astype(bf16), jnp.where(even, zero, x).astype(bf16)


def scope(name):
    return contextlib.nullcontext()


def across_gather(x, lane):
    return jnp.take_along_axis(x, jnp.full((8, LANES), lane, jnp.int32), axis=1)


def across_sum(x, lane):
    lanes = lax.broadcasted_iota(jnp.int32, (8, LANES), 1)
    return jnp.broadcast_to(jnp.sum(jnp.where(lanes == lane, x, 0.0), axis=1, keepdims=True), (8, LANES))


def eliminate(tiles, inverse, across, rights=()):
    tiles, rights = list(tiles), list(rights)
    sub = lax.broadcasted_iota(jnp.int32, (8, LANES), 0)
    lanes = lax.broadcasted_iota(jnp.int32, (8, LANES), 1)

    def down(x, row):
        return jnp.broadcast_to(x[row:row + 1, :], (8, LANES))

    for home in range(len(tiles)):
        mine = tiles[home]
        cols = [across(mine, 8 * home + c) for c in range(8)]
        for step in range(8):
            pivot = 1.0 / down(cols[step], step)
            here = sub == step
            factor = cols[step]
            if inverse:
                mine = jnp.where(lanes == 8 * home + step, jnp.where(here, 1.0, 0.0), mine)
            scaled = down(mine, step) * pivot
            mine = jnp.where(here, scaled, mine - factor * scaled)
            if rights:
                scaled = down(rights[home], step) * pivot
                rights[home] = jnp.where(here, scaled, rights[home] - factor * scaled)
            for c in range(step + 1, 8):
                scaled = down(cols[c], step) * pivot
                cols[c] = jnp.where(here, scaled, cols[c] - factor * scaled)
        tiles[home] = mine
        rows8 = [down(mine, c) for c in range(8)]
        for t in [t % len(tiles) for t in range(home + 1, home + len(tiles))]:
            factors = [across(tiles[t], 8 * home + c) for c in range(8)]
            base = jnp.where(lanes // 8 == home, 0.0, tiles[t]) if inverse else tiles[t]
            tiles[t] = base - tree([factor * row for factor, row in zip(factors, rows8)])
            if rights:
                rights[t] = rights[t] - tree([factor * down(rights[home], c) for c, factor in enumerate(factors)])
    return jnp.concatenate(rights or tiles, axis=0)


def tree(terms):
    while len(terms) > 1:
        terms = [terms[k] + terms[k + 1] for k in range(0, len(terms), 2)]
    return terms[0]


def split3(x):
    hi, rest = split(x)
    mid, low = split(rest)
    return [part.astype(bf16) for part in (hi, mid, low)]


def high_dot(left, right, dims):
    rows = left.shape[0]
    along = 1 - dims[1][0]
    left = jnp.concatenate(split3(left), axis=0)
    right = jnp.concatenate(split3(right), axis=along)
    out = lax.dot_general(left, right, (dims, ((), ())), preferred_element_type=f32)
    width = out.shape[1] // 3

    def block(i, j):
        return out[i * rows:(i + 1) * rows, j * width:(j + 1) * width]

    small = (block(1, 1) + block(0, 2)) + block(2, 0)
    return block(0, 0) + ((block(0, 1) + block(1, 0)) + small)


def kernel(shape, right_hbm, coupling_hbm, columns_hbm, ghost_hbm, sol_ref, res_ref,
           right_ref, columns_ref, ghost_ref,
           stage, mats, w0, w1, w2, w3, ordered, tiles, acc, send_buf, recv_buf,
           zbuf, newest, vbuf, early_buf, early_plane, early_line, early_all,
           late_plane, late_line,
           small_sem, load_sem, send_sem, recv_sem, gram_sem, token_sem):
    n_fx, n_fy, low, faces = shape
    plane = low * n_fy
    high = n_fx // low
    i = lax.axis_index("fx")
    j = lax.axis_index("fy")
    my_low = i % low
    my_high = i // low
    my_rank = my_low * n_fy + j
    fields = [w0, w1, w2, w3]

    def plane_target(offset):
        rank = lax.rem(my_rank + offset, plane)
        return rank, (my_high * low + rank // n_fy, rank % n_fy)

    def line_target(offset):
        place = lax.rem(my_high + offset, high)
        return (place * low + my_low, j)

    routes = [
        (1, i < n_fx - 1, (i + 1, j), i > 0),
        (0, i > 0, (i - 1, j), i < n_fx - 1),
        (3, j < n_fy - 1, (i, j + 1), j > 0),
        (2, j > 0, (i, j - 1), j < n_fy - 1),
    ]

    barrier = pltpu.get_barrier_semaphore()
    for _, has_target, target, _ in routes:
        @pl.when(has_target)
        def _(target=target):
            pl.semaphore_signal(barrier, inc=1, device_id=target, device_id_type=MESH)

    small = [
        pltpu.make_async_copy(src, dst, small_sem.at[place])
        for place, (src, dst) in enumerate([
            (ghost_hbm, ghost_ref), (columns_hbm, columns_ref),
        ])
    ]
    rights = [
        pltpu.make_async_copy(right_hbm.at[:, :, s], right_ref.at[:, s], small_sem.at[2]) for s in range(8)
    ]
    for load in rights + small:
        load.start()
    batches = [(k, min(k + BATCH, BLOCKS)) for k in range(0, BLOCKS, BATCH)]
    loads = [
        [
            pltpu.make_async_copy(coupling_hbm.at[k, :, :, s], stage.at[k, :, s], load_sem.at[place])
            for k in range(first, last) for s in range(8)
        ]
        for place, (first, last) in enumerate(batches)
    ]
    reach = TOKENS + 1
    neighbours = sum(jnp.where(route[1], 1, 0) for route in routes)
    strangers = []
    if low + n_fy - 2 > reach:
        for offset in range(1, plane):
            target = plane_target(offset)[1]
            strangers.append((jnp.abs(target[0] - i) + jnp.abs(target[1] - j) > reach, target))
    if (high - 1) * low > reach + 1:
        for offset in range(1, high):
            target = line_target(offset)
            strangers.append((jnp.abs(target[0] - i) > reach + 1, target))
    for strange, target in strangers:
        @pl.when(strange)
        def _(target=target):
            pl.semaphore_signal(barrier, inc=1, device_id=target, device_id_type=MESH)

    def pass_token(place):
        for _, has_target, target, _ in routes:
            @pl.when(has_target)
            def _(target=target):
                pl.semaphore_signal(token_sem.at[place % 2], inc=1, device_id=target, device_id_type=MESH)

    def take_token(place):
        pl.semaphore_wait(token_sem.at[place % 2], neighbours)

    for batch in loads:
        for load in batch:
            load.start()

    g8 = lane_group(8)
    g64 = lane_group(DOF)
    g32 = lane_group(HALF)

    with scope("relay"):
        pltpu.make_async_copy(right_ref, right_ref, small_sem.at[2]).wait()
        sub = lax.broadcasted_iota(jnp.int32, (8, LANES), 0)
        turn = (g8 - sub) % GROUPS
        for face in range(faces):
            for tile in range(0, DOF // GROUPS, 2):
                x = right_ref[face // 8, face % 8, tile:tile + 2, :]
                x = jnp.where(sub < GROUPS, jnp.broadcast_to(x[0:1], (8, LANES)), jnp.broadcast_to(x[1:2], (8, LANES)))
                w0[face, tile * GROUPS:tile * GROUPS + 8, :] = pick(turn, rolls(x))
        small[0].wait()

    def field_copies(power):
        return [
            pltpu.make_async_remote_copy(
                src_ref=send_buf.at[power, q], dst_ref=recv_buf.at[power, q],
                send_sem=send_sem.at[q], recv_sem=recv_sem.at[power % 2, q],
                device_id=routes[q][2], device_id_type=MESH,
            )
            for q in range(4)
        ]

    def start_copies(copies, directions):
        for q in directions:
            @pl.when(routes[q][1])
            def _(copy=copies[q]):
                copy.start()

    def send_field(power, copies, directions):
        field = fields[power]
        for q in directions:
            picked = [field[ghost_ref[routes[q][0], g]] for g in range(GROUPS)]
            send_buf[power, q] = pick(g64, picked)
        if power == 0:
            pl.semaphore_wait(barrier, neighbours + sum(jnp.where(strange, 1, 0) for strange, _ in strangers))
        start_copies(copies, directions)
        if power == 0:
            pass_token(0)

    def send_products(power, copies, directions):
        listed = {q: [ghost_ref[routes[q][0], g] for g in range(GROUPS)] for q in directions}
        for q in directions:
            pairs = [far_rows(face) for face in listed[q]]
            for parity in range(2):
                send_buf[power, q, pl.ds(parity, HALF, stride=2), :] = pick(g32, [pair[parity] for pair in pairs])
        start_copies(copies, directions)

    def build_own(power):
        field = fields[power]

        @pl.loop(0, faces, unroll=4)
        def _(face):
            x = field[face]
            top, bottom = product_tile(x, g64)
            tiles[face, 0:DOF] = top
            tiles[face, DOF:2 * DOF] = bottom

    def own_products():
        for face in range(faces):
            left = mats[face, :, :OWNED * LANES]
            right = jnp.concatenate([tiles[columns_ref[face, k]] for k in range(OWNED)], axis=0)
            out = jnp.dot(left, right, preferred_element_type=f32)
            acc[face] = out[:HALF] + out[HALF:]

    def far_rows(face):
        left = mats[face, :, OWNED * LANES:]
        right = jnp.concatenate([tiles[columns_ref[face, k]] for k in range(OWNED, BLOCKS)], axis=0)
        out = jnp.dot(left, right, preferred_element_type=f32)
        total = acc[face] + (out[:HALF] + out[HALF:])
        total = total + pltpu.roll(total, LANES // 2, 1)
        turned = pltpu.roll(total, NRHS, 1)
        even = g32 % 2 == 0
        return jnp.where(even, total, turned), jnp.where(even, turned, total)

    def far_products(power, part):
        field = fields[power + 1]
        for face in part:
            first, second = far_rows(face)
            field[face, pl.ds(0, HALF, stride=2), :] = first
            field[face, pl.ds(1, HALF, stride=2), :] = second
            both = jnp.concatenate([first, second], axis=0)
            if power < POWERS - 1:
                ordered[power + 1, face] = both
            else:
                late_rows(face, both)

    def first_rows():
        for face in range(faces):
            rows = slice(face * DOF, (face + 1) * DOF)
            a = jnp.concatenate([w0[face, pl.ds(parity, HALF, stride=2), :] for parity in range(2)], axis=0)
            hi, lo = split(pick(g64, [a + ordered[1, face], jnp.zeros_like(a), jnp.zeros_like(a), a]))
            zbuf[rows, :LANES] = hi.astype(bf16)
            zbuf[rows, LANES:] = lo.astype(bf16)
            newest[rows, :] = jnp.where(g64 < 2, hi, pltpu.roll(lo, LANES // 2, 1)).astype(bf16)

    def late_rows(face, newer):
        rows = slice(face * DOF, (face + 1) * DOF)
        hi, lo = split(ordered[POWERS - 1, face] + newer)
        zero = jnp.zeros_like(hi)
        third = g64 == POWERS - 1
        zbuf[rows, :LANES] = zbuf[rows, :LANES] + jnp.where(third, hi, zero).astype(bf16)
        zbuf[rows, LANES:] = zbuf[rows, LANES:] + jnp.where(third, lo, zero).astype(bf16)
        newest[rows, :] = jnp.where(g64 == 0, hi, lo).astype(bf16)

    def receive_field(power, copies, directions):
        for q in directions:
            has_source = routes[q][3]

            @pl.when(has_source)
            def _(copy=copies[q]):
                copy.wait_recv()

            @pl.when(jnp.logical_not(has_source))
            def _(q=q):
                recv_buf[power, q] = jnp.zeros((DOF, LANES), f32)
        for q in directions:
            hi, lo = split(recv_buf[power, q])
            hi, lo = rolls(hi), rolls(lo)
            for g in range(GROUPS):
                top, bottom = halves(pick(g64, [
                    (hi if lane < GROUPS // 2 else lo)[(lane - g) % GROUPS] for lane in range(GROUPS)
                ]), g64)
                tiles[faces + q * GROUPS + g, 0:DOF] = top
                tiles[faces + q * GROUPS + g, DOF:2 * DOF] = bottom

    def finish_sends(copies):
        for q in range(4):
            @pl.when(routes[q][1])
            def _(copy=copies[q]):
                copy.wait_send()

    def prepare():
        for place, (first, last) in enumerate(batches):
            whole = stage.at[first:last]
            pltpu.make_async_copy(whole, whole, load_sem.at[place]).wait()
            for k in range(first, last):
                for face in range(faces):
                    hi, lo = split(stage[k, face // 8, face % 8])
                    mats[face, 0:HALF, k * LANES:(k + 1) * LANES] = hi.astype(bf16)
                    mats[face, HALF:DOF, k * LANES:(k + 1) * LANES] = lo.astype(bf16)

    def wait_for(buf, count, sem):
        whole = buf.at[0:count]
        pltpu.make_async_copy(whole, whole, sem).wait()

    def scatter(which, buf, landed):
        for offset in range(1, plane):
            rank, target = plane_target(offset)
            pltpu.make_async_remote_copy(
                src_ref=buf.at[rank], dst_ref=landed.at[offset - 1], send_sem=gram_sem.at[4 * which],
                recv_sem=gram_sem.at[4 * which + 1], device_id=target, device_id_type=MESH).start()

    def scatter_sum(which, buf, landed):
        total = buf[my_rank]
        wait_for(landed, plane - 1, gram_sem.at[4 * which + 1])
        for offset in range(1, plane):
            total = total + landed[offset - 1]
        return total

    def exchange(which, line, total):
        line[my_high] = total
        for offset in range(1, high):
            pltpu.make_async_remote_copy(
                src_ref=line.at[my_high], dst_ref=line.at[my_high], send_sem=gram_sem.at[4 * which],
                recv_sem=gram_sem.at[4 * which + 2], device_id=line_target(offset), device_id_type=MESH).start()

    def add_all(buf, count):
        terms = [buf[place] for place in range(count)]
        while len(terms) > 1:
            terms = [sum(terms[k:k + 2][1:], terms[k]) for k in range(0, len(terms), 2)]
        return terms[0]

    def exchange_sum(which, line):
        wait_for(line, high - 1, gram_sem.at[4 * which + 2])
        return add_all(line, high)

    def gather(which, final, first):
        for offset in range(1, plane):
            pltpu.make_async_remote_copy(
                src_ref=final.at[my_rank], dst_ref=final.at[my_rank], send_sem=gram_sem.at[4 * which],
                recv_sem=gram_sem.at[4 * which + first], device_id=plane_target(offset)[1], device_id_type=MESH).start()

    def gathered(which, final):
        wait_for(final, plane - 1, gram_sem.at[4 * which + 3])
        return jnp.concatenate([final[rank] for rank in range(plane)], axis=0)

    def early_gram():
        @pl.loop(0, faces, unroll=4)
        def _(face):
            rows = pl.ds(pl.multiple_of(face * DOF, DOF), DOF)
            hi, lo = split(ordered[1, face] + ordered[2, face])
            hi, lo = hi.astype(bf16), lo.astype(bf16)
            second = g64 == 1
            zbuf[rows, :LANES] = jnp.where(second, hi, zbuf[rows, :LANES])
            zbuf[rows, LANES:] = jnp.where(second, lo, zbuf[rows, LANES:])
            newest[rows, :] = jnp.where(second, hi, jnp.where(g64 == 3, lo, newest[rows, :]))

        both = lax.dot_general(newest[...], zbuf[...], (((0,), (0,)), ((), ())), preferred_element_type=f32)
        half = 2 * NRHS
        gram = (both[:half, :LANES] + both[half:, LANES:]) + (both[:half, LANES:] + both[half:, :LANES])
        share = early_buf.shape[1]
        for rank in range(plane):
            early_buf[rank] = gram[rank * share:(rank + 1) * share]

    def late_gram():
        both = lax.dot_general(newest[:, :2 * NRHS], zbuf[...], (((0,), (0,)), ((), ())), preferred_element_type=f32)
        gram = (both[:NRHS, :LANES] + both[NRHS:2 * NRHS, LANES:]) + (both[:NRHS, LANES:] + both[NRHS:2 * NRHS, :LANES])
        late_plane[my_rank] = gram

    flat = [field.reshape(faces * DOF, LANES) for field in fields]

    def order_rows():
        for block in range(faces // 8):
            for pair in range(DOF // GROUPS // 2):
                for q in range(GROUPS):
                    halves = []
                    for tile in (2 * pair, 2 * pair + 1):
                        at = pl.ds(8 * block * DOF + tile * GROUPS + q, 8, stride=DOF)
                        halves.append(pick(g8, [view[at, :] for view in flat]))
                    hi, lo = split(jnp.concatenate(halves, axis=0))
                    row = 8 * (block * (DOF // GROUPS) + 2 * pair)
                    vbuf[q, row:row + 16, :LANES] = hi.astype(bf16)
                    vbuf[q, row:row + 16, LANES:] = lo.astype(bf16)

    copies = field_copies(0)
    with scope("send0"):
        send_field(0, copies, range(4))
    for power in range(POWERS):
        if power == POWERS - 1:
            with scope("egram"):
                early_gram()
                scatter(0, early_buf, early_plane)
        with scope("build%d" % power):
            build_own(power)
        if power == 0:
            with scope("prepare"):
                prepare()
                small[1].wait()
        with scope("own%d" % power):
            own_products()
        if power == 1:
            first_rows()
        if power < TOKENS // 2:
            take_token(2 * power)
            pass_token(2 * power + 1)
        with scope("recvy%d" % power):
            receive_field(power, copies, (2, 3))
            finish_sends(copies)
            if power < TOKENS // 2:
                take_token(2 * power + 1)
        with scope("recvx%d" % power):
            receive_field(power, copies, (0, 1))
        if power < POWERS - 1:
            copies = field_copies(power + 1)
            with scope("send%d" % (power + 1)):
                send_products(power + 1, copies, (0, 1))
            if power < TOKENS // 2 and 2 * power + 2 < TOKENS:
                pass_token(2 * power + 2)
            with scope("far%d" % power):
                far_products(power, range(faces))
            with scope("sendy%d" % (power + 1)):
                send_field(power + 1, copies, (2, 3))
        else:
            with scope("far%d" % power):
                far_products(power, range(faces // 2))
                with scope("eplane"):
                    exchange(0, early_line, scatter_sum(0, early_buf, early_plane))
                far_products(power, range(faces // 2, faces))

    with scope("lgram"):
        late_gram()
        gather(1, late_plane, 1)
    with scope("order"):
        order_rows()
    with scope("eline"):
        early_all[my_rank] = exchange_sum(0, early_line)
        gather(0, early_all, 3)
    with scope("lplane"):
        wait_for(late_plane, plane - 1, gram_sem.at[5])
        exchange(1, late_line, add_all(late_plane, plane))
    with scope("eall"):
        system = gathered(0, early_all)
    with scope("esolve"):
        count = 2 * NRHS
        solved = eliminate([system[t:t + 8] for t in range(0, count, 8)], True, across_gather)
        spread_early = replicate(lane_group(count), rolls(solved), GROUPS - 1)
    with scope("lall"):
        last = exchange_sum(1, late_line)
    with scope("lsolve"):
        left_half = lax.broadcasted_iota(jnp.int32, (NRHS, LANES), 1) < count
        cross = jnp.where(left_half, last, 0.0)
        pad = jnp.zeros((LANES - count, LANES), f32)
        done = high_dot(cross, jnp.concatenate([solved, pad], axis=0), ((1,), (0,)))
        inner = jnp.where(left_half, done, 0.0)
        outer = high_dot(jnp.where(lax.broadcasted_iota(jnp.int32, (count, LANES), 1) < count, solved, 0.0), jnp.concatenate([cross, jnp.zeros((LANES - NRHS, LANES), f32)], axis=0), ((1,), (1,)))
        schur = high_dot(inner, jnp.concatenate([cross, jnp.zeros((LANES - NRHS, LANES), f32)], axis=0), ((1,), (1,)))
        turned = rolls(last - done)
        small_system = turned[GROUPS // 2] - schur
        rights = replicate(g32, turned, GROUPS - 1)
        cuts = range(0, NRHS, 8)
        newest_part = eliminate(
            [small_system[t:t + 8] for t in cuts], False, across_sum, [rights[t:t + 8] for t in cuts])
        older = spread_early - high_dot(outer[:, :NRHS], newest_part, ((1,), (0,)))
        coeffs = jnp.concatenate([older, newest_part], axis=0)
    with scope("coeffs"):
        none = jnp.zeros((NRHS, LANES), f32)
        row = lax.broadcasted_iota(jnp.int32, (LANES, LANES), 0)
        col = lax.broadcasted_iota(jnp.int32, (LANES, LANES), 1) % NRHS
        first = jnp.where(row == col, 1.0, 0.0)
        padded = jnp.concatenate([coeffs, none], axis=0)
        combo = first - (padded + jnp.concatenate([none, coeffs], axis=0))
        hi, lo = split(jnp.concatenate([padded, combo], axis=1))
        group = lax.broadcasted_iota(jnp.int32, (LANES, 2 * LANES), 1) % LANES // NRHS
        his = [jnp.where(group == q, hi, 0.0).astype(bf16) for q in range(GROUPS)]
        los = [jnp.where(group == q, lo, 0.0).astype(bf16) for q in range(GROUPS)]
        right = jnp.concatenate(his + his + los, axis=0)
    with scope("outdot"):
        vhi = [vbuf[q, :, :LANES] for q in range(GROUPS)]
        vlo = [vbuf[q, :, LANES:] for q in range(GROUPS)]
        out = jnp.dot(jnp.concatenate(vhi + vlo + vhi, axis=1), right, preferred_element_type=f32)
        for part, out_ref in enumerate((sol_ref, res_ref)):
            for block in range(faces // 8):
                for tile in range(DOF // GROUPS):
                    row = 8 * (block * (DOF // GROUPS) + tile)
                    out_ref[8 * block:8 * block + 8, tile * LANES:(tile + 1) * LANES] = out[
                        row:row + 8, part * LANES:(part + 1) * LANES]
    with scope("drain"):
        sized = ordered.reshape(POWERS * faces * DOF, LANES)
        sent = 2 * (plane - 1) + high - 1
        wait_for(sized, sent * early_buf.shape[1], gram_sem.at[0])
        wait_for(sized, (sent - plane + 1) * NRHS, gram_sem.at[4])


def put_out(sol_ref, res_ref, sol_out, res_out, sem):
    width = sol_ref.shape[1] // PIECES
    copies = [
        pltpu.make_async_copy(src.at[:, pl.ds(piece * width, width)], dst.at[:, pl.ds(piece * width, width)], sem.at[part, piece])
        for part, (src, dst) in enumerate([(sol_ref, sol_out), (res_ref, res_out)]) for piece in range(PIECES)
    ]
    for copy in copies:
        copy.start()
    for copy in copies:
        copy.wait()


def on_device(shape, right_side, coupling, face_columns, ghost_lists):
    n_fx, n_fy, low, faces = shape
    plane = low * n_fy
    high = n_fx // low
    right_rows = right_side.reshape(faces // 8, 8, DOF // GROUPS, LANES).transpose(0, 2, 1, 3)
    coupling = coupling.reshape(faces // 8, 8, BLOCKS, HALF, LANES).transpose(2, 0, 3, 1, 4)
    rows = faces * DOF
    early = 2 * NRHS // plane
    vmem = pl.BlockSpec(memory_space=pltpu.VMEM)
    hbm = pl.BlockSpec(memory_space=pltpu.HBM)
    dma = pltpu.SemaphoreType.DMA
    i32 = jnp.int32
    out = jax.ShapeDtypeStruct(right_side.shape, f32)
    gram = [
        pltpu.VMEM((plane, early, LANES), f32),
        pltpu.VMEM((plane - 1, early, LANES), f32),
        pltpu.VMEM((high, early, LANES), f32),
        pltpu.VMEM((plane, early, LANES), f32),
        pltpu.VMEM((plane, NRHS, LANES), f32),
        pltpu.VMEM((high, NRHS, LANES), f32),
    ]
    results = pl.pallas_call(
        functools.partial(kernel, shape),
        out_shape=(out, out),
        in_specs=[hbm] * 4,
        out_specs=(vmem, vmem),
        scratch_shapes=[
            pltpu.VMEM((faces // 8, 8, DOF // GROUPS, LANES), f32),
            pltpu.SMEM(face_columns.shape, i32),
            pltpu.SMEM(ghost_lists.shape, i32),
            pltpu.VMEM((BLOCKS, faces // 8, 8, HALF, LANES), f32),
            pltpu.VMEM((faces, DOF, BLOCKS * LANES), bf16),
        ]
        + [pltpu.VMEM((faces, DOF, LANES), f32)] * (POWERS + 1)
        + [
            pltpu.VMEM((POWERS, faces, DOF, LANES), f32),
            pltpu.VMEM((faces + 4 * GROUPS, LANES, LANES), bf16),
            pltpu.VMEM((faces, HALF, LANES), f32),
            pltpu.VMEM((POWERS, 4, DOF, LANES), f32),
            pltpu.VMEM((POWERS, 4, DOF, LANES), f32),
            pltpu.VMEM((rows, 2 * LANES), bf16),
            pltpu.VMEM((rows, LANES), bf16),
            pltpu.VMEM((GROUPS, rows // GROUPS, 2 * LANES), bf16),
        ]
        + gram
        + [
            dma((3,)),
            dma((-(-BLOCKS // BATCH),)),
            dma((4,)),
            dma((2, 4)),
            dma((7,)),
            pltpu.SemaphoreType.REGULAR((2,)),
        ],
        compiler_params=pltpu.CompilerParams(
            collective_id=0, has_side_effects=True, vmem_limit_bytes=40 * 2**20
        ),
    )(*[pltpu.with_memory_space_constraint(x, pltpu.HBM) for x in (right_rows, coupling, face_columns, ghost_lists)])
    return pl.pallas_call(
        put_out,
        out_shape=(out, out),
        in_specs=[vmem, vmem],
        out_specs=(hbm, hbm),
        scratch_shapes=[dma((2, PIECES))],
        compiler_params=pltpu.CompilerParams(vmem_limit_bytes=2**20),
    )(*results)


def solution(mesh):
    n_fx, n_fy = mesh.shape["fx"], mesh.shape["fy"]
    low = 1
    while low * low * 4 <= n_fx:
        low *= 2

    def body(right_side, coupling, face_columns, ghost_lists):
        shape = (n_fx, n_fy, low, right_side.shape[0])
        return on_device(shape, right_side, coupling, face_columns, ghost_lists)

    placed = (
        P(("fx", "fy"), None),
        P(("fx", "fy"), None, None),
        P(("fx", "fy"), None),
        P(("fx", "fy"), None),
    )
    return jax.shard_map(
        body,
        mesh=mesh,
        in_specs=placed,
        out_specs=(P(("fx", "fy"), None), P(("fx", "fy"), None)),
        check_vma=False,
    )
```

```python
import contextlib
import functools

import jax
import jax.numpy as jnp
from jax import lax
from jax.experimental import pallas as pl
from jax.experimental.pallas import tpu as pltpu
from jax.sharding import PartitionSpec as P

DOF = 64
NRHS = 32
BLOCKS = 11
OWNED = 7
POWERS = 3
LANES = 128
HALF = DOF // 2
BATCH = 11
PIECES = 1
TOKENS = 2 * (POWERS - 1)
GROUPS = LANES // NRHS
MESH = pl.DeviceIdType.MESH
f32 = jnp.float32
bf16 = jnp.bfloat16


def split(x):
    hi = x.astype(bf16).astype(f32)
    return hi, x - hi


def lane_group(rows):
    return lax.broadcasted_iota(jnp.int32, (rows, LANES), 1) // NRHS


def pick(group, parts):
    out = parts[-1]
    for index in range(len(parts) - 2, -1, -1):
        out = jnp.where(group == index, parts[index], out)
    return out


def replicate(group, rolled, source):
    return pick(group, [rolled[(lane - source) % GROUPS] for lane in range(GROUPS)])


def rolls(x):
    return [x] + [pltpu.roll(x, step * NRHS, 1) for step in range(1, GROUPS)]


def product_tile(x, group):
    hi, lo = split(x)
    return halves(jnp.where(group < GROUPS // 2, hi, lo), group)


def halves(x, group):
    zero = jnp.zeros_like(x)
    even = group % 2 == 0
    return jnp.where(even, x, zero).astype(bf16), jnp.where(even, zero, x).astype(bf16)


def scope(name):
    return contextlib.nullcontext()


def across_gather(x, lane):
    return jnp.take_along_axis(x, jnp.full((8, LANES), lane, jnp.int32), axis=1)


def across_sum(x, lane):
    lanes = lax.broadcasted_iota(jnp.int32, (8, LANES), 1)
    return jnp.broadcast_to(jnp.sum(jnp.where(lanes == lane, x, 0.0), axis=1, keepdims=True), (8, LANES))


def eliminate(tiles, inverse, across, rights=()):
    tiles, rights = list(tiles), list(rights)
    sub = lax.broadcasted_iota(jnp.int32, (8, LANES), 0)
    lanes = lax.broadcasted_iota(jnp.int32, (8, LANES), 1)

    def down(x, row):
        return jnp.broadcast_to(x[row:row + 1, :], (8, LANES))

    for home in range(len(tiles)):
        mine = tiles[home]
        cols = [across(mine, 8 * home + c) for c in range(8)]
        for step in range(8):
            pivot = 1.0 / down(cols[step], step)
            here = sub == step
            factor = cols[step]
            if inverse:
                mine = jnp.where(lanes == 8 * home + step, jnp.where(here, 1.0, 0.0), mine)
            scaled = down(mine, step) * pivot
            mine = jnp.where(here, scaled, mine - factor * scaled)
            if rights:
                scaled = down(rights[home], step) * pivot
                rights[home] = jnp.where(here, scaled, rights[home] - factor * scaled)
            for c in range(step + 1, 8):
                scaled = down(cols[c], step) * pivot
                cols[c] = jnp.where(here, scaled, cols[c] - factor * scaled)
        tiles[home] = mine
        rows8 = [down(mine, c) for c in range(8)]
        for t in [t % len(tiles) for t in range(home + 1, home + len(tiles))]:
            factors = [across(tiles[t], 8 * home + c) for c in range(8)]
            base = jnp.where(lanes // 8 == home, 0.0, tiles[t]) if inverse else tiles[t]
            tiles[t] = base - tree([factor * row for factor, row in zip(factors, rows8)])
            if rights:
                rights[t] = rights[t] - tree([factor * down(rights[home], c) for c, factor in enumerate(factors)])
    return jnp.concatenate(rights or tiles, axis=0)


def tree(terms):
    while len(terms) > 1:
        terms = [terms[k] + terms[k + 1] for k in range(0, len(terms), 2)]
    return terms[0]


def split3(x):
    hi, rest = split(x)
    mid, low = split(rest)
    return [part.astype(bf16) for part in (hi, mid, low)]


def high_dot(left, right, dims):
    rows = left.shape[0]
    along = 1 - dims[1][0]
    left = jnp.concatenate(split3(left), axis=0)
    right = jnp.concatenate(split3(right), axis=along)
    out = lax.dot_general(left, right, (dims, ((), ())), preferred_element_type=f32)
    width = out.shape[1] // 3

    def block(i, j):
        return out[i * rows:(i + 1) * rows, j * width:(j + 1) * width]

    small = (block(1, 1) + block(0, 2)) + block(2, 0)
    return block(0, 0) + ((block(0, 1) + block(1, 0)) + small)


def kernel(shape, right_hbm, coupling_hbm, columns_hbm, ghost_hbm, sol_ref, res_ref,
           right_ref, columns_ref, ghost_ref,
           stage, mats, w0, w1, w2, w3, ordered, tiles, acc, send_buf, recv_buf,
           zbuf, newest, vbuf, early_buf, early_plane, early_line, early_all,
           late_plane, late_line,
           small_sem, load_sem, send_sem, recv_sem, gram_sem, token_sem):
    n_fx, n_fy, low, faces = shape
    plane = low * n_fy
    high = n_fx // low
    i = lax.axis_index("fx")
    j = lax.axis_index("fy")
    my_low = i % low
    my_high = i // low
    my_rank = my_low * n_fy + j
    fields = [w0, w1, w2, w3]

    def plane_target(offset):
        rank = lax.rem(my_rank + offset, plane)
        return rank, (my_high * low + rank // n_fy, rank % n_fy)

    def line_target(offset):
        place = lax.rem(my_high + offset, high)
        return (place * low + my_low, j)

    routes = [
        (1, i < n_fx - 1, (i + 1, j), i > 0),
        (0, i > 0, (i - 1, j), i < n_fx - 1),
        (3, j < n_fy - 1, (i, j + 1), j > 0),
        (2, j > 0, (i, j - 1), j < n_fy - 1),
    ]

    barrier = pltpu.get_barrier_semaphore()
    for _, has_target, target, _ in routes:
        @pl.when(has_target)
        def _(target=target):
            pl.semaphore_signal(barrier, inc=1, device_id=target, device_id_type=MESH)

    small = [
        pltpu.make_async_copy(src, dst, small_sem.at[place])
        for place, (src, dst) in enumerate([
            (ghost_hbm, ghost_ref), (columns_hbm, columns_ref),
        ])
    ]
    rights = [
        pltpu.make_async_copy(right_hbm.at[:, :, s], right_ref.at[:, s], small_sem.at[2]) for s in range(8)
    ]
    for load in rights + small:
        load.start()
    batches = [(k, min(k + BATCH, BLOCKS)) for k in range(0, BLOCKS, BATCH)]
    loads = [
        [
            pltpu.make_async_copy(coupling_hbm.at[k, :, :, s], stage.at[k, :, s], load_sem.at[place])
            for k in range(first, last) for s in range(8)
        ]
        for place, (first, last) in enumerate(batches)
    ]
    reach = TOKENS + 1
    neighbours = sum(jnp.where(route[1], 1, 0) for route in routes)
    strangers = []
    if low + n_fy - 2 > reach:
        for offset in range(1, plane):
            target = plane_target(offset)[1]
            strangers.append((jnp.abs(target[0] - i) + jnp.abs(target[1] - j) > reach, target))
    if (high - 1) * low > reach + 1:
        for offset in range(1, high):
            target = line_target(offset)
            strangers.append((jnp.abs(target[0] - i) > reach + 1, target))
    for strange, target in strangers:
        @pl.when(strange)
        def _(target=target):
            pl.semaphore_signal(barrier, inc=1, device_id=target, device_id_type=MESH)

    def pass_token(place):
        for _, has_target, target, _ in routes:
            @pl.when(has_target)
            def _(target=target):
                pl.semaphore_signal(token_sem.at[place % 2], inc=1, device_id=target, device_id_type=MESH)

    def take_token(place):
        pl.semaphore_wait(token_sem.at[place % 2], neighbours)

    for batch in loads:
        for load in batch:
            load.start()

    g8 = lane_group(8)
    g64 = lane_group(DOF)
    g32 = lane_group(HALF)

    with scope("relay"):
        pltpu.make_async_copy(right_ref, right_ref, small_sem.at[2]).wait()
        sub = lax.broadcasted_iota(jnp.int32, (8, LANES), 0)
        turn = (g8 - sub) % GROUPS
        for face in range(faces):
            for tile in range(0, DOF // GROUPS, 2):
                x = right_ref[face // 8, face % 8, tile:tile + 2, :]
                x = jnp.where(sub < GROUPS, jnp.broadcast_to(x[0:1], (8, LANES)), jnp.broadcast_to(x[1:2], (8, LANES)))
                w0[face, tile * GROUPS:tile * GROUPS + 8, :] = pick(turn, rolls(x))
        small[0].wait()

    def field_copies(power):
        return [
            pltpu.make_async_remote_copy(
                src_ref=send_buf.at[power, q], dst_ref=recv_buf.at[power, q],
                send_sem=send_sem.at[q], recv_sem=recv_sem.at[power % 2, q],
                device_id=routes[q][2], device_id_type=MESH,
            )
            for q in range(4)
        ]

    def start_copies(copies, directions):
        for q in directions:
            @pl.when(routes[q][1])
            def _(copy=copies[q]):
                copy.start()

    def send_field(power, copies, directions):
        field = fields[power]
        for q in directions:
            picked = [field[ghost_ref[routes[q][0], g]] for g in range(GROUPS)]
            send_buf[power, q] = pick(g64, picked)
        if power == 0:
            pl.semaphore_wait(barrier, neighbours + sum(jnp.where(strange, 1, 0) for strange, _ in strangers))
        start_copies(copies, directions)
        if power == 0:
            pass_token(0)

    def send_products(power, copies, directions):
        listed = {q: [ghost_ref[routes[q][0], g] for g in range(GROUPS)] for q in directions}
        for q in directions:
            pairs = [far_rows(face) for face in listed[q]]
            for parity in range(2):
                send_buf[power, q, pl.ds(parity, HALF, stride=2), :] = pick(g32, [pair[parity] for pair in pairs])
        start_copies(copies, directions)

    def build_own(power):
        field = fields[power]

        @pl.loop(0, faces, unroll=4)
        def _(face):
            x = field[face]
            top, bottom = product_tile(x, g64)
            tiles[face, 0:DOF] = top
            tiles[face, DOF:2 * DOF] = bottom

    def own_products():
        for face in range(faces):
            left = mats[face, :, :OWNED * LANES]
            right = jnp.concatenate([tiles[columns_ref[face, k]] for k in range(OWNED)], axis=0)
            out = jnp.dot(left, right, preferred_element_type=f32)
            acc[face] = out[:HALF] + out[HALF:]

    def far_rows(face):
        left = mats[face, :, OWNED * LANES:]
        right = jnp.concatenate([tiles[columns_ref[face, k]] for k in range(OWNED, BLOCKS)], axis=0)
        out = jnp.dot(left, right, preferred_element_type=f32)
        total = acc[face] + (out[:HALF] + out[HALF:])
        total = total + pltpu.roll(total, LANES // 2, 1)
        turned = pltpu.roll(total, NRHS, 1)
        even = g32 % 2 == 0
        return jnp.where(even, total, turned), jnp.where(even, turned, total)

    def far_products(power, part):
        field = fields[power + 1]
        for face in part:
            first, second = far_rows(face)
            field[face, pl.ds(0, HALF, stride=2), :] = first
            field[face, pl.ds(1, HALF, stride=2), :] = second
            both = jnp.concatenate([first, second], axis=0)
            if power < POWERS - 1:
                ordered[power + 1, face] = both
                if power == POWERS - 2:
                    second_rows(face, both)
            else:
                late_rows(face, both)

    def first_rows():
        for face in range(faces):
            rows = slice(face * DOF, (face + 1) * DOF)
            a = jnp.concatenate([w0[face, pl.ds(parity, HALF, stride=2), :] for parity in range(2)], axis=0)
            hi, lo = split(pick(g64, [a + ordered[1, face], jnp.zeros_like(a), jnp.zeros_like(a), a]))
            zbuf[rows, :LANES] = hi.astype(bf16)
            zbuf[rows, LANES:] = lo.astype(bf16)
            newest[rows, :] = jnp.where(g64 < 2, hi, pltpu.roll(lo, LANES // 2, 1)).astype(bf16)

    def second_rows(face, newer):
        rows = slice(face * DOF, (face + 1) * DOF)
        hi, lo = split(ordered[1, face] + newer)
        hi, lo = hi.astype(bf16), lo.astype(bf16)
        second = g64 == 1
        zbuf[rows, :LANES] = jnp.where(second, hi, zbuf[rows, :LANES])
        zbuf[rows, LANES:] = jnp.where(second, lo, zbuf[rows, LANES:])
        newest[rows, :] = jnp.where(second, hi, jnp.where(g64 == 3, lo, newest[rows, :]))

    def late_rows(face, newer):
        rows = slice(face * DOF, (face + 1) * DOF)
        hi, lo = split(ordered[POWERS - 1, face] + newer)
        zero = jnp.zeros_like(hi)
        third = g64 == POWERS - 1
        zbuf[rows, :LANES] = zbuf[rows, :LANES] + jnp.where(third, hi, zero).astype(bf16)
        zbuf[rows, LANES:] = zbuf[rows, LANES:] + jnp.where(third, lo, zero).astype(bf16)
        newest[rows, :] = jnp.where(g64 == 0, hi, lo).astype(bf16)

    def receive_field(power, copies, directions):
        for q in directions:
            has_source = routes[q][3]

            @pl.when(has_source)
            def _(copy=copies[q]):
                copy.wait_recv()

            @pl.when(jnp.logical_not(has_source))
            def _(q=q):
                recv_buf[power, q] = jnp.zeros((DOF, LANES), f32)
        for q in directions:
            hi, lo = split(recv_buf[power, q])
            hi, lo = rolls(hi), rolls(lo)
            for g in range(GROUPS):
                top, bottom = halves(pick(g64, [
                    (hi if lane < GROUPS // 2 else lo)[(lane - g) % GROUPS] for lane in range(GROUPS)
                ]), g64)
                tiles[faces + q * GROUPS + g, 0:DOF] = top
                tiles[faces + q * GROUPS + g, DOF:2 * DOF] = bottom

    def finish_sends(copies):
        for q in range(4):
            @pl.when(routes[q][1])
            def _(copy=copies[q]):
                copy.wait_send()

    def prepare():
        for place, (first, last) in enumerate(batches):
            whole = stage.at[first:last]
            pltpu.make_async_copy(whole, whole, load_sem.at[place]).wait()
            for k in range(first, last):
                for face in range(faces):
                    hi, lo = split(stage[k, face // 8, face % 8])
                    mats[face, 0:HALF, k * LANES:(k + 1) * LANES] = hi.astype(bf16)
                    mats[face, HALF:DOF, k * LANES:(k + 1) * LANES] = lo.astype(bf16)

    def wait_for(buf, count, sem):
        whole = buf.at[0:count]
        pltpu.make_async_copy(whole, whole, sem).wait()

    def scatter(which, buf, landed):
        for offset in range(1, plane):
            rank, target = plane_target(offset)
            pltpu.make_async_remote_copy(
                src_ref=buf.at[rank], dst_ref=landed.at[offset - 1], send_sem=gram_sem.at[4 * which],
                recv_sem=gram_sem.at[4 * which + 1], device_id=target, device_id_type=MESH).start()

    def scatter_sum(which, buf, landed):
        total = buf[my_rank]
        wait_for(landed, plane - 1, gram_sem.at[4 * which + 1])
        for offset in range(1, plane):
            total = total + landed[offset - 1]
        return total

    def exchange(which, line, total):
        line[my_high] = total
        for offset in range(1, high):
            pltpu.make_async_remote_copy(
                src_ref=line.at[my_high], dst_ref=line.at[my_high], send_sem=gram_sem.at[4 * which],
                recv_sem=gram_sem.at[4 * which + 2], device_id=line_target(offset), device_id_type=MESH).start()

    def add_all(buf, count):
        terms = [buf[place] for place in range(count)]
        while len(terms) > 1:
            terms = [sum(terms[k:k + 2][1:], terms[k]) for k in range(0, len(terms), 2)]
        return terms[0]

    def exchange_sum(which, line):
        wait_for(line, high - 1, gram_sem.at[4 * which + 2])
        return add_all(line, high)

    def gather(which, final, first):
        for offset in range(1, plane):
            pltpu.make_async_remote_copy(
                src_ref=final.at[my_rank], dst_ref=final.at[my_rank], send_sem=gram_sem.at[4 * which],
                recv_sem=gram_sem.at[4 * which + first], device_id=plane_target(offset)[1], device_id_type=MESH).start()

    def gathered(which, final):
        wait_for(final, plane - 1, gram_sem.at[4 * which + 3])
        return jnp.concatenate([final[rank] for rank in range(plane)], axis=0)

    def early_gram():
        both = lax.dot_general(newest[...], zbuf[...], (((0,), (0,)), ((), ())), preferred_element_type=f32)
        half = 2 * NRHS
        gram = (both[:half, :LANES] + both[half:, LANES:]) + (both[:half, LANES:] + both[half:, :LANES])
        share = early_buf.shape[1]
        for rank in range(plane):
            early_buf[rank] = gram[rank * share:(rank + 1) * share]

    def late_gram():
        both = lax.dot_general(newest[:, :2 * NRHS], zbuf[...], (((0,), (0,)), ((), ())), preferred_element_type=f32)
        gram = (both[:NRHS, :LANES] + both[NRHS:2 * NRHS, LANES:]) + (both[:NRHS, LANES:] + both[NRHS:2 * NRHS, :LANES])
        late_plane[my_rank] = gram

    flat = [field.reshape(faces * DOF, LANES) for field in fields]

    def order_rows():
        for block in range(faces // 8):
            for pair in range(DOF // GROUPS // 2):
                for q in range(GROUPS):
                    halves = []
                    for tile in (2 * pair, 2 * pair + 1):
                        at = pl.ds(8 * block * DOF + tile * GROUPS + q, 8, stride=DOF)
                        halves.append(pick(g8, [view[at, :] for view in flat]))
                    hi, lo = split(jnp.concatenate(halves, axis=0))
                    row = 8 * (block * (DOF // GROUPS) + 2 * pair)
                    vbuf[q, row:row + 16, :LANES] = hi.astype(bf16)
                    vbuf[q, row:row + 16, LANES:] = lo.astype(bf16)

    copies = field_copies(0)
    with scope("send0"):
        send_field(0, copies, range(4))
    for power in range(POWERS):
        if power == POWERS - 1:
            with scope("egram"):
                early_gram()
                scatter(0, early_buf, early_plane)
        with scope("build%d" % power):
            build_own(power)
        if power == 0:
            with scope("prepare"):
                prepare()
                small[1].wait()
        with scope("own%d" % power):
            own_products()
        if power == 1:
            first_rows()
        if power < TOKENS // 2:
            take_token(2 * power)
            pass_token(2 * power + 1)
        with scope("recvy%d" % power):
            receive_field(power, copies, (2, 3))
            finish_sends(copies)
            if power < TOKENS // 2:
                take_token(2 * power + 1)
        with scope("recvx%d" % power):
            receive_field(power, copies, (0, 1))
        if power < POWERS - 1:
            copies = field_copies(power + 1)
            with scope("send%d" % (power + 1)):
                send_products(power + 1, copies, (0, 1))
            if power < TOKENS // 2 and 2 * power + 2 < TOKENS:
                pass_token(2 * power + 2)
            with scope("far%d" % power):
                far_products(power, range(faces))
            with scope("sendy%d" % (power + 1)):
                send_field(power + 1, copies, (2, 3))
        else:
            with scope("far%d" % power):
                far_products(power, range(faces // 4))
                with scope("eplane"):
                    exchange(0, early_line, scatter_sum(0, early_buf, early_plane))
                far_products(power, range(faces // 4, faces))

    with scope("lgram"):
        late_gram()
        gather(1, late_plane, 1)
    with scope("order"):
        order_rows()
    with scope("eline"):
        early_all[my_rank] = exchange_sum(0, early_line)
        gather(0, early_all, 3)
    with scope("lplane"):
        wait_for(late_plane, plane - 1, gram_sem.at[5])
        exchange(1, late_line, add_all(late_plane, plane))
    with scope("eall"):
        system = gathered(0, early_all)
    with scope("esolve"):
        count = 2 * NRHS
        solved = eliminate([system[t:t + 8] for t in range(0, count, 8)], True, across_gather)
        spread_early = replicate(lane_group(count), rolls(solved), GROUPS - 1)
    with scope("lall"):
        last = exchange_sum(1, late_line)
    with scope("lsolve"):
        left_half = lax.broadcasted_iota(jnp.int32, (NRHS, LANES), 1) < count
        cross = jnp.where(left_half, last, 0.0)
        pad = jnp.zeros((LANES - count, LANES), f32)
        done = high_dot(cross, jnp.concatenate([solved, pad], axis=0), ((1,), (0,)))
        inner = jnp.where(left_half, done, 0.0)
        outer = high_dot(jnp.where(lax.broadcasted_iota(jnp.int32, (count, LANES), 1) < count, solved, 0.0), jnp.concatenate([cross, jnp.zeros((LANES - NRHS, LANES), f32)], axis=0), ((1,), (1,)))
        schur = high_dot(inner, jnp.concatenate([cross, jnp.zeros((LANES - NRHS, LANES), f32)], axis=0), ((1,), (1,)))
        turned = rolls(last - done)
        small_system = turned[GROUPS // 2] - schur
        rights = replicate(g32, turned, GROUPS - 1)
        cuts = range(0, NRHS, 8)
        newest_part = eliminate(
            [small_system[t:t + 8] for t in cuts], False, across_sum, [rights[t:t + 8] for t in cuts])
        older = spread_early - high_dot(outer[:, :NRHS], newest_part, ((1,), (0,)))
        coeffs = jnp.concatenate([older, newest_part], axis=0)
    with scope("coeffs"):
        none = jnp.zeros((NRHS, LANES), f32)
        row = lax.broadcasted_iota(jnp.int32, (LANES, LANES), 0)
        col = lax.broadcasted_iota(jnp.int32, (LANES, LANES), 1) % NRHS
        first = jnp.where(row == col, 1.0, 0.0)
        padded = jnp.concatenate([coeffs, none], axis=0)
        combo = first - (padded + jnp.concatenate([none, coeffs], axis=0))
        hi, lo = split(jnp.concatenate([padded, combo], axis=1))
        group = lax.broadcasted_iota(jnp.int32, (LANES, 2 * LANES), 1) % LANES // NRHS
        his = [jnp.where(group == q, hi, 0.0).astype(bf16) for q in range(GROUPS)]
        los = [jnp.where(group == q, lo, 0.0).astype(bf16) for q in range(GROUPS)]
        right = jnp.concatenate(his + his + los, axis=0)
    with scope("outdot"):
        vhi = [vbuf[q, :, :LANES] for q in range(GROUPS)]
        vlo = [vbuf[q, :, LANES:] for q in range(GROUPS)]
        out = jnp.dot(jnp.concatenate(vhi + vlo + vhi, axis=1), right, preferred_element_type=f32)
        for part, out_ref in enumerate((sol_ref, res_ref)):
            for block in range(faces // 8):
                for tile in range(DOF // GROUPS):
                    row = 8 * (block * (DOF // GROUPS) + tile)
                    out_ref[8 * block:8 * block + 8, tile * LANES:(tile + 1) * LANES] = out[
                        row:row + 8, part * LANES:(part + 1) * LANES]
    with scope("drain"):
        sized = ordered.reshape(POWERS * faces * DOF, LANES)
        sent = 2 * (plane - 1) + high - 1
        wait_for(sized, sent * early_buf.shape[1], gram_sem.at[0])
        wait_for(sized, (sent - plane + 1) * NRHS, gram_sem.at[4])


def put_out(sol_ref, res_ref, sol_out, res_out, sem):
    width = sol_ref.shape[1] // PIECES
    copies = [
        pltpu.make_async_copy(src.at[:, pl.ds(piece * width, width)], dst.at[:, pl.ds(piece * width, width)], sem.at[part, piece])
        for part, (src, dst) in enumerate([(sol_ref, sol_out), (res_ref, res_out)]) for piece in range(PIECES)
    ]
    for copy in copies:
        copy.start()
    for copy in copies:
        copy.wait()


def on_device(shape, right_side, coupling, face_columns, ghost_lists):
    n_fx, n_fy, low, faces = shape
    plane = low * n_fy
    high = n_fx // low
    right_rows = right_side.reshape(faces // 8, 8, DOF // GROUPS, LANES).transpose(0, 2, 1, 3)
    coupling = coupling.reshape(faces // 8, 8, BLOCKS, HALF, LANES).transpose(2, 0, 3, 1, 4)
    rows = faces * DOF
    early = 2 * NRHS // plane
    vmem = pl.BlockSpec(memory_space=pltpu.VMEM)
    hbm = pl.BlockSpec(memory_space=pltpu.HBM)
    dma = pltpu.SemaphoreType.DMA
    i32 = jnp.int32
    out = jax.ShapeDtypeStruct(right_side.shape, f32)
    gram = [
        pltpu.VMEM((plane, early, LANES), f32),
        pltpu.VMEM((plane - 1, early, LANES), f32),
        pltpu.VMEM((high, early, LANES), f32),
        pltpu.VMEM((plane, early, LANES), f32),
        pltpu.VMEM((plane, NRHS, LANES), f32),
        pltpu.VMEM((high, NRHS, LANES), f32),
    ]
    results = pl.pallas_call(
        functools.partial(kernel, shape),
        out_shape=(out, out),
        in_specs=[hbm] * 4,
        out_specs=(vmem, vmem),
        scratch_shapes=[
            pltpu.VMEM((faces // 8, 8, DOF // GROUPS, LANES), f32),
            pltpu.SMEM(face_columns.shape, i32),
            pltpu.SMEM(ghost_lists.shape, i32),
            pltpu.VMEM((BLOCKS, faces // 8, 8, HALF, LANES), f32),
            pltpu.VMEM((faces, DOF, BLOCKS * LANES), bf16),
        ]
        + [pltpu.VMEM((faces, DOF, LANES), f32)] * (POWERS + 1)
        + [
            pltpu.VMEM((POWERS, faces, DOF, LANES), f32),
            pltpu.VMEM((faces + 4 * GROUPS, LANES, LANES), bf16),
            pltpu.VMEM((faces, HALF, LANES), f32),
            pltpu.VMEM((POWERS, 4, DOF, LANES), f32),
            pltpu.VMEM((POWERS, 4, DOF, LANES), f32),
            pltpu.VMEM((rows, 2 * LANES), bf16),
            pltpu.VMEM((rows, LANES), bf16),
            pltpu.VMEM((GROUPS, rows // GROUPS, 2 * LANES), bf16),
        ]
        + gram
        + [
            dma((3,)),
            dma((-(-BLOCKS // BATCH),)),
            dma((4,)),
            dma((2, 4)),
            dma((7,)),
            pltpu.SemaphoreType.REGULAR((2,)),
        ],
        compiler_params=pltpu.CompilerParams(
            collective_id=0, has_side_effects=True, vmem_limit_bytes=40 * 2**20
        ),
    )(*[pltpu.with_memory_space_constraint(x, pltpu.HBM) for x in (right_rows, coupling, face_columns, ghost_lists)])
    return pl.pallas_call(
        put_out,
        out_shape=(out, out),
        in_specs=[vmem, vmem],
        out_specs=(hbm, hbm),
        scratch_shapes=[dma((2, PIECES))],
        compiler_params=pltpu.CompilerParams(vmem_limit_bytes=2**20),
    )(*results)


def solution(mesh):
    n_fx, n_fy = mesh.shape["fx"], mesh.shape["fy"]
    low = 1
    while low * low * 4 <= n_fx:
        low *= 2

    def body(right_side, coupling, face_columns, ghost_lists):
        shape = (n_fx, n_fy, low, right_side.shape[0])
        return on_device(shape, right_side, coupling, face_columns, ghost_lists)

    placed = (
        P(("fx", "fy"), None),
        P(("fx", "fy"), None, None),
        P(("fx", "fy"), None),
        P(("fx", "fy"), None),
    )
    return jax.shard_map(
        body,
        mesh=mesh,
        in_specs=placed,
        out_specs=(P(("fx", "fy"), None), P(("fx", "fy"), None)),
        check_vma=False,
    )
```
